256 devices in a mesh: mem: 4 (over y), sec: 64 (over x, z, core).
Axes of the slice: x: 4, y: 4, z: 8, core: 2. Of those that a mesh axis runs over, the one named last changes fastest.
Arguments:
- outer_source: float32 [8, 8192, 1024], P('mem', 'sec'), may hold values from -6 to 6
- outer_depth: float32 [8192, 1024], P('sec'), may hold values from 0.05 to 0.45
- wet_tiles: int32 [64, 8], replicated, may hold values 0 or 1
- nest_host: int32 [64], replicated, may hold values from 0 to 63, as said below
- nest_anchor: int32 [64, 2], replicated, may hold values from 0 to 960, as said below
- nest_source: float32 [8, 64, 384, 384], P('mem', 'sec'), may hold values from -6 to 6
- nest_depth: float32 [64, 384, 384], P('sec'), may hold values from 0.05 to 0.45
Outputs:
- outer_level: float32 [8, 8192, 1024], P('mem', 'sec')
- outer_flux: float32 [2, 8, 8192, 1024], P(None, 'mem', 'sec')
- peak_mean: float32 [64, 384, 384], P('sec')
- peak_var: float32 [64, 384, 384], P('sec')
The draws below stay inside these ranges and needn't reach their ends.
Inputs may be any that keep to these rules, and one draw needn't show every extreme that they name: `nest_host`: every section holds either no nest or exactly 2 nests; sections 0 and 63 hold nests. `nest_anchor`: column 0 is at most 64 and column 1 at most 960, so that a nest's block lies within its host section; some nest reaches both.
All inputs are finite; a program needn't handle non-finite values.
Results may differ from the reference program's by a relative error of at most 0.00002.
Values sent between devices are 32-bit elements; how exact they have to be, the bound alone decides.
A program may use at most 64 MiB of HBM per device.

```python
import math
import jax
import jax.numpy as jnp
from jax import lax

ROWS_DEV = 128
COLS = 1024
TILE = 128
NEST_COARSE = 64
REFINE = 6
STEPS = 3
HOST_MOST = 2
FINE = 384
MEMBERS = 8
ROWS = 8192
NESTS = 64


def draw_nest_host(key, part):
    first_key = jax.random.fold_in(key, 31)
    second_key = jax.random.fold_in(key, 32)
    middle = (jax.random.permutation(first_key, NESTS - 2) + 1).astype(jnp.int32)
    hosting = jnp.concatenate([jnp.array([0, NESTS - 1], jnp.int32), middle[:NESTS // HOST_MOST - 2]])
    shuffle = jax.random.permutation(second_key, NESTS).astype(jnp.int32)
    return hosting[shuffle // HOST_MOST].astype(jnp.int32)


def draw_nest_anchor(key, part):
    row_key = jax.random.fold_in(key, 41)
    col_key = jax.random.fold_in(key, 42)
    pick_key = jax.random.fold_in(key, 43)
    row_values = jax.random.randint(row_key, (NESTS,), 0, ROWS_DEV - NEST_COARSE + 1).astype(jnp.int32)
    col_values = jax.random.randint(col_key, (NESTS,), 0, COLS - NEST_COARSE + 1).astype(jnp.int32)
    chosen = jax.random.randint(pick_key, (), 0, NESTS).astype(jnp.int32)
    positions = jnp.arange(NESTS, dtype=jnp.int32)
    row_values = jnp.where(positions == chosen, ROWS_DEV - NEST_COARSE, row_values)
    col_values = jnp.where(positions == chosen, COLS - NEST_COARSE, col_values)
    return jnp.stack([row_values, col_values], axis=1).astype(jnp.int32)


def touch_ends(values, own_key, smallest, high):
    longest = values.shape.index(max(values.shape))
    spots = []
    for shift in (0, 1):
        where = [jax.random.randint(jax.random.fold_in(own_key, axis), (), 0, length) for axis, length in enumerate(values.shape)]
        where[longest] = (where[longest] + shift) % values.shape[longest]
        spots.append(tuple(where))
    return values.at[spots[0]].set(smallest).at[spots[1]].set(high)


def level_of(key, extent, pieces, low, largest):
    factor_of = 1.0
    for dim, shards_of in pieces:
        heights = jax.random.uniform(jax.random.fold_in(jax.random.fold_in(key, 6), dim), (shards_of,), jnp.float32, low / len(pieces), largest / len(pieces))
        factor_of = factor_of * jnp.repeat(jnp.exp(heights), extent[dim] // shards_of).reshape((-1,) + (1,) * (len(extent) - 1 - dim))
    return factor_of


def noise(own_key, dims, scale, reach, shards=(), kind=jnp.bfloat16):
    loudness = level_of(own_key, dims, shards, -0.22, 0.18) if shards else 1.0
    values = jax.random.normal(own_key, dims, jnp.float32) * scale * loudness
    return jnp.minimum(jnp.maximum(values, -reach), reach).astype(kind)


def setup_inputs(seed: int = 0) -> dict:
    seeds = jax.random.split(jax.random.key(seed), 8)
    return {
        "outer_source": noise(seeds[0], (MEMBERS, ROWS, COLS), 1.0, 6.0, ((0, 4), (1, 64)), jnp.float32),
        "outer_depth": jnp.clip(jnp.exp(math.log(0.45) - 2.1972245 * jax.random.uniform(seeds[1], (ROWS, COLS), jnp.float32) ** level_of(seeds[1], (ROWS, COLS), ((0, 64),), -0.2, 0.2)), 0.05, 0.45),
        "wet_tiles": touch_ends((jax.random.randint(seeds[2], (ROWS // TILE, COLS // TILE), 0, 4) < 3).astype(jnp.int32), jax.random.fold_in(seeds[2], 1), 0, 1),
        "nest_host": draw_nest_host(jax.random.fold_in(seeds[7], 71), 0),
        "nest_anchor": draw_nest_anchor(jax.random.fold_in(seeds[7], 71), 0),
        "nest_source": noise(seeds[5], (MEMBERS, NESTS, FINE, FINE), 1.0, 6.0, ((0, 4), (1, 64)), jnp.float32),
        "nest_depth": jnp.clip(jnp.exp(math.log(0.45) - 2.1972245 * jax.random.uniform(seeds[6], (NESTS, FINE, FINE), jnp.float32) ** level_of(seeds[6], (NESTS, FINE, FINE), ((0, 64),), -0.2, 0.2)), 0.05, 0.45),
    }


def from_left(field):
    return jnp.concatenate([jnp.zeros_like(field[..., :1]), field[..., :-1]], axis=-1)


def from_right(field):
    return jnp.concatenate([field[..., 1:], jnp.zeros_like(field[..., :1])], axis=-1)


def from_above(field):
    return jnp.concatenate([jnp.zeros_like(field[..., :1, :]), field[..., :-1, :]], axis=-2)


def from_below(field):
    return jnp.concatenate([field[..., 1:, :], jnp.zeros_like(field[..., :1, :])], axis=-2)


def edge_cells(surface, row_start, col_start):
    zero_index = jnp.zeros((), jnp.int32)
    coarse_block = lax.dynamic_slice(surface, (zero_index, row_start, col_start), (surface.shape[0], NEST_COARSE, NEST_COARSE))
    return jnp.concatenate([coarse_block[:, 0, :], coarse_block[:, -1, :], coarse_block[:, :, 0], coarse_block[:, :, -1]], axis=-1)


def force_edges(updated, edge_values):
    width = NEST_COARSE
    top_edge = jnp.repeat(edge_values[..., 0:width], REFINE, axis=-1)
    bottom_edge = jnp.repeat(edge_values[..., width:2 * width], REFINE, axis=-1)
    west_edge = jnp.repeat(edge_values[..., 2 * width:3 * width], REFINE, axis=-1)
    east_edge = jnp.repeat(edge_values[..., 3 * width:4 * width], REFINE, axis=-1)
    updated = updated.at[..., 0, :].set(top_edge)
    updated = updated.at[..., -1, :].set(bottom_edge)
    updated = updated.at[..., :, 0].set(west_edge)
    updated = updated.at[..., :, -1].set(east_edge)
    return updated


def nest_substep(surface, flux_x, flux_y, depth_coef, edge_values):
    updated = surface - (flux_x - from_left(flux_x)) - (flux_y - from_above(flux_y))
    updated = force_edges(updated, edge_values)
    flux_x = flux_x - depth_coef * (from_right(updated) - updated)
    flux_y = flux_y - depth_coef * (from_below(updated) - updated)
    return updated, flux_x, flux_y


def reference(outer_source, outer_depth, wet_tiles, nest_host, nest_anchor, nest_source, nest_depth):
    tile_flags = wet_tiles.astype(jnp.float32)
    wet_mask = jnp.broadcast_to(tile_flags[:, None, :, None], (tile_flags.shape[0], TILE, tile_flags.shape[1], TILE)).reshape(ROWS, COLS)
    surface = outer_source
    flux_x = jnp.zeros_like(surface)
    flux_y = jnp.zeros_like(surface)
    row_starts = (nest_host * ROWS_DEV + nest_anchor[:, 0]).astype(jnp.int32)
    col_starts = nest_anchor[:, 1].astype(jnp.int32)
    fine_level = nest_source
    fine_x = jnp.zeros_like(fine_level)
    fine_y = jnp.zeros_like(fine_level)
    peak_level = jnp.full(fine_level.shape, -jnp.inf, jnp.float32)
    for step_index in range(STEPS):
        updated = wet_mask * (surface - (flux_x - from_left(flux_x)) - (flux_y - from_above(flux_y)))
        flux_x = wet_mask * (flux_x - outer_depth * (from_right(updated) - updated))
        flux_y = wet_mask * (flux_y - outer_depth * (from_below(updated) - updated))
        surface = updated
        edges = jax.vmap(lambda row_start, col_start: edge_cells(surface, row_start, col_start))(row_starts, col_starts)
        edges = jnp.transpose(edges, (1, 0, 2))
        for substep in range(REFINE):
            fine_level, fine_x, fine_y = nest_substep(fine_level, fine_x, fine_y, nest_depth, edges)
            peak_level = jnp.maximum(peak_level, fine_level)
    member_mean = jnp.sum(peak_level, axis=0) / MEMBERS
    deviation = peak_level - member_mean
    member_var = jnp.sum(deviation * deviation, axis=0) / MEMBERS
    return surface, jnp.stack([flux_x, flux_y]), member_mean, member_var
```

```python
import jax
import jax.numpy as jnp
from jax import lax
from jax.experimental import pallas as pl
from jax.experimental.pallas import tpu as pltpu
from jax.sharding import PartitionSpec as P

MESH = pl.DeviceIdType.MESH
STEPS = 3
REFINE = 6
SECTIONS = 64
X_PLANES = 4
Z_CORES = 16
STRIP = 48
VMEM = pltpu.VMEM
ANY = pl.ANY


def vmem_spec():
    return pl.BlockSpec(memory_space=pltpu.VMEM)


def smem_spec():
    return pl.BlockSpec(memory_space=pltpu.SMEM)


def any_spec():
    return pl.BlockSpec(memory_space=pl.ANY)


def halo_kernel(eta_ref, depth_ref, up_eta, dn_eta, up_depth, dn_depth, send_sem, recv_sem):
    me = lax.axis_index("sec")
    below = lax.rem(me + 1, SECTIONS)
    above = lax.rem(me + SECTIONS - 1, SECTIONS)
    barrier = pltpu.get_barrier_semaphore()
    for peer in (below, above):
        pl.semaphore_signal(barrier, inc=1, device_id={"sec": peer}, device_id_type=MESH)
    pl.semaphore_wait(barrier, 2)
    plan = (
        (eta_ref.at[:, 15], up_eta, below),
        (eta_ref.at[:, 0], dn_eta, above),
        (depth_ref.at[15], up_depth, below),
        (depth_ref.at[0], dn_depth, above),
    )
    copies = []
    for number, (source, target, peer) in enumerate(plan):
        copy = pltpu.make_async_remote_copy(
            src_ref=source,
            dst_ref=target,
            send_sem=send_sem.at[number],
            recv_sem=recv_sem.at[number],
            device_id={"sec": peer},
            device_id_type=MESH,
        )
        copy.start()
        copies.append(copy)
    for copy in copies:
        copy.wait()


def exchange_halos(eta, depth):
    rows = jax.ShapeDtypeStruct((2, 8, 1024), jnp.float32)
    coef = jax.ShapeDtypeStruct((8, 1024), jnp.float32)
    return pl.pallas_call(
        halo_kernel,
        out_shape=(rows, rows, coef, coef),
        in_specs=[any_spec()] * 2,
        out_specs=(any_spec(),) * 4,
        scratch_shapes=[pltpu.SemaphoreType.DMA((4,)), pltpu.SemaphoreType.DMA((4,))],
        compiler_params=pltpu.CompilerParams(collective_id=0, has_side_effects=True),
        name="halo",
    )(eta, depth)


def outer_kernel(
    wet_ref, host_ref, anchor_ref, eta_in, depth_in, up_eta, dn_eta, up_depth, dn_depth,
    level_ref, flux_ref, edges_ref, pick_ref,
    eta, fx, fy, dw, masks, first, last,
):
    section = lax.axis_index("sec")
    lanes = lax.broadcasted_iota(jnp.int32, (8, 1024), 1)
    subs = lax.broadcasted_iota(jnp.int32, (8, 1024), 0)

    first[section] = 0
    last[section] = 0

    def note(n, _):
        last[host_ref[n]] = n
        first[host_ref[SECTIONS - 1 - n]] = SECTIONS - 1 - n
        return 0

    lax.fori_loop(0, SECTIONS, note, 0)

    def choose(n, _):
        host = host_ref[n]
        pick_ref[n] = (host // Z_CORES) * 2 + jnp.where(first[host] == n, 0, 1)
        return 0

    lax.fori_loop(0, SECTIONS, choose, 0)

    for band in range(3):
        row = section + band - 1
        inside = (row >= 0) & (row < SECTIONS)
        row = jnp.clip(row, 0, SECTIONS - 1)
        for tile in range(8):
            flag = jnp.where(inside, wet_ref[row, tile], 0)
            masks[band, :, tile * 128 : (tile + 1) * 128] = jnp.full(
                (8, 128), flag, jnp.int32
            ).astype(jnp.float32)
    zeros = jnp.zeros((8, 1024), jnp.float32)
    masks[3] = zeros

    def band_of(k):
        return jnp.where(k == 1, 0, jnp.where(k <= 17, 1, jnp.where(k == 18, 2, 3)))

    for k, (rows, coef) in ((1, (up_eta, up_depth)), (18, (dn_eta, dn_depth))):
        mask = masks[0 if k == 1 else 2]
        dw[k] = mask * coef[...]
        for m in range(2):
            eta[m, k] = mask * rows[m]
    dw[0] = zeros
    for m in range(2):
        for k in (0, 19):
            eta[m, k] = zeros
            fx[m, k] = zeros
        fy[m, 0] = zeros
        fy[m, 19] = zeros
    dw[19] = zeros

    def fill(k, _):
        mask = masks[1]
        dw[k + 2] = mask * depth_in[k]
        for m in range(2):
            eta[m, k + 2] = mask * eta_in[m, k]
        return 0

    lax.fori_loop(0, 16, fill, 0)

    def east(x):
        return jnp.where(lanes == 1023, 0.0, pltpu.roll(x, 1023, 1))

    def west(x):
        return jnp.where(lanes == 0, 0.0, pltpu.roll(x, 1, 1))

    def south(x, following):
        return jnp.where(subs == 7, pltpu.roll(following, 7, 0), pltpu.roll(x, 7, 0))

    def north(x, previous):
        return jnp.where(subs == 0, pltpu.roll(previous, 1, 0), pltpu.roll(x, 1, 0))

    def sweep_first(k, _):
        for m in range(2):
            now = eta[m, k]
            before = eta[m, k - 1]
            fx[m, k] = -(dw[k] * (east(now) - now))
            fy[m, k - 1] = -(dw[k - 1] * (south(before, now) - before))
        return 0

    def edges(step):
        rows128 = (
            lax.broadcasted_iota(jnp.int32, (16, 8, 128), 0) * 8
            + lax.broadcasted_iota(jnp.int32, (16, 8, 128), 1)
        )
        lane16 = lax.broadcasted_iota(jnp.int32, (16, 8, 128), 2)
        lane_row = lax.broadcasted_iota(jnp.int32, (8, 128), 1)
        for slot in range(2):
            nest = (first if slot == 0 else last)[section]
            r0 = anchor_ref[nest, 0]
            c0 = anchor_ref[nest, 1]
            base = pl.multiple_of(jnp.minimum(c0 // 128, 6) * 128, 128)
            left = pl.multiple_of((c0 // 128) * 128, 128)
            right = pl.multiple_of(((c0 + 63) // 128) * 128, 128)
            for m in range(2):

                def row_of(r):
                    tile = r // 8 + 2
                    x = eta[m, tile, pl.ds(lax.rem(r, 8), 1), pl.ds(base, 256)]
                    return jnp.broadcast_to(x, (8, 256))

                shift = c0 - base
                top = pltpu.roll(row_of(r0), 256 - shift, 1)[:, :128]
                bottom = pltpu.roll(row_of(r0 + 63), lax.rem(320 - shift, 256), 1)[:, :128]
                pair = jnp.where(lane_row < 64, top, bottom)
                at = (step * 2 + m) * 2
                edges_ref[slot, at : at + 1, :] = pair[0:1]
                west_block = eta[m, 2:18, :, pl.ds(left, 128)]
                east_block = eta[m, 2:18, :, pl.ds(right, 128)]
                west_col = jnp.sum(jnp.where(lane16 == c0 - left, west_block, 0.0), axis=2, keepdims=True)
                east_col = jnp.sum(jnp.where(lane16 == c0 + 63 - right, east_block, 0.0), axis=2, keepdims=True)
                place = rows128 - r0
                both = jnp.where((lane16 == place) & (lane16 < 64), west_col, 0.0) + jnp.where(
                    (lane16 == place + 64) & (lane16 >= 64), east_col, 0.0
                )
                edges_ref[slot, at + 1 : at + 2, :] = jnp.sum(jnp.sum(both, axis=0), axis=0, keepdims=True)

    for slot in range(2):
        edges_ref[slot, 12:16, :] = jnp.zeros((4, 128), jnp.float32)
    lax.fori_loop(1, 20, sweep_first, 0)
    edges(0)

    def full_step(step):
        def body(k, carry):
            new_carry = []
            mask = masks[band_of(k)]
            for m in range(2):
                px = fx[m, k]
                py = fy[m, k]
                py_before = carry[m]
                before = eta[m, k - 1]
                now = mask * (eta[m, k] - (px - west(px)) - (py - north(py, py_before)))
                eta[m, k] = now
                fx[m, k] = px - dw[k] * (east(now) - now)
                fy[m, k - 1] = py_before - dw[k - 1] * (south(before, now) - before)
                new_carry.append(py)
            return tuple(new_carry)

        lax.fori_loop(1, 20, body, (zeros, zeros))
        edges(step)

    full_step(1)
    full_step(2)

    def emit(k, _):
        for m in range(2):
            level_ref[m, k] = eta[m, k + 2]
            flux_ref[0, m, k] = fx[m, k + 2]
            flux_ref[1, m, k] = fy[m, k + 2]
        return 0

    lax.fori_loop(0, 16, emit, 0)


def outer_steps(wet_tiles, nest_host, nest_anchor, eta, depth, halos):
    return pl.pallas_call(
        outer_kernel,
        out_shape=(
            jax.ShapeDtypeStruct((2, 16, 8, 1024), jnp.float32),
            jax.ShapeDtypeStruct((2, 2, 16, 8, 1024), jnp.float32),
            jax.ShapeDtypeStruct((2, 16, 128), jnp.float32),
            jax.ShapeDtypeStruct((SECTIONS,), jnp.int32),
        ),
        in_specs=[smem_spec()] * 3 + [vmem_spec()] * 6,
        out_specs=(vmem_spec(), vmem_spec(), vmem_spec(), smem_spec()),
        scratch_shapes=[
            VMEM((2, 20, 8, 1024), jnp.float32),
            VMEM((2, 20, 8, 1024), jnp.float32),
            VMEM((2, 20, 8, 1024), jnp.float32),
            VMEM((20, 8, 1024), jnp.float32),
            VMEM((4, 8, 1024), jnp.float32),
            pltpu.SMEM((SECTIONS,), jnp.int32),
            pltpu.SMEM((SECTIONS,), jnp.int32),
        ],
        compiler_params=pltpu.CompilerParams(vmem_limit_bytes=40 << 20),
        name="outer",
    )(wet_tiles, nest_host, nest_anchor, eta, depth, *halos)


def route_kernel(
    host_ref, pick_ref, edges_ref, out_ref,
    gathered, outgoing, incoming, send_x, recv_x, send_z, recv_z,
):
    me = lax.axis_index("sec")
    plane = me // Z_CORES
    spot = lax.rem(me, Z_CORES)
    barrier = pltpu.get_barrier_semaphore()
    for step in range(1, X_PLANES):
        peer = lax.rem(plane + step, X_PLANES) * Z_CORES + spot
        pl.semaphore_signal(barrier, inc=1, device_id={"sec": peer}, device_id_type=MESH)
    for step in range(1, Z_CORES):
        peer = plane * Z_CORES + lax.rem(spot + step, Z_CORES)
        pl.semaphore_signal(barrier, inc=1, device_id={"sec": peer}, device_id_type=MESH)
    gathered[plane] = edges_ref[...]
    pl.semaphore_wait(barrier, X_PLANES + Z_CORES - 2)

    copies = []
    for step in range(1, X_PLANES):
        peer = lax.rem(plane + step, X_PLANES) * Z_CORES + spot
        copy = pltpu.make_async_remote_copy(
            src_ref=edges_ref,
            dst_ref=gathered.at[plane],
            send_sem=send_x.at[step - 1],
            recv_sem=recv_x.at[step - 1],
            device_id={"sec": peer},
            device_id_type=MESH,
        )
        copy.start()
        copies.append(copy)
    for copy in copies:
        copy.wait()

    second = []
    for step in range(Z_CORES):
        target = lax.rem(spot + step, Z_CORES)
        choice = pick_ref[plane * Z_CORES + target]
        message = gathered[choice // 2, lax.rem(choice, 2)]
        if step == 0:
            incoming[spot] = message
            continue
        outgoing[step] = message
        copy = pltpu.make_async_remote_copy(
            src_ref=outgoing.at[step],
            dst_ref=incoming.at[spot],
            send_sem=send_z.at[step - 1],
            recv_sem=recv_z.at[step - 1],
            device_id={"sec": plane * Z_CORES + target},
            device_id_type=MESH,
        )
        copy.start()
        second.append(copy)
    for copy in second:
        copy.wait()
    out_ref[...] = incoming[lax.rem(host_ref[me], Z_CORES)]


def route_edges(nest_host, pick, edges):
    return pl.pallas_call(
        route_kernel,
        out_shape=jax.ShapeDtypeStruct((16, 128), jnp.float32),
        in_specs=[smem_spec(), smem_spec(), vmem_spec()],
        out_specs=vmem_spec(),
        scratch_shapes=[
            VMEM((X_PLANES, 2, 16, 128), jnp.float32),
            VMEM((Z_CORES, 16, 128), jnp.float32),
            VMEM((Z_CORES, 16, 128), jnp.float32),
            pltpu.SemaphoreType.DMA((X_PLANES - 1,)),
            pltpu.SemaphoreType.DMA((X_PLANES - 1,)),
            pltpu.SemaphoreType.DMA((Z_CORES - 1,)),
            pltpu.SemaphoreType.DMA((Z_CORES - 1,)),
        ],
        compiler_params=pltpu.CompilerParams(collective_id=1, has_side_effects=True),
        name="route",
    )(nest_host, pick, edges)


def nest_kernel(edge_ref, source_ref, depth_ref, peak_ref, h, div, peak, coef, cols, rows, src, dsrc, sem):
    copies = []
    for t in range(3):
        part = pl.ds(128 * t, 128)
        for m in range(2):
            copies.append(
                pltpu.make_async_copy(source_ref.at[m, 0, :, part], src.at[m, t], sem.at[3 * m + t])
            )
        copies.append(pltpu.make_async_copy(depth_ref.at[0, :, part], dsrc.at[t], sem.at[6 + t]))
    for copy in copies:
        copy.start()

    lane = lax.broadcasted_iota(jnp.int32, (8, 128), 1)
    sub = lax.broadcasted_iota(jnp.int32, (8, 128), 0)

    def spread(row, index):
        wide = jnp.broadcast_to(row, (8, 128))
        return jnp.take_along_axis(wide, index, axis=1)

    for step in range(STEPS):
        for m in range(2):
            at = (step * 2 + m) * 2
            level = edge_ref[at : at + 1, :]
            upright = edge_ref[at + 1 : at + 2, :]
            for q in range(8):
                cols[step, m, 0, q] = spread(upright, sub * 8 + q)
                cols[step, m, 1, q] = spread(upright, sub * 8 + q + 64)
            for side in range(2):
                for t in range(3):
                    value = spread(level, (lane + 128 * t) // REFINE + 64 * side)
                    if t == 0:
                        value = jnp.where(lane == 0, cols[step, m, 0, 7 * side], value)
                    if t == 2:
                        value = jnp.where(lane == 127, cols[step, m, 1, 7 * side], value)
                    rows[step, m, side, t] = value

    def force(value, step, m, t, i, side):
        if side is not None:
            edge_sub = 0 if side == 0 else 7
            value = jnp.where(sub == edge_sub, rows[step, m, side, t], value)
        if t == 0:
            value = jnp.where(lane == 0, cols[step, m, 0, i // REFINE], value)
        if t == 2:
            value = jnp.where(lane == 127, cols[step, m, 1, i // REFINE], value)
        return value

    for copy in copies:
        copy.wait()

    def load(i, side=None):
        for t in range(3):
            coef[i, t] = dsrc[t, pl.ds(i, 8, stride=STRIP), :]
            for m in range(2):
                value = force(src[m, t, pl.ds(i, 8, stride=STRIP), :], 0, m, t, i, side)
                h[m, i, t] = value
                peak[m, i, t] = value
                div[m, i, t] = jnp.zeros((8, 128), jnp.float32)

    load(0, 0)

    def load_body(i, _):
        load(i)
        return 0

    lax.fori_loop(1, STRIP - 1, load_body, 0)
    load(STRIP - 1, 1)

    def advance(i, step, carry, side=None, last=False):
        out = []
        for m in range(2):
            now, above = carry[m]
            following = [h[m, i + 1, t] for t in range(3)]
            lefts = [pltpu.roll(now[t], 127, 1) for t in range(3)]
            f = []
            for t in range(3):
                ahead = lefts[t] if t == 2 else jnp.where(lane == 127, lefts[t + 1], lefts[t])
                f.append(coef[i, t] * (ahead - now[t]))
            rights = [pltpu.roll(f[t], 1, 1) for t in range(3)]
            g = []
            for t in range(3):
                behind = rights[t] if t == 0 else jnp.where(lane == 0, rights[t - 1], rights[t])
                g.append(coef[i, t] * (following[t] - now[t]))
                change = div[m, i, t] - ((f[t] - behind) + (g[t] - above[t]))
                value = force(now[t] - change, step, m, t, i, side)
                div[m, i, t] = change
                h[m, i, t] = value
                peak[m, i, t] = jnp.maximum(peak[m, i, t], value)
            out.append((following, g))
        return out

    def substep(k, _):
        step = k // REFINE
        carry = []
        for m in range(2):
            now = [h[m, 0, t] for t in range(3)]
            above = []
            for t in range(3):
                wrapped = pltpu.roll(now[t], 7, 0)
                h[m, STRIP, t] = wrapped
                above.append(
                    pltpu.roll(coef[STRIP - 1, t] * (wrapped - h[m, STRIP - 1, t]), 1, 0)
                )
            carry.append((now, above))
        carry = advance(0, step, carry, side=0)
        carry = lax.fori_loop(1, STRIP - 1, lambda i, c: advance(i, step, c), carry, unroll=2)
        advance(STRIP - 1, step, carry, side=1)
        return 0

    lax.fori_loop(1, STEPS * REFINE, substep, 0)

    def store(i, _):
        for m in range(2):
            for t in range(3):
                peak_ref[m, t, pl.ds(i, 8, stride=STRIP), :] = peak[m, i, t]
        return 0

    lax.fori_loop(0, STRIP, store, 0)


def advance_nests(edges, source, depth):
    return pl.pallas_call(
        nest_kernel,
        out_shape=jax.ShapeDtypeStruct((2, 3, 384, 128), jnp.float32),
        in_specs=[vmem_spec(), any_spec(), any_spec()],
        out_specs=vmem_spec(),
        scratch_shapes=[
            VMEM((2, STRIP + 1, 3, 8, 128), jnp.float32),
            VMEM((2, STRIP, 3, 8, 128), jnp.float32),
            VMEM((2, STRIP, 3, 8, 128), jnp.float32),
            VMEM((STRIP, 3, 8, 128), jnp.float32),
            VMEM((STEPS, 2, 2, 8, 8, 128), jnp.float32),
            VMEM((STEPS, 2, 2, 3, 8, 128), jnp.float32),
            VMEM((2, 3, 384, 128), jnp.float32),
            VMEM((3, 384, 128), jnp.float32),
            pltpu.SemaphoreType.DMA((9,)),
        ],
        compiler_params=pltpu.CompilerParams(vmem_limit_bytes=40 << 20),
        name="nests",
    )(edges, source, depth)


def reduce_kernel(peak_ref, mean_ref, var_ref, r1, st, r2, mv, s1, q1, s2, q2, s3, q3, s4, q4, osem):
    m = lax.axis_index("mem")
    near = m + 1 - 2 * lax.rem(m, 2)
    far = 3 - m
    high = m // 2
    gray = lax.rem(lax.rem(m, 2) + high, 2)
    barrier = pltpu.get_barrier_semaphore()
    for peer in (near, far):
        pl.semaphore_signal(barrier, inc=1, device_id={"mem": peer}, device_id_type=MESH)
    pl.semaphore_wait(barrier, 2)

    one = (near, far)
    two = (far, near)
    keep1 = (gray, high)
    keep2 = (high, gray)

    def rows_of(half, bit1):
        return pl.multiple_of(half * 192 + bit1 * 96, 8)

    def remote(src, dst, send, recv, peer):
        return pltpu.make_async_remote_copy(
            src_ref=src, dst_ref=dst, send_sem=send, recv_sem=recv,
            device_id={"mem": peer}, device_id_type=MESH,
        )

    flows = [(t, half) for t in range(3) for half in range(2)]
    first = {}
    for t, half in flows:
        n = 2 * t + half
        away = pl.ds(rows_of(half, 1 - keep1[half]), 96)
        first[n] = remote(peak_ref.at[:, t, away, :], r1.at[n], s1.at[n], q1.at[n], one[half])
        first[n].start()

    second = {}
    for t, half in flows:
        n = 2 * t + half
        first[n].wait_recv()
        kept = rows_of(half, keep1[half])

        def merge(index, part, n=n, t=t, kept=kept):
            local = pl.multiple_of(part * 48 + index * 8, 8)
            here = pl.ds(pl.multiple_of(kept + local, 8), 8)
            a = peak_ref[0, t, here, :]
            b = peak_ref[1, t, here, :]
            c = r1[n, 0, pl.ds(local, 8), :]
            d = r1[n, 1, pl.ds(local, 8), :]
            total = (a + b) + (c + d)
            middle = total * 0.25
            a = a - middle
            b = b - middle
            c = c - middle
            d = d - middle
            st[n, 0, pl.ds(local, 8), :] = total
            st[n, 1, pl.ds(local, 8), :] = (a * a + b * b) + (c * c + d * d)

        def merge_part(part):
            lax.fori_loop(0, 6, lambda index, _: (merge(index, part), 0)[1], 0)

        merge_part(1 - keep2[half])
        away = pl.ds(pl.multiple_of((1 - keep2[half]) * 48, 8), 48)
        second[n] = remote(st.at[n, :, away, :], r2.at[n], s2.at[n], q2.at[n], two[half])
        second[n].start()
        merge_part(keep2[half])

    third = {}
    for t, half in flows:
        n = 2 * t + half
        second[n].wait_recv()
        kept = rows_of(half, keep1[half])

        def finish(index, _, n=n, t=t, kept=kept, half=half):
            offset = pl.multiple_of(index * 8, 8)
            local = pl.multiple_of(keep2[half] * 48 + offset, 8)
            own = st[n, 0, pl.ds(local, 8), :]
            other = r2[n, 0, pl.ds(offset, 8), :]
            gap = own - other
            squares = (st[n, 1, pl.ds(local, 8), :] + r2[n, 1, pl.ds(offset, 8), :]) + gap * gap * 0.125
            here = pl.ds(pl.multiple_of(kept + local, 8), 8)
            mv[0, t, here, :] = (own + other) * 0.125
            mv[1, t, here, :] = squares * 0.125
            return 0

        lax.fori_loop(0, 6, finish, 0)
        mine = pl.ds(pl.multiple_of(kept + keep2[half] * 48, 8), 48)
        third[n] = remote(mv.at[:, t, mine, :], mv.at[:, t, mine, :], s3.at[n], q3.at[n], two[half])
        third[n].start()

    fourth = {}
    for t, half in flows:
        n = 2 * t + half
        third[n].wait_recv()
        kept = pl.ds(rows_of(half, keep1[half]), 96)
        fourth[n] = remote(mv.at[:, t, kept, :], mv.at[:, t, kept, :], s4.at[n], q4.at[n], one[half])
        fourth[n].start()

    outs = []
    for t in range(3):
        for half in range(2):
            fourth[2 * t + half].wait_recv()
        part = pl.ds(128 * t, 128)
        for number, target in enumerate((mean_ref, var_ref)):
            copy = pltpu.make_async_copy(mv.at[number, t], target.at[0, :, part], osem.at[number, t])
            copy.start()
            outs.append(copy)
    for n in range(6):
        first[n].wait_send()
        second[n].wait_send()
        third[n].wait_send()
        fourth[n].wait_send()
    for copy in outs:
        copy.wait()


def reduce_members(peak):
    shape = jax.ShapeDtypeStruct((1, 384, 384), jnp.float32)
    sems = [pltpu.SemaphoreType.DMA((6,))] * 8
    return pl.pallas_call(
        reduce_kernel,
        out_shape=(shape, shape),
        in_specs=[vmem_spec()],
        out_specs=(any_spec(), any_spec()),
        scratch_shapes=[
            VMEM((6, 2, 96, 128), jnp.float32),
            VMEM((6, 2, 96, 128), jnp.float32),
            VMEM((6, 2, 48, 128), jnp.float32),
            VMEM((2, 3, 384, 128), jnp.float32),
            *sems,
            pltpu.SemaphoreType.DMA((2, 3)),
        ],
        compiler_params=pltpu.CompilerParams(
            collective_id=2, has_side_effects=True, vmem_limit_bytes=40 << 20
        ),
        name="reduce",
    )(peak)


def body(outer_source, outer_depth, wet_tiles, nest_host, nest_anchor, nest_source, nest_depth):
    eta = outer_source.reshape(2, 16, 8, 1024)
    depth = outer_depth.reshape(16, 8, 1024)
    halos = exchange_halos(eta, depth)
    level, flux, edges, pick = outer_steps(wet_tiles, nest_host, nest_anchor, eta, depth, halos)
    own = route_edges(nest_host, pick, edges)
    peak = advance_nests(own, nest_source, nest_depth)
    mean, var = reduce_members(peak)
    return (level.reshape(2, 128, 1024), flux.reshape(2, 2, 128, 1024), mean, var)


def solution(mesh):
    return jax.shard_map(
        body,
        mesh=mesh,
        in_specs=(
            P("mem", "sec", None),
            P("sec", None),
            P(),
            P(),
            P(),
            P("mem", "sec", None, None),
            P("sec", None, None),
        ),
        out_specs=(
            P("mem", "sec", None),
            P(None, "mem", "sec", None),
            P("sec", None, None),
            P("sec", None, None),
        ),
        check_vma=False,
    )
```

```python
import jax
import jax.numpy as jnp
from jax import lax
from jax.experimental import pallas as pl
from jax.experimental.pallas import tpu as pltpu
from jax.sharding import PartitionSpec as P

MESH = pl.DeviceIdType.MESH
STEPS = 3
REFINE = 6
SECTIONS = 64
X_PLANES = 4
Z_CORES = 16
STRIP = 48
BATCH = 48
VMEM = pltpu.VMEM
ANY = pl.ANY


def vmem_spec():
    return pl.BlockSpec(memory_space=pltpu.VMEM)


def smem_spec():
    return pl.BlockSpec(memory_space=pltpu.SMEM)


def any_spec():
    return pl.BlockSpec(memory_space=pl.ANY)


def halo_kernel(eta_ref, depth_ref, up_eta, dn_eta, up_depth, dn_depth, send_sem, recv_sem):
    me = lax.axis_index("sec")
    below = lax.rem(me + 1, SECTIONS)
    above = lax.rem(me + SECTIONS - 1, SECTIONS)
    barrier = pltpu.get_barrier_semaphore()
    for peer in (below, above):
        pl.semaphore_signal(barrier, inc=1, device_id={"sec": peer}, device_id_type=MESH)
    pl.semaphore_wait(barrier, 2)
    plan = (
        (eta_ref.at[:, 15], up_eta, below),
        (eta_ref.at[:, 0], dn_eta, above),
        (depth_ref.at[15], up_depth, below),
        (depth_ref.at[0], dn_depth, above),
    )
    copies = []
    for number, (source, target, peer) in enumerate(plan):
        copy = pltpu.make_async_remote_copy(
            src_ref=source,
            dst_ref=target,
            send_sem=send_sem.at[number],
            recv_sem=recv_sem.at[number],
            device_id={"sec": peer},
            device_id_type=MESH,
        )
        copy.start()
        copies.append(copy)
    for copy in copies:
        copy.wait()


def exchange_halos(eta, depth):
    rows = jax.ShapeDtypeStruct((2, 8, 1024), jnp.float32)
    coef = jax.ShapeDtypeStruct((8, 1024), jnp.float32)
    return pl.pallas_call(
        halo_kernel,
        out_shape=(rows, rows, coef, coef),
        in_specs=[any_spec()] * 2,
        out_specs=(any_spec(),) * 4,
        scratch_shapes=[pltpu.SemaphoreType.DMA((4,)), pltpu.SemaphoreType.DMA((4,))],
        compiler_params=pltpu.CompilerParams(collective_id=0, has_side_effects=True),
        name="halo",
    )(eta, depth)


def outer_kernel(
    wet_ref, host_ref, anchor_ref, eta_in, depth_in, up_eta, dn_eta, up_depth, dn_depth,
    level_ref, flux_ref, edges_ref, pick_ref,
    eta, fx, fy, dw, masks, first, last,
):
    section = lax.axis_index("sec")
    lanes = lax.broadcasted_iota(jnp.int32, (8, 1024), 1)
    subs = lax.broadcasted_iota(jnp.int32, (8, 1024), 0)

    first[section] = 0
    last[section] = 0

    def note(n, _):
        last[host_ref[n]] = n
        first[host_ref[SECTIONS - 1 - n]] = SECTIONS - 1 - n
        return 0

    lax.fori_loop(0, SECTIONS, note, 0)

    def choose(n, _):
        host = host_ref[n]
        pick_ref[n] = (host // Z_CORES) * 2 + jnp.where(first[host] == n, 0, 1)
        return 0

    lax.fori_loop(0, SECTIONS, choose, 0)

    for band in range(3):
        row = section + band - 1
        inside = (row >= 0) & (row < SECTIONS)
        row = jnp.clip(row, 0, SECTIONS - 1)
        for tile in range(8):
            flag = jnp.where(inside, wet_ref[row, tile], 0)
            masks[band, :, tile * 128 : (tile + 1) * 128] = jnp.full(
                (8, 128), flag, jnp.int32
            ).astype(jnp.float32)
    zeros = jnp.zeros((8, 1024), jnp.float32)
    masks[3] = zeros

    def band_of(k):
        return jnp.where(k == 1, 0, jnp.where(k <= 17, 1, jnp.where(k == 18, 2, 3)))

    for k, (rows, coef) in ((1, (up_eta, up_depth)), (18, (dn_eta, dn_depth))):
        mask = masks[0 if k == 1 else 2]
        dw[k] = mask * coef[...]
        for m in range(2):
            eta[m, k] = mask * rows[m]
    dw[0] = zeros
    for m in range(2):
        for k in (0, 19):
            eta[m, k] = zeros
            fx[m, k] = zeros
        fy[m, 0] = zeros
        fy[m, 19] = zeros
    dw[19] = zeros

    def fill(k, _):
        mask = masks[1]
        dw[k + 2] = mask * depth_in[k]
        for m in range(2):
            eta[m, k + 2] = mask * eta_in[m, k]
        return 0

    lax.fori_loop(0, 16, fill, 0)

    def east(x):
        return jnp.where(lanes == 1023, 0.0, pltpu.roll(x, 1023, 1))

    def west(x):
        return jnp.where(lanes == 0, 0.0, pltpu.roll(x, 1, 1))

    def south(x, following):
        return jnp.where(subs == 7, pltpu.roll(following, 7, 0), pltpu.roll(x, 7, 0))

    def north(x, previous):
        return jnp.where(subs == 0, pltpu.roll(previous, 1, 0), pltpu.roll(x, 1, 0))

    def sweep_first(k, _):
        for m in range(2):
            now = eta[m, k]
            before = eta[m, k - 1]
            fx[m, k] = -(dw[k] * (east(now) - now))
            fy[m, k - 1] = -(dw[k - 1] * (south(before, now) - before))
        return 0

    def edges(step):
        rows128 = (
            lax.broadcasted_iota(jnp.int32, (16, 8, 128), 0) * 8
            + lax.broadcasted_iota(jnp.int32, (16, 8, 128), 1)
        )
        lane16 = lax.broadcasted_iota(jnp.int32, (16, 8, 128), 2)
        lane_row = lax.broadcasted_iota(jnp.int32, (8, 128), 1)
        for slot in range(2):
            nest = (first if slot == 0 else last)[section]
            r0 = anchor_ref[nest, 0]
            c0 = anchor_ref[nest, 1]
            base = pl.multiple_of(jnp.minimum(c0 // 128, 6) * 128, 128)
            left = pl.multiple_of((c0 // 128) * 128, 128)
            right = pl.multiple_of(((c0 + 63) // 128) * 128, 128)
            for m in range(2):

                def row_of(r):
                    tile = r // 8 + 2
                    x = eta[m, tile, pl.ds(lax.rem(r, 8), 1), pl.ds(base, 256)]
                    return jnp.broadcast_to(x, (8, 256))

                shift = c0 - base
                top = pltpu.roll(row_of(r0), 256 - shift, 1)[:, :128]
                bottom = pltpu.roll(row_of(r0 + 63), lax.rem(320 - shift, 256), 1)[:, :128]
                pair = jnp.where(lane_row < 64, top, bottom)
                at = (step * 2 + m) * 2
                edges_ref[slot, at : at + 1, :] = pair[0:1]
                west_block = eta[m, 2:18, :, pl.ds(left, 128)]
                east_block = eta[m, 2:18, :, pl.ds(right, 128)]
                west_col = jnp.sum(jnp.where(lane16 == c0 - left, west_block, 0.0), axis=2, keepdims=True)
                east_col = jnp.sum(jnp.where(lane16 == c0 + 63 - right, east_block, 0.0), axis=2, keepdims=True)
                place = rows128 - r0
                both = jnp.where((lane16 == place) & (lane16 < 64), west_col, 0.0) + jnp.where(
                    (lane16 == place + 64) & (lane16 >= 64), east_col, 0.0
                )
                edges_ref[slot, at + 1 : at + 2, :] = jnp.sum(jnp.sum(both, axis=0), axis=0, keepdims=True)

    for slot in range(2):
        edges_ref[slot, 12:16, :] = jnp.zeros((4, 128), jnp.float32)
    lax.fori_loop(1, 20, sweep_first, 0)
    edges(0)

    def full_step(step):
        def body(k, carry):
            new_carry = []
            mask = masks[band_of(k)]
            for m in range(2):
                px = fx[m, k]
                py = fy[m, k]
                py_before = carry[m]
                before = eta[m, k - 1]
                now = mask * (eta[m, k] - (px - west(px)) - (py - north(py, py_before)))
                eta[m, k] = now
                fx[m, k] = px - dw[k] * (east(now) - now)
                fy[m, k - 1] = py_before - dw[k - 1] * (south(before, now) - before)
                new_carry.append(py)
            return tuple(new_carry)

        lax.fori_loop(1, 20, body, (zeros, zeros))
        edges(step)

    full_step(1)
    full_step(2)

    def emit(k, _):
        for m in range(2):
            level_ref[m, k] = eta[m, k + 2]
            flux_ref[0, m, k] = fx[m, k + 2]
            flux_ref[1, m, k] = fy[m, k + 2]
        return 0

    lax.fori_loop(0, 16, emit, 0)


def outer_steps(wet_tiles, nest_host, nest_anchor, eta, depth, halos):
    return pl.pallas_call(
        outer_kernel,
        out_shape=(
            jax.ShapeDtypeStruct((2, 16, 8, 1024), jnp.float32),
            jax.ShapeDtypeStruct((2, 2, 16, 8, 1024), jnp.float32),
            jax.ShapeDtypeStruct((2, 16, 128), jnp.float32),
            jax.ShapeDtypeStruct((SECTIONS,), jnp.int32),
        ),
        in_specs=[smem_spec()] * 3 + [vmem_spec()] * 6,
        out_specs=(vmem_spec(), vmem_spec(), vmem_spec(), smem_spec()),
        scratch_shapes=[
            VMEM((2, 20, 8, 1024), jnp.float32),
            VMEM((2, 20, 8, 1024), jnp.float32),
            VMEM((2, 20, 8, 1024), jnp.float32),
            VMEM((20, 8, 1024), jnp.float32),
            VMEM((4, 8, 1024), jnp.float32),
            pltpu.SMEM((SECTIONS,), jnp.int32),
            pltpu.SMEM((SECTIONS,), jnp.int32),
        ],
        compiler_params=pltpu.CompilerParams(vmem_limit_bytes=40 << 20),
        name="outer",
    )(wet_tiles, nest_host, nest_anchor, eta, depth, *halos)


def route_kernel(
    host_ref, pick_ref, edges_ref, out_ref,
    gathered, outgoing, incoming, send_x, recv_x, send_z, recv_z,
):
    me = lax.axis_index("sec")
    plane = me // Z_CORES
    spot = lax.rem(me, Z_CORES)
    barrier = pltpu.get_barrier_semaphore()
    for step in range(1, X_PLANES):
        peer = lax.rem(plane + step, X_PLANES) * Z_CORES + spot
        pl.semaphore_signal(barrier, inc=1, device_id={"sec": peer}, device_id_type=MESH)
    for step in range(1, Z_CORES):
        peer = plane * Z_CORES + lax.rem(spot + step, Z_CORES)
        pl.semaphore_signal(barrier, inc=1, device_id={"sec": peer}, device_id_type=MESH)
    gathered[plane] = edges_ref[...]
    pl.semaphore_wait(barrier, X_PLANES + Z_CORES - 2)

    copies = []
    for step in range(1, X_PLANES):
        peer = lax.rem(plane + step, X_PLANES) * Z_CORES + spot
        copy = pltpu.make_async_remote_copy(
            src_ref=edges_ref,
            dst_ref=gathered.at[plane],
            send_sem=send_x.at[step - 1],
            recv_sem=recv_x.at[step - 1],
            device_id={"sec": peer},
            device_id_type=MESH,
        )
        copy.start()
        copies.append(copy)
    for copy in copies:
        copy.wait()

    second = []
    for step in range(Z_CORES):
        target = lax.rem(spot + step, Z_CORES)
        choice = pick_ref[plane * Z_CORES + target]
        message = gathered[choice // 2, lax.rem(choice, 2)]
        if step == 0:
            incoming[spot] = message
            continue
        outgoing[step] = message
        copy = pltpu.make_async_remote_copy(
            src_ref=outgoing.at[step],
            dst_ref=incoming.at[spot],
            send_sem=send_z.at[step - 1],
            recv_sem=recv_z.at[step - 1],
            device_id={"sec": plane * Z_CORES + target},
            device_id_type=MESH,
        )
        copy.start()
        second.append(copy)
    for copy in second:
        copy.wait()
    out_ref[...] = incoming[lax.rem(host_ref[me], Z_CORES)]


def route_edges(nest_host, pick, edges):
    return pl.pallas_call(
        route_kernel,
        out_shape=jax.ShapeDtypeStruct((16, 128), jnp.float32),
        in_specs=[smem_spec(), smem_spec(), vmem_spec()],
        out_specs=vmem_spec(),
        scratch_shapes=[
            VMEM((X_PLANES, 2, 16, 128), jnp.float32),
            VMEM((Z_CORES, 16, 128), jnp.float32),
            VMEM((Z_CORES, 16, 128), jnp.float32),
            pltpu.SemaphoreType.DMA((X_PLANES - 1,)),
            pltpu.SemaphoreType.DMA((X_PLANES - 1,)),
            pltpu.SemaphoreType.DMA((Z_CORES - 1,)),
            pltpu.SemaphoreType.DMA((Z_CORES - 1,)),
        ],
        compiler_params=pltpu.CompilerParams(collective_id=1, has_side_effects=True),
        name="route",
    )(nest_host, pick, edges)


def lane_ids():
    return lax.broadcasted_iota(jnp.int32, (8, 128), 1)


def sub_ids():
    return lax.broadcasted_iota(jnp.int32, (8, 128), 0)


def interleave(parts):
    lane = lane_ids()
    out = []
    for t in range(3):
        origin = (3 * lax.rem((lane - t + 128) * 43, 128) + t) // 128
        mixed = jnp.where(origin == 0, parts[0], jnp.where(origin == 1, parts[1], parts[2]))
        out.append(jnp.take_along_axis(mixed, lax.rem(3 * lane + t, 128), axis=1))
    return out


def straighten(parts):
    lane = lane_ids()
    spread_parts = []
    origins = []
    for t in range(3):
        spot = lax.rem((lane - t + 128) * 43, 128)
        spread_parts.append(jnp.take_along_axis(parts[t], spot, axis=1))
        origins.append((3 * spot + t) // 128)
    return [
        jnp.where(origins[0] == t, spread_parts[0], jnp.where(origins[1] == t, spread_parts[1], spread_parts[2]))
        for t in range(3)
    ]


def spread_edges(edge_ref, cols, rows, steps):
    lane = lane_ids()
    sub = sub_ids()

    def spread(row, index):
        wide = jnp.broadcast_to(row, (8, 128))
        return jnp.take_along_axis(wide, index, axis=1)

    for step in steps:
        for m in range(2):
            at = (step * 2 + m) * 2
            level = edge_ref[at : at + 1, :]
            upright = edge_ref[at + 1 : at + 2, :]
            for q in range(8):
                cols[step, m, 0, q] = spread(upright, sub * 8 + q)
                cols[step, m, 1, q] = spread(upright, sub * 8 + q + 64)
            for side in range(2):
                for t in range(3):
                    value = spread(level, (3 * lane + t) // REFINE + 64 * side)
                    if t == 0:
                        value = jnp.where(lane == 0, cols[step, m, 0, 7 * side], value)
                    if t == 2:
                        value = jnp.where(lane == 127, cols[step, m, 1, 7 * side], value)
                    rows[step, m, side, t] = value


def force_sides(value, t, sides):
    lane = lane_ids()
    if t == 0:
        value = jnp.where(lane == 0, sides[0], value)
    if t == 2:
        value = jnp.where(lane == 127, sides[1], value)
    return value


def fix_rows(h, rows, step, m):
    sub = sub_ids()
    for t in range(3):
        h[m, 0, t] = jnp.where(sub == 0, rows[step, m, 0, t], h[m, 0, t])
        h[m, STRIP - 1, t] = jnp.where(sub == 7, rows[step, m, 1, t], h[m, STRIP - 1, t])


def load_depth(dsrc, coef, d2):
    def load(i, _):
        parts = interleave([dsrc[t, pl.ds(i, 8, stride=STRIP), :] for t in range(3)])
        for t in range(3):
            coef[i, t] = parts[t]
        d2[i] = pltpu.roll(parts[2], 1, 1)
        return 0

    lax.fori_loop(0, STRIP, load, 0, unroll=4)


def load_source(src, h, div, peak, cols, rows, m):
    def load(i, _):
        parts = interleave([src[m, t, pl.ds(i, 8, stride=STRIP), :] for t in range(3)])
        sides = [cols[0, m, side, i // REFINE] for side in range(2)]
        for t in range(3):
            value = force_sides(parts[t], t, sides)
            h[m, i, t] = value
            peak[m, i, t] = value
            div[m, i, t] = jnp.zeros((8, 128), jnp.float32)
        return 0

    lax.fori_loop(0, STRIP, load, 0, unroll=4)
    fix_rows(h, rows, 0, m)


def advance(m, start, step, carry, h, div, peak, coef, d2, cols):
    now, above = carry
    for r in range(BATCH):
        i = start + r
        if r % REFINE == 0:
            sides = [cols[step, m, side, i // REFINE] for side in range(2)]
        following = [h[m, i + 1, t] for t in range(3)]
        d = [coef[i, t] for t in range(3)]
        beyond = [now[1], now[2], pltpu.roll(now[0], 127, 1)]
        f = [d[t] * (beyond[t] - now[t]) for t in range(3)]
        behind = [d2[i] * (now[0] - pltpu.roll(now[2], 1, 1)), f[0], f[1]]
        g = []
        for t in range(3):
            g.append(d[t] * (following[t] - now[t]))
            change = div[m, i, t] - ((f[t] - behind[t]) + (g[t] - above[t]))
            value = force_sides(now[t] - change, t, sides)
            div[m, i, t] = change
            h[m, i, t] = value
            peak[m, i, t] = jnp.maximum(peak[m, i, t], value)
        now, above = following, g
    return now, above


def substeps(m, low, high, h, div, peak, coef, d2, cols, rows):
    def substep(k, _):
        step = k // REFINE
        now = [h[m, 0, t] for t in range(3)]
        above = []
        for t in range(3):
            wrapped = pltpu.roll(now[t], 7, 0)
            h[m, STRIP, t] = wrapped
            above.append(pltpu.roll(coef[STRIP - 1, t] * (wrapped - h[m, STRIP - 1, t]), 1, 0))
        lax.fori_loop(
            0,
            STRIP // BATCH,
            lambda b, c: advance(m, b * BATCH, step, c, h, div, peak, coef, d2, cols),
            (now, above),
        )
        fix_rows(h, rows, step, m)
        return 0

    lax.fori_loop(low, high, substep, 0)


def store_peak(peak, peak_ref, rows, m):
    sub = sub_ids()
    for t in range(3):
        for side, i, edge_sub in ((0, 0, 0), (1, STRIP - 1, 7)):
            top = jnp.maximum(
                jnp.maximum(rows[0, m, side, t], rows[1, m, side, t]), rows[2, m, side, t]
            )
            peak[m, i, t] = jnp.where(sub == edge_sub, top, peak[m, i, t])

    def store(i, _):
        parts = straighten([peak[m, i, t] for t in range(3)])
        for t in range(3):
            peak_ref[m, t, pl.ds(i, 8, stride=STRIP), :] = parts[t]
        return 0

    lax.fori_loop(0, STRIP, store, 0, unroll=4)


def nest_kernel(
    edge_ref, source_ref, depth_ref, peak_ref, h, div, peak, coef, d2, cols, rows, src, dsrc, sem
):
    copies = []
    for t in range(3):
        part = pl.ds(128 * t, 128)
        copies.append(pltpu.make_async_copy(depth_ref.at[0, :, part], dsrc.at[t], sem.at[6 + t]))
        for m in range(2):
            copies.append(
                pltpu.make_async_copy(source_ref.at[m, 0, :, part], src.at[m, t], sem.at[3 * m + t])
            )
    for copy in copies:
        copy.start()
    spread_edges(edge_ref, cols, rows, range(STEPS))
    for copy in copies:
        copy.wait()
    load_depth(dsrc, coef, d2)
    for m in range(2):
        load_source(src, h, div, peak, cols, rows, m)
        substeps(m, 1, STEPS * REFINE, h, div, peak, coef, d2, cols, rows)
        store_peak(peak, peak_ref, rows, m)


def advance_nests(edges, source, depth):
    return pl.pallas_call(
        nest_kernel,
        out_shape=jax.ShapeDtypeStruct((2, 3, 384, 128), jnp.float32),
        in_specs=[vmem_spec(), any_spec(), any_spec()],
        out_specs=vmem_spec(),
        scratch_shapes=[
            VMEM((2, STRIP + 1, 3, 8, 128), jnp.float32),
            VMEM((2, STRIP, 3, 8, 128), jnp.float32),
            VMEM((2, STRIP, 3, 8, 128), jnp.float32),
            VMEM((STRIP, 3, 8, 128), jnp.float32),
            VMEM((STRIP, 8, 128), jnp.float32),
            VMEM((STEPS, 2, 2, 8, 8, 128), jnp.float32),
            VMEM((STEPS, 2, 2, 3, 8, 128), jnp.float32),
            VMEM((2, 3, 384, 128), jnp.float32),
            VMEM((3, 384, 128), jnp.float32),
            pltpu.SemaphoreType.DMA((9,)),
        ],
        compiler_params=pltpu.CompilerParams(vmem_limit_bytes=40 << 20),
        name="nests",
    )(edges, source, depth)


def reduce_kernel(peak_ref, mean_ref, var_ref, r1, st, r2, mv, s1, q1, s2, q2, s3, q3, s4, q4, osem):
    m = lax.axis_index("mem")
    near = m + 1 - 2 * lax.rem(m, 2)
    far = 3 - m
    high = m // 2
    gray = lax.rem(lax.rem(m, 2) + high, 2)
    barrier = pltpu.get_barrier_semaphore()
    for peer in (near, far):
        pl.semaphore_signal(barrier, inc=1, device_id={"mem": peer}, device_id_type=MESH)
    pl.semaphore_wait(barrier, 2)

    one = (near, far)
    two = (far, near)
    keep1 = (gray, high)
    keep2 = (high, gray)

    def rows_of(half, bit1):
        return pl.multiple_of(half * 192 + bit1 * 96, 8)

    def remote(src, dst, send, recv, peer):
        return pltpu.make_async_remote_copy(
            src_ref=src, dst_ref=dst, send_sem=send, recv_sem=recv,
            device_id={"mem": peer}, device_id_type=MESH,
        )

    flows = [(t, half) for t in range(3) for half in range(2)]
    first = {}
    for t, half in flows:
        n = 2 * t + half
        away = pl.ds(rows_of(half, 1 - keep1[half]), 96)
        first[n] = remote(peak_ref.at[:, t, away, :], r1.at[n], s1.at[n], q1.at[n], one[half])
        first[n].start()

    second = {}
    for t, half in flows:
        n = 2 * t + half
        first[n].wait_recv()
        kept = rows_of(half, keep1[half])

        def merge(index, part, n=n, t=t, kept=kept):
            local = pl.multiple_of(part * 48 + index * 8, 8)
            here = pl.ds(pl.multiple_of(kept + local, 8), 8)
            a = peak_ref[0, t, here, :]
            b = peak_ref[1, t, here, :]
            c = r1[n, 0, pl.ds(local, 8), :]
            d = r1[n, 1, pl.ds(local, 8), :]
            total = (a + b) + (c + d)
            middle = total * 0.25
            a = a - middle
            b = b - middle
            c = c - middle
            d = d - middle
            st[n, 0, pl.ds(local, 8), :] = total
            st[n, 1, pl.ds(local, 8), :] = (a * a + b * b) + (c * c + d * d)

        def merge_part(part):
            lax.fori_loop(0, 6, lambda index, _: (merge(index, part), 0)[1], 0)

        merge_part(1 - keep2[half])
        away = pl.ds(pl.multiple_of((1 - keep2[half]) * 48, 8), 48)
        second[n] = remote(st.at[n, :, away, :], r2.at[n], s2.at[n], q2.at[n], two[half])
        second[n].start()
        merge_part(keep2[half])

    third = {}
    for t, half in flows:
        n = 2 * t + half
        second[n].wait_recv()
        kept = rows_of(half, keep1[half])

        def finish(index, _, n=n, t=t, kept=kept, half=half):
            offset = pl.multiple_of(index * 8, 8)
            local = pl.multiple_of(keep2[half] * 48 + offset, 8)
            own = st[n, 0, pl.ds(local, 8), :]
            other = r2[n, 0, pl.ds(offset, 8), :]
            gap = own - other
            squares = (st[n, 1, pl.ds(local, 8), :] + r2[n, 1, pl.ds(offset, 8), :]) + gap * gap * 0.125
            here = pl.ds(pl.multiple_of(kept + local, 8), 8)
            mv[0, t, here, :] = (own + other) * 0.125
            mv[1, t, here, :] = squares * 0.125
            return 0

        lax.fori_loop(0, 6, finish, 0)
        mine = pl.ds(pl.multiple_of(kept + keep2[half] * 48, 8), 48)
        third[n] = remote(mv.at[:, t, mine, :], mv.at[:, t, mine, :], s3.at[n], q3.at[n], two[half])
        third[n].start()

    fourth = {}
    for t, half in flows:
        n = 2 * t + half
        third[n].wait_recv()
        kept = pl.ds(rows_of(half, keep1[half]), 96)
        fourth[n] = remote(mv.at[:, t, kept, :], mv.at[:, t, kept, :], s4.at[n], q4.at[n], one[half])
        fourth[n].start()

    outs = []
    for t in range(3):
        for half in range(2):
            fourth[2 * t + half].wait_recv()
        part = pl.ds(128 * t, 128)
        for number, target in enumerate((mean_ref, var_ref)):
            copy = pltpu.make_async_copy(mv.at[number, t], target.at[0, :, part], osem.at[number, t])
            copy.start()
            outs.append(copy)
    for n in range(6):
        first[n].wait_send()
        second[n].wait_send()
        third[n].wait_send()
        fourth[n].wait_send()
    for copy in outs:
        copy.wait()


def reduce_members(peak):
    shape = jax.ShapeDtypeStruct((1, 384, 384), jnp.float32)
    sems = [pltpu.SemaphoreType.DMA((6,))] * 8
    return pl.pallas_call(
        reduce_kernel,
        out_shape=(shape, shape),
        in_specs=[vmem_spec()],
        out_specs=(any_spec(), any_spec()),
        scratch_shapes=[
            VMEM((6, 2, 96, 128), jnp.float32),
            VMEM((6, 2, 96, 128), jnp.float32),
            VMEM((6, 2, 48, 128), jnp.float32),
            VMEM((2, 3, 384, 128), jnp.float32),
            *sems,
            pltpu.SemaphoreType.DMA((2, 3)),
        ],
        compiler_params=pltpu.CompilerParams(
            collective_id=2, has_side_effects=True, vmem_limit_bytes=40 << 20
        ),
        name="reduce",
    )(peak)


def body(outer_source, outer_depth, wet_tiles, nest_host, nest_anchor, nest_source, nest_depth):
    eta = outer_source.reshape(2, 16, 8, 1024)
    depth = outer_depth.reshape(16, 8, 1024)
    halos = exchange_halos(eta, depth)
    level, flux, edges, pick = outer_steps(wet_tiles, nest_host, nest_anchor, eta, depth, halos)
    own = route_edges(nest_host, pick, edges)
    peak = advance_nests(own, nest_source, nest_depth)
    mean, var = reduce_members(peak)
    return (level.reshape(2, 128, 1024), flux.reshape(2, 2, 128, 1024), mean, var)


def solution(mesh):
    return jax.shard_map(
        body,
        mesh=mesh,
        in_specs=(
            P("mem", "sec", None),
            P("sec", None),
            P(),
            P(),
            P(),
            P("mem", "sec", None, None),
            P("sec", None, None),
        ),
        out_specs=(
            P("mem", "sec", None),
            P(None, "mem", "sec", None),
            P("sec", None, None),
            P("sec", None, None),
        ),
        check_vma=False,
    )
```

```python
import jax
import jax.numpy as jnp
from jax import lax
from jax.experimental import pallas as pl
from jax.experimental.pallas import tpu as pltpu
from jax.sharding import PartitionSpec as P

MESH = pl.DeviceIdType.MESH
STEPS = 3
REFINE = 6
SECTIONS = 64
X_PLANES = 4
Z_CORES = 16
STRIP = 48
BATCH = 48
VMEM = pltpu.VMEM
ANY = pl.ANY


def vmem_spec():
    return pl.BlockSpec(memory_space=pltpu.VMEM)


def smem_spec():
    return pl.BlockSpec(memory_space=pltpu.SMEM)


def any_spec():
    return pl.BlockSpec(memory_space=pl.ANY)


def halo_kernel(eta_ref, depth_ref, up_eta, dn_eta, up_depth, dn_depth, send_sem, recv_sem):
    me = lax.axis_index("sec")
    below = lax.rem(me + 1, SECTIONS)
    above = lax.rem(me + SECTIONS - 1, SECTIONS)
    barrier = pltpu.get_barrier_semaphore()
    for peer in (below, above):
        pl.semaphore_signal(barrier, inc=1, device_id={"sec": peer}, device_id_type=MESH)
    pl.semaphore_wait(barrier, 2)
    plan = (
        (eta_ref.at[:, 15], up_eta, below),
        (eta_ref.at[:, 0], dn_eta, above),
        (depth_ref.at[15], up_depth, below),
        (depth_ref.at[0], dn_depth, above),
    )
    copies = []
    for number, (source, target, peer) in enumerate(plan):
        copy = pltpu.make_async_remote_copy(
            src_ref=source,
            dst_ref=target,
            send_sem=send_sem.at[number],
            recv_sem=recv_sem.at[number],
            device_id={"sec": peer},
            device_id_type=MESH,
        )
        copy.start()
        copies.append(copy)
    for copy in copies:
        copy.wait()


def exchange_halos(eta, depth):
    rows = jax.ShapeDtypeStruct((2, 8, 1024), jnp.float32)
    coef = jax.ShapeDtypeStruct((8, 1024), jnp.float32)
    return pl.pallas_call(
        halo_kernel,
        out_shape=(rows, rows, coef, coef),
        in_specs=[any_spec()] * 2,
        out_specs=(any_spec(),) * 4,
        scratch_shapes=[pltpu.SemaphoreType.DMA((4,)), pltpu.SemaphoreType.DMA((4,))],
        compiler_params=pltpu.CompilerParams(collective_id=0, has_side_effects=True),
        name="halo",
    )(eta, depth)


def outer_kernel(
    wet_ref, host_ref, anchor_ref, eta_in, depth_in, up_eta, dn_eta, up_depth, dn_depth,
    level_ref, flux_ref, edges_ref, pick_ref,
    eta, fx, fy, dw, masks, first, last,
):
    section = lax.axis_index("sec")
    lanes = lax.broadcasted_iota(jnp.int32, (8, 1024), 1)
    subs = lax.broadcasted_iota(jnp.int32, (8, 1024), 0)

    first[section] = 0
    last[section] = 0

    def note(n, _):
        last[host_ref[n]] = n
        first[host_ref[SECTIONS - 1 - n]] = SECTIONS - 1 - n
        return 0

    lax.fori_loop(0, SECTIONS, note, 0)

    def choose(n, _):
        host = host_ref[n]
        pick_ref[n] = (host // Z_CORES) * 2 + jnp.where(first[host] == n, 0, 1)
        return 0

    lax.fori_loop(0, SECTIONS, choose, 0)

    for band in range(3):
        row = section + band - 1
        inside = (row >= 0) & (row < SECTIONS)
        row = jnp.clip(row, 0, SECTIONS - 1)
        for tile in range(8):
            flag = jnp.where(inside, wet_ref[row, tile], 0)
            masks[band, :, tile * 128 : (tile + 1) * 128] = jnp.full(
                (8, 128), flag, jnp.int32
            ).astype(jnp.float32)
    zeros = jnp.zeros((8, 1024), jnp.float32)
    masks[3] = zeros

    def band_of(k):
        return jnp.where(k == 1, 0, jnp.where(k <= 17, 1, jnp.where(k == 18, 2, 3)))

    for k, (rows, coef) in ((1, (up_eta, up_depth)), (18, (dn_eta, dn_depth))):
        mask = masks[0 if k == 1 else 2]
        dw[k] = mask * coef[...]
        for m in range(2):
            eta[m, k] = mask * rows[m]
    dw[0] = zeros
    for m in range(2):
        for k in (0, 19):
            eta[m, k] = zeros
            fx[m, k] = zeros
        fy[m, 0] = zeros
        fy[m, 19] = zeros
    dw[19] = zeros

    def fill(k, _):
        mask = masks[1]
        dw[k + 2] = mask * depth_in[k]
        for m in range(2):
            eta[m, k + 2] = mask * eta_in[m, k]
        return 0

    lax.fori_loop(0, 16, fill, 0)

    def east(x):
        return jnp.where(lanes == 1023, 0.0, pltpu.roll(x, 1023, 1))

    def west(x):
        return jnp.where(lanes == 0, 0.0, pltpu.roll(x, 1, 1))

    def south(x, following):
        return jnp.where(subs == 7, pltpu.roll(following, 7, 0), pltpu.roll(x, 7, 0))

    def north(x, previous):
        return jnp.where(subs == 0, pltpu.roll(previous, 1, 0), pltpu.roll(x, 1, 0))

    def sweep_first(k, _):
        for m in range(2):
            now = eta[m, k]
            before = eta[m, k - 1]
            fx[m, k] = -(dw[k] * (east(now) - now))
            fy[m, k - 1] = -(dw[k - 1] * (south(before, now) - before))
        return 0

    def edges(step):
        rows128 = (
            lax.broadcasted_iota(jnp.int32, (16, 8, 128), 0) * 8
            + lax.broadcasted_iota(jnp.int32, (16, 8, 128), 1)
        )
        lane16 = lax.broadcasted_iota(jnp.int32, (16, 8, 128), 2)
        lane_row = lax.broadcasted_iota(jnp.int32, (8, 128), 1)
        for slot in range(2):
            nest = (first if slot == 0 else last)[section]
            r0 = anchor_ref[nest, 0]
            c0 = anchor_ref[nest, 1]
            base = pl.multiple_of(jnp.minimum(c0 // 128, 6) * 128, 128)
            left = pl.multiple_of((c0 // 128) * 128, 128)
            right = pl.multiple_of(((c0 + 63) // 128) * 128, 128)
            for m in range(2):

                def row_of(r):
                    tile = r // 8 + 2
                    x = eta[m, tile, pl.ds(lax.rem(r, 8), 1), pl.ds(base, 256)]
                    return jnp.broadcast_to(x, (8, 256))

                shift = c0 - base
                top = pltpu.roll(row_of(r0), 256 - shift, 1)[:, :128]
                bottom = pltpu.roll(row_of(r0 + 63), lax.rem(320 - shift, 256), 1)[:, :128]
                pair = jnp.where(lane_row < 64, top, bottom)
                at = (step * 2 + m) * 2
                edges_ref[slot, at : at + 1, :] = pair[0:1]
                west_block = eta[m, 2:18, :, pl.ds(left, 128)]
                east_block = eta[m, 2:18, :, pl.ds(right, 128)]
                west_col = jnp.sum(jnp.where(lane16 == c0 - left, west_block, 0.0), axis=2, keepdims=True)
                east_col = jnp.sum(jnp.where(lane16 == c0 + 63 - right, east_block, 0.0), axis=2, keepdims=True)
                place = rows128 - r0
                both = jnp.where((lane16 == place) & (lane16 < 64), west_col, 0.0) + jnp.where(
                    (lane16 == place + 64) & (lane16 >= 64), east_col, 0.0
                )
                edges_ref[slot, at + 1 : at + 2, :] = jnp.sum(jnp.sum(both, axis=0), axis=0, keepdims=True)

    for slot in range(2):
        edges_ref[slot, 12:16, :] = jnp.zeros((4, 128), jnp.float32)
    lax.fori_loop(1, 20, sweep_first, 0)
    edges(0)

    def full_step(step):
        def body(k, carry):
            new_carry = []
            mask = masks[band_of(k)]
            for m in range(2):
                px = fx[m, k]
                py = fy[m, k]
                py_before = carry[m]
                before = eta[m, k - 1]
                now = mask * (eta[m, k] - (px - west(px)) - (py - north(py, py_before)))
                eta[m, k] = now
                fx[m, k] = px - dw[k] * (east(now) - now)
                fy[m, k - 1] = py_before - dw[k - 1] * (south(before, now) - before)
                new_carry.append(py)
            return tuple(new_carry)

        lax.fori_loop(1, 20, body, (zeros, zeros))
        edges(step)

    full_step(1)
    full_step(2)

    def emit(k, _):
        for m in range(2):
            level_ref[m, k] = eta[m, k + 2]
            flux_ref[0, m, k] = fx[m, k + 2]
            flux_ref[1, m, k] = fy[m, k + 2]
        return 0

    lax.fori_loop(0, 16, emit, 0)


def outer_steps(wet_tiles, nest_host, nest_anchor, eta, depth, halos):
    return pl.pallas_call(
        outer_kernel,
        out_shape=(
            jax.ShapeDtypeStruct((2, 16, 8, 1024), jnp.float32),
            jax.ShapeDtypeStruct((2, 2, 16, 8, 1024), jnp.float32),
            jax.ShapeDtypeStruct((2, 16, 128), jnp.float32),
            jax.ShapeDtypeStruct((SECTIONS,), jnp.int32),
        ),
        in_specs=[smem_spec()] * 3 + [vmem_spec()] * 6,
        out_specs=(vmem_spec(), vmem_spec(), vmem_spec(), smem_spec()),
        scratch_shapes=[
            VMEM((2, 20, 8, 1024), jnp.float32),
            VMEM((2, 20, 8, 1024), jnp.float32),
            VMEM((2, 20, 8, 1024), jnp.float32),
            VMEM((20, 8, 1024), jnp.float32),
            VMEM((4, 8, 1024), jnp.float32),
            pltpu.SMEM((SECTIONS,), jnp.int32),
            pltpu.SMEM((SECTIONS,), jnp.int32),
        ],
        compiler_params=pltpu.CompilerParams(vmem_limit_bytes=40 << 20),
        name="outer",
    )(wet_tiles, nest_host, nest_anchor, eta, depth, *halos)


def lane_ids():
    return lax.broadcasted_iota(jnp.int32, (8, 128), 1)


def sub_ids():
    return lax.broadcasted_iota(jnp.int32, (8, 128), 0)


def interleave(parts):
    lane = lane_ids()
    out = []
    for t in range(3):
        origin = (3 * lax.rem((lane - t + 128) * 43, 128) + t) // 128
        mixed = jnp.where(origin == 0, parts[0], jnp.where(origin == 1, parts[1], parts[2]))
        out.append(jnp.take_along_axis(mixed, lax.rem(3 * lane + t, 128), axis=1))
    return out


def straighten(parts):
    lane = lane_ids()
    spread_parts = []
    origins = []
    for t in range(3):
        spot = lax.rem((lane - t + 128) * 43, 128)
        spread_parts.append(jnp.take_along_axis(parts[t], spot, axis=1))
        origins.append((3 * spot + t) // 128)
    return [
        jnp.where(origins[0] == t, spread_parts[0], jnp.where(origins[1] == t, spread_parts[1], spread_parts[2]))
        for t in range(3)
    ]


def spread_edges(edge_ref, cols, rows, steps):
    lane = lane_ids()
    sub = sub_ids()

    def spread(row, index):
        wide = jnp.broadcast_to(row, (8, 128))
        return jnp.take_along_axis(wide, index, axis=1)

    for step in steps:
        for m in range(2):
            at = (step * 2 + m) * 2
            level = edge_ref[at : at + 1, :]
            upright = edge_ref[at + 1 : at + 2, :]
            for q in range(8):
                cols[step, m, 0, q] = spread(upright, sub * 8 + q)
                cols[step, m, 1, q] = spread(upright, sub * 8 + q + 64)
            for side in range(2):
                for t in range(3):
                    value = spread(level, (3 * lane + t) // REFINE + 64 * side)
                    if t == 0:
                        value = jnp.where(lane == 0, cols[step, m, 0, 7 * side], value)
                    if t == 2:
                        value = jnp.where(lane == 127, cols[step, m, 1, 7 * side], value)
                    rows[step, m, side, t] = value


def force_sides(value, t, sides):
    lane = lane_ids()
    if t == 0:
        value = jnp.where(lane == 0, sides[0], value)
    if t == 2:
        value = jnp.where(lane == 127, sides[1], value)
    return value


def fix_rows(h, rows, step, m):
    sub = sub_ids()
    for t in range(3):
        h[m, 0, t] = jnp.where(sub == 0, rows[step, m, 0, t], h[m, 0, t])
        h[m, STRIP - 1, t] = jnp.where(sub == 7, rows[step, m, 1, t], h[m, STRIP - 1, t])


def load_depth(dsrc, coef, d2):
    def load(i, _):
        parts = interleave([dsrc[t, pl.ds(i, 8, stride=STRIP), :] for t in range(3)])
        for t in range(3):
            coef[i, t] = parts[t]
        d2[i] = pltpu.roll(parts[2], 1, 1)
        return 0

    lax.fori_loop(0, STRIP, load, 0, unroll=4)


def load_source(src, h, div, m):
    def load(i, _):
        parts = interleave([src[m, t, pl.ds(i, 8, stride=STRIP), :] for t in range(3)])
        for t in range(3):
            h[m, i, t] = parts[t]
            div[m, i, t] = jnp.zeros((8, 128), jnp.float32)
        return 0

    lax.fori_loop(0, STRIP, load, 0, unroll=4)


def first_substep(h, peak, cols, rows, m):
    def start(q, _):
        sides = [cols[0, m, side, q] for side in range(2)]
        for r in range(REFINE):
            for t in range(3):
                i = q * REFINE + r
                value = force_sides(h[m, i, t], t, sides)
                if t != 1:
                    h[m, i, t] = value
                peak[m, i, t] = value
        return 0

    lax.fori_loop(0, STRIP // REFINE, start, 0)
    fix_rows(h, rows, 0, m)


def advance(m, start, step, carry, h, div, peak, coef, d2, cols):
    now, above = carry
    for r in range(BATCH):
        i = start + r
        if r % REFINE == 0:
            sides = [cols[step, m, side, i // REFINE] for side in range(2)]
        following = [h[m, i + 1, t] for t in range(3)]
        d = [coef[i, t] for t in range(3)]
        beyond = [now[1], now[2], pltpu.roll(now[0], 127, 1)]
        f = [d[t] * (beyond[t] - now[t]) for t in range(3)]
        behind = [d2[i] * (now[0] - pltpu.roll(now[2], 1, 1)), f[0], f[1]]
        g = []
        for t in range(3):
            g.append(d[t] * (following[t] - now[t]))
            change = div[m, i, t] - ((f[t] - behind[t]) + (g[t] - above[t]))
            value = force_sides(now[t] - change, t, sides)
            div[m, i, t] = change
            h[m, i, t] = value
            peak[m, i, t] = jnp.maximum(peak[m, i, t], value)
        now, above = following, g
    return now, above


def substeps(m, low, high, h, div, peak, coef, d2, cols, rows):
    def substep(k, _):
        step = k // REFINE
        now = [h[m, 0, t] for t in range(3)]
        above = []
        for t in range(3):
            wrapped = pltpu.roll(now[t], 7, 0)
            h[m, STRIP, t] = wrapped
            above.append(pltpu.roll(coef[STRIP - 1, t] * (wrapped - h[m, STRIP - 1, t]), 1, 0))
        lax.fori_loop(
            0,
            STRIP // BATCH,
            lambda b, c: advance(m, b * BATCH, step, c, h, div, peak, coef, d2, cols),
            (now, above),
        )
        fix_rows(h, rows, step, m)
        return 0

    lax.fori_loop(low, high, substep, 0)


def store_peak(peak, peak_ref, rows, m):
    sub = sub_ids()
    for t in range(3):
        for side, i, edge_sub in ((0, 0, 0), (1, STRIP - 1, 7)):
            top = jnp.maximum(
                jnp.maximum(rows[0, m, side, t], rows[1, m, side, t]), rows[2, m, side, t]
            )
            peak[m, i, t] = jnp.where(sub == edge_sub, top, peak[m, i, t])

    def store(i, _):
        parts = straighten([peak[m, i, t] for t in range(3)])
        for t in range(3):
            peak_ref[m, t, pl.ds(i, 8, stride=STRIP), :] = parts[t]
        return 0

    lax.fori_loop(0, STRIP, store, 0, unroll=4)


def coast_kernel(
    host_ref, pick_ref, edges_ref, source_ref, depth_ref, mean_ref, var_ref,
    gathered, outgoing, incoming, own_edge,
    h, div, peak, coef, d2, cols, rows, src, dsrc, pn,
    r1, st, r2, mv,
    load_sem, send_x, recv_x, send_z, recv_z, s1, q1, s2, q2, s3, q3, s4, q4, osem,
):
    sec = lax.axis_index("sec")
    plane = sec // Z_CORES
    spot = lax.rem(sec, Z_CORES)
    mem = lax.axis_index("mem")
    near = mem + 1 - 2 * lax.rem(mem, 2)
    far = 3 - mem
    high = mem // 2
    gray = lax.rem(lax.rem(mem, 2) + high, 2)

    loads = []
    for t in range(3):
        part = pl.ds(128 * t, 128)
        loads.append(pltpu.make_async_copy(depth_ref.at[0, :, part], dsrc.at[t], load_sem.at[t]))
    for m in range(2):
        for t in range(3):
            part = pl.ds(128 * t, 128)
            loads.append(
                pltpu.make_async_copy(
                    source_ref.at[m, 0, :, part], src.at[m, t], load_sem.at[3 + 3 * m + t]
                )
            )
    for copy in loads:
        copy.start()

    barrier = pltpu.get_barrier_semaphore()
    for step in range(1, X_PLANES):
        peer = lax.rem(plane + step, X_PLANES) * Z_CORES + spot
        pl.semaphore_signal(barrier, inc=1, device_id={"sec": peer}, device_id_type=MESH)
    for step in range(1, Z_CORES):
        peer = plane * Z_CORES + lax.rem(spot + step, Z_CORES)
        pl.semaphore_signal(barrier, inc=1, device_id={"sec": peer}, device_id_type=MESH)
    for peer in (near, far):
        pl.semaphore_signal(barrier, inc=1, device_id={"mem": peer}, device_id_type=MESH)
    gathered[plane] = edges_ref[...]
    pl.semaphore_wait(barrier, X_PLANES + Z_CORES)

    along_x = []
    for step in range(1, X_PLANES):
        peer = lax.rem(plane + step, X_PLANES) * Z_CORES + spot
        copy = pltpu.make_async_remote_copy(
            src_ref=edges_ref,
            dst_ref=gathered.at[plane],
            send_sem=send_x.at[step - 1],
            recv_sem=recv_x.at[step - 1],
            device_id={"sec": peer},
            device_id_type=MESH,
        )
        copy.start()
        along_x.append(copy)
    for copy in loads[:3]:
        copy.wait()
    load_depth(dsrc, coef, d2)
    for copy in along_x:
        copy.wait()
    along_z = []
    for step in range(Z_CORES):
        target = lax.rem(spot + step, Z_CORES)
        choice = pick_ref[plane * Z_CORES + target]
        message = gathered[choice // 2, lax.rem(choice, 2)]
        if step == 0:
            incoming[spot] = message
            continue
        outgoing[step] = message
        copy = pltpu.make_async_remote_copy(
            src_ref=outgoing.at[step],
            dst_ref=incoming.at[spot],
            send_sem=send_z.at[step - 1],
            recv_sem=recv_z.at[step - 1],
            device_id={"sec": plane * Z_CORES + target},
            device_id_type=MESH,
        )
        copy.start()
        along_z.append(copy)
    for copy in loads[3:]:
        copy.wait()
    for m in range(2):
        load_source(src, h, div, m)
    for copy in along_z:
        copy.wait()
    own_edge[...] = incoming[lax.rem(host_ref[sec], Z_CORES)]
    spread_edges(own_edge, cols, rows, range(STEPS))

    one = (near, far)
    two = (far, near)
    keep1 = (gray, high)
    keep2 = (high, gray)
    flows = [(t, half) for t in range(3) for half in range(2)]

    def rows_of(half, bit1):
        return pl.multiple_of(half * 192 + bit1 * 96, 8)

    def remote(src_ref, dst_ref, send, recv, peer):
        return pltpu.make_async_remote_copy(
            src_ref=src_ref, dst_ref=dst_ref, send_sem=send, recv_sem=recv,
            device_id={"mem": peer}, device_id_type=MESH,
        )

    first = {}
    for m in range(2):
        first_substep(h, peak, cols, rows, m)
        substeps(m, 1, STEPS * REFINE, h, div, peak, coef, d2, cols, rows)
        store_peak(peak, pn, rows, m)
        for t, half in flows:
            n = 2 * t + half
            away = pl.ds(rows_of(half, 1 - keep1[half]), 96)
            first[m, n] = remote(pn.at[m, t, away, :], r1.at[n, m], s1.at[n, m], q1.at[n, m], one[half])
            first[m, n].start()

    second = {}
    for t, half in flows:
        n = 2 * t + half
        for m in range(2):
            first[m, n].wait_recv()
        kept = rows_of(half, keep1[half])

        def merge_part(part, n=n, t=t, kept=kept):
            for index in range(6):
                local = pl.multiple_of(part * 48 + index * 8, 8)
                here = pl.ds(pl.multiple_of(kept + local, 8), 8)
                a = pn[0, t, here, :]
                b = pn[1, t, here, :]
                c = r1[n, 0, pl.ds(local, 8), :]
                d = r1[n, 1, pl.ds(local, 8), :]
                total = (a + b) + (c + d)
                middle = total * 0.25
                a = a - middle
                b = b - middle
                c = c - middle
                d = d - middle
                st[n, 0, pl.ds(local, 8), :] = total
                st[n, 1, pl.ds(local, 8), :] = (a * a + b * b) + (c * c + d * d)

        merge_part(1 - keep2[half])
        away = pl.ds(pl.multiple_of((1 - keep2[half]) * 48, 8), 48)
        second[n] = remote(st.at[n, :, away, :], r2.at[n], s2.at[n], q2.at[n], two[half])
        second[n].start()
        merge_part(keep2[half])

    third = {}
    for t, half in flows:
        n = 2 * t + half
        second[n].wait_recv()
        kept = rows_of(half, keep1[half])
        for index in range(6):
            offset = index * 8
            local = pl.multiple_of(keep2[half] * 48 + offset, 8)
            mine = st[n, 0, pl.ds(local, 8), :]
            other = r2[n, 0, offset : offset + 8, :]
            gap = mine - other
            squares = (st[n, 1, pl.ds(local, 8), :] + r2[n, 1, offset : offset + 8, :]) + gap * gap * 0.125
            here = pl.ds(pl.multiple_of(kept + local, 8), 8)
            mv[0, t, here, :] = (mine + other) * 0.125
            mv[1, t, here, :] = squares * 0.125
        block = pl.ds(pl.multiple_of(kept + keep2[half] * 48, 8), 48)
        third[n] = remote(mv.at[:, t, block, :], mv.at[:, t, block, :], s3.at[n], q3.at[n], two[half])
        third[n].start()

    fourth = {}
    for t, half in flows:
        n = 2 * t + half
        third[n].wait_recv()
        kept = pl.ds(rows_of(half, keep1[half]), 96)
        fourth[n] = remote(mv.at[:, t, kept, :], mv.at[:, t, kept, :], s4.at[n], q4.at[n], one[half])
        fourth[n].start()

    outs = []
    for t in range(3):
        for half in range(2):
            fourth[2 * t + half].wait_recv()
        part = pl.ds(128 * t, 128)
        for number, target in enumerate((mean_ref, var_ref)):
            copy = pltpu.make_async_copy(mv.at[number, t], target.at[0, :, part], osem.at[number, t])
            copy.start()
            outs.append(copy)
    for n in range(6):
        for m in range(2):
            first[m, n].wait_send()
        second[n].wait_send()
        third[n].wait_send()
        fourth[n].wait_send()
    for copy in outs:
        copy.wait()


def advance_coast(nest_host, pick, edges, source, depth):
    shape = jax.ShapeDtypeStruct((1, 384, 384), jnp.float32)
    dma = pltpu.SemaphoreType.DMA
    return pl.pallas_call(
        coast_kernel,
        out_shape=(shape, shape),
        in_specs=[smem_spec(), smem_spec(), vmem_spec(), any_spec(), any_spec()],
        out_specs=(any_spec(), any_spec()),
        scratch_shapes=[
            VMEM((X_PLANES, 2, 16, 128), jnp.float32),
            VMEM((Z_CORES, 16, 128), jnp.float32),
            VMEM((Z_CORES, 16, 128), jnp.float32),
            VMEM((16, 128), jnp.float32),
            VMEM((2, STRIP + 1, 3, 8, 128), jnp.float32),
            VMEM((2, STRIP, 3, 8, 128), jnp.float32),
            VMEM((2, STRIP, 3, 8, 128), jnp.float32),
            VMEM((STRIP, 3, 8, 128), jnp.float32),
            VMEM((STRIP, 8, 128), jnp.float32),
            VMEM((STEPS, 2, 2, 8, 8, 128), jnp.float32),
            VMEM((STEPS, 2, 2, 3, 8, 128), jnp.float32),
            VMEM((2, 3, 384, 128), jnp.float32),
            VMEM((3, 384, 128), jnp.float32),
            VMEM((2, 3, 384, 128), jnp.float32),
            VMEM((6, 2, 96, 128), jnp.float32),
            VMEM((6, 2, 96, 128), jnp.float32),
            VMEM((6, 2, 48, 128), jnp.float32),
            VMEM((2, 3, 384, 128), jnp.float32),
            dma((9,)),
            dma((X_PLANES - 1,)),
            dma((X_PLANES - 1,)),
            dma((Z_CORES - 1,)),
            dma((Z_CORES - 1,)),
            dma((6, 2)),
            dma((6, 2)),
            *([dma((6,))] * 6),
            dma((2, 3)),
        ],
        compiler_params=pltpu.CompilerParams(
            collective_id=1, has_side_effects=True, vmem_limit_bytes=40 << 20
        ),
        name="coast",
    )(nest_host, pick, edges, source, depth)


def body(outer_source, outer_depth, wet_tiles, nest_host, nest_anchor, nest_source, nest_depth):
    eta = outer_source.reshape(2, 16, 8, 1024)
    depth = outer_depth.reshape(16, 8, 1024)
    halos = exchange_halos(eta, depth)
    level, flux, edges, pick = outer_steps(wet_tiles, nest_host, nest_anchor, eta, depth, halos)
    mean, var = advance_coast(nest_host, pick, edges, nest_source, nest_depth)
    return (level.reshape(2, 128, 1024), flux.reshape(2, 2, 128, 1024), mean, var)


def solution(mesh):
    return jax.shard_map(
        body,
        mesh=mesh,
        in_specs=(
            P("mem", "sec", None),
            P("sec", None),
            P(),
            P(),
            P(),
            P("mem", "sec", None, None),
            P("sec", None, None),
        ),
        out_specs=(
            P("mem", "sec", None),
            P(None, "mem", "sec", None),
            P("sec", None, None),
            P("sec", None, None),
        ),
        check_vma=False,
    )
```

```python
import jax
import jax.numpy as jnp
from jax import lax
from jax.experimental import pallas as pl
from jax.experimental.pallas import tpu as pltpu
from jax.sharding import PartitionSpec as P

MESH = pl.DeviceIdType.MESH
STEPS = 3
REFINE = 6
SECTIONS = 64
X_PLANES = 4
Z_CORES = 16
STRIP = 48
BATCH = 48
VMEM = pltpu.VMEM


def vmem_spec():
    return pl.BlockSpec(memory_space=pltpu.VMEM)


def smem_spec():
    return pl.BlockSpec(memory_space=pltpu.SMEM)


def hbm_spec():
    return pl.BlockSpec(memory_space=pltpu.HBM)


def halo_kernel(eta_ref, depth_ref, up_eta, dn_eta, up_depth, dn_depth, send_sem, recv_sem):
    me = lax.axis_index("sec")
    below = lax.rem(me + 1, SECTIONS)
    above = lax.rem(me + SECTIONS - 1, SECTIONS)
    barrier = pltpu.get_barrier_semaphore()
    for peer in (below, above):
        pl.semaphore_signal(barrier, inc=1, device_id={"sec": peer}, device_id_type=MESH)
    pl.semaphore_wait(barrier, 2)
    bottom = pl.ds(960, 64)
    top = pl.ds(0, 64)
    plan = (
        (eta_ref.at[:, bottom, :], up_eta, below),
        (eta_ref.at[:, top, :], dn_eta, above),
        (depth_ref.at[bottom, :], up_depth, below),
        (depth_ref.at[top, :], dn_depth, above),
    )
    copies = []
    for number, (source, target, peer) in enumerate(plan):
        copy = pltpu.make_async_remote_copy(
            src_ref=source,
            dst_ref=target,
            send_sem=send_sem.at[number],
            recv_sem=recv_sem.at[number],
            device_id={"sec": peer},
            device_id_type=MESH,
        )
        copy.start()
        copies.append(copy)
    for copy in copies:
        copy.wait()


def exchange_halos(eta, depth):
    rows = jax.ShapeDtypeStruct((2, 64, 128), jnp.float32)
    coef = jax.ShapeDtypeStruct((64, 128), jnp.float32)
    return pl.pallas_call(
        halo_kernel,
        out_shape=(rows, rows, coef, coef),
        in_specs=[hbm_spec()] * 2,
        out_specs=(hbm_spec(),) * 4,
        scratch_shapes=[pltpu.SemaphoreType.DMA((4,)), pltpu.SemaphoreType.DMA((4,))],
        compiler_params=pltpu.CompilerParams(collective_id=0, has_side_effects=True),
        name="halo",
    )(eta, depth)


LOW = 2
ROWS_HELD = 21


def outer_kernel(
    wet_hbm, host_hbm, anchor_hbm, eta_hbm, depth_hbm, up_eta_hbm, dn_eta_hbm, up_depth_hbm, dn_depth_hbm,
    level_hbm, flux_hbm, edges_ref, pick_ref,
    eta_in, depth_in, up_eta, dn_eta, up_depth, dn_depth, wet, host, anchor,
    eta, fx, fy, dw, masks, levels, flux_out, first, last,
    in_sem, out_sem,
):
    section = lax.axis_index("sec")
    lane = lane_ids()
    sub = sub_ids()
    loads = [
        pltpu.make_async_copy(source, target, in_sem.at[number])
        for number, (source, target) in enumerate(
            (
                (wet_hbm, wet),
                (host_hbm, host),
                (anchor_hbm, anchor),
                (depth_hbm, depth_in),
                (up_depth_hbm, up_depth),
                (dn_depth_hbm, dn_depth),
                (eta_hbm, eta_in),
                (up_eta_hbm, up_eta),
                (dn_eta_hbm, dn_eta),
            )
        )
    ]
    for copy in loads:
        copy.start()
    for copy in loads[:3]:
        copy.wait()

    first[section] = 0
    last[section] = 0

    def note(n, _):
        last[host[n]] = n
        first[host[SECTIONS - 1 - n]] = SECTIONS - 1 - n
        return 0

    lax.fori_loop(0, SECTIONS, note, 0, unroll=8)

    def choose(n, _):
        section_of = host[n]
        pick_ref[n] = (section_of // Z_CORES) * 2 + jnp.where(first[section_of] == n, 0, 1)
        return 0

    lax.fori_loop(0, SECTIONS, choose, 0, unroll=8)

    def flag(row, t):
        inside = (row >= 0) & (row < SECTIONS)
        value = jnp.where(inside, wet[t, jnp.clip(row, 0, SECTIONS - 1)], 0)
        return jnp.full((8, 128), value, jnp.int32).astype(jnp.float32)

    for t in range(8):
        own = flag(section, t)
        masks[0, t] = jnp.where(sub == 0, flag(section - 1, t), own)
        masks[1, t] = own
        masks[2, t] = jnp.where(sub == 7, flag(section + 1, t), own)

    def strip(ref, i, t):
        return ref[pl.ds((i // 8) * 64 + t * 8 + i % 8, 8, stride=128), :]

    def held(ref, before, after, i, t):
        if i < 0:
            edge = before[t * 8 + 8 + i : t * 8 + 9 + i, :]
            return jnp.where(sub == 0, jnp.broadcast_to(edge, (8, 128)), pltpu.roll(strip(ref, i + 16, t), 1, 0))
        if i > 15:
            edge = after[t * 8 + i - 16 : t * 8 + i - 15, :]
            return jnp.where(sub == 7, jnp.broadcast_to(edge, (8, 128)), pltpu.roll(strip(ref, i - 16, t), 7, 0))
        return strip(ref, i, t)

    def mask_of(i, t):
        return masks[0 if i < 0 else 1 if i < 16 else 2, t]

    for copy in loads[3:6]:
        copy.wait()
    for i in range(-2, 18):
        for t in range(8):
            dw[i + LOW, t] = mask_of(i, t) * held(depth_in, up_depth, dn_depth, i, t)

    def east_change(now):
        rolled = [pltpu.roll(now[t], 127, 1) for t in range(8)]
        out = []
        for t in range(8):
            beyond = jnp.where(lane == 127, 0.0 if t == 7 else rolled[t + 1], rolled[t])
            out.append(beyond - now[t])
        return out

    def west_change(flow):
        rolled = [pltpu.roll(flow[t], 1, 1) for t in range(8)]
        out = []
        for t in range(8):
            behind = jnp.where(lane == 0, 0.0 if t == 0 else rolled[t - 1], rolled[t])
            out.append(flow[t] - behind)
        return out

    def place(ref, i, t, value):
        ref[pl.ds((i // 8) * 64 + t * 8 + i % 8, 8, stride=128), :] = value

    def edges(m, step):
        level = levels.at[m]
        for slot in range(2):
            nest = (first if slot == 0 else last)[section]
            r0 = anchor[0, nest]
            c0 = anchor[1, nest]
            shift = lax.rem(c0, 128)
            t0 = c0 // 128
            t1 = jnp.minimum(t0 + 1, 7)
            t2 = (c0 + 63) // 128

            def row_of(r, offset):
                spot = lane - offset + shift
                index = lax.rem(spot + 128, 128)
                at = (r // 8) * 64 + lax.rem(r, 8)
                here = jnp.broadcast_to(level[pl.ds(at + t0 * 8, 1), :], (8, 128))
                there = jnp.broadcast_to(level[pl.ds(at + t1 * 8, 1), :], (8, 128))
                return jnp.where(
                    spot < 128,
                    jnp.take_along_axis(here, index, axis=1),
                    jnp.take_along_axis(there, index, axis=1),
                )

            pair = jnp.where(lane < 64, row_of(r0, 0), row_of(r0 + 63, 64))
            edges_ref[slot, m, 2 * step : 2 * step + 1, :] = pair[0:1]
            total = jnp.zeros((8, 128), jnp.float32)
            for tile in range(16):
                west_block = level[pl.ds(pl.multiple_of(tile * 64 + t0 * 8, 8), 8), :]
                east_block = level[pl.ds(pl.multiple_of(tile * 64 + t2 * 8, 8), 8), :]
                west_col = jnp.take_along_axis(west_block, jnp.full((8, 128), shift, jnp.int32), axis=1)
                east_col = jnp.take_along_axis(
                    east_block, jnp.full((8, 128), lax.rem(c0 + 63, 128), jnp.int32), axis=1
                )
                column = jnp.where(lane < 64, west_col, east_col)
                row = tile * 8 + sub - r0
                wanted = (row >= 0) & (row < 64) & (lax.rem(lane, 64) == row)
                total = total + jnp.where(wanted, column, 0.0)
            edges_ref[slot, m, 2 * step + 1 : 2 * step + 2, :] = jnp.sum(total, axis=0, keepdims=True)

    for slot in range(2):
        for m in range(2):
            edges_ref[slot, m, 6:8, :] = jnp.zeros((2, 128), jnp.float32)
    for copy in loads[6:]:
        copy.wait()

    def member(m, _):
        before = None
        for i in range(-2, 19):
            now = [
                mask_of(i, t) * held(eta_in.at[m], up_eta.at[m], dn_eta.at[m], i, t) for t in range(8)
            ]
            change = east_change(now) if -1 <= i <= 17 else None
            for t in range(8):
                eta[i + LOW, t] = now[t]
                if 0 <= i <= 15:
                    place(levels.at[m], i, t, now[t])
                if change is not None:
                    fx[i + LOW, t] = -(dw[i + LOW, t] * change[t])
                if before is not None:
                    fy[i - 1 + LOW, t] = -(dw[i - 1 + LOW, t] * (now[t] - before[t]))
            before = now
        edges(m, 0)

        for step, low, high in ((1, -1, 17), (2, 0, 16)):
            before = None
            flow_before = [fy[low - 1 + LOW, t] for t in range(8)]
            for i in range(low, high + 1):
                px = [fx[i + LOW, t] for t in range(8)]
                py = [fy[i + LOW, t] for t in range(8)]
                leave = west_change(px)
                now = [
                    mask_of(i, t) * (eta[i + LOW, t] - leave[t] - (py[t] - flow_before[t])) for t in range(8)
                ]
                change = east_change(now) if (0 if step == 1 else low) <= i < high or step == 1 else None
                for t in range(8):
                    if step == 1:
                        eta[i + LOW, t] = now[t]
                    if 0 <= i <= 15:
                        place(levels.at[m], i, t, now[t])
                    if change is not None:
                        value = px[t] - dw[i + LOW, t] * change[t]
                        if step == 1:
                            fx[i + LOW, t] = value
                        else:
                            place(flux_out.at[0, m], i, t, value)
                    if before is not None:
                        value = flow_before[t] - dw[i - 1 + LOW, t] * (now[t] - before[t])
                        if step == 1:
                            fy[i - 1 + LOW, t] = value
                        else:
                            place(flux_out.at[1, m], i - 1, t, value)
                before = now
                flow_before = py
            if step == 2:
                pltpu.make_async_copy(levels.at[m], level_hbm.at[m], out_sem.at[0, m]).start()
                for side in range(2):
                    pltpu.make_async_copy(
                        flux_out.at[side, m], flux_hbm.at[side, m], out_sem.at[1 + side, m]
                    ).start()
            edges(m, step)
        return 0

    lax.fori_loop(0, 2, member, 0)
    for m in range(2):
        pltpu.make_async_copy(levels.at[m], level_hbm.at[m], out_sem.at[0, m]).wait()
        for side in range(2):
            pltpu.make_async_copy(
                flux_out.at[side, m], flux_hbm.at[side, m], out_sem.at[1 + side, m]
            ).wait()


def outer_steps(wet_tiles, nest_host, nest_anchor, eta, depth, halos):
    f32 = jnp.float32
    return pl.pallas_call(
        outer_kernel,
        out_shape=(
            jax.ShapeDtypeStruct((2, 1024, 128), f32),
            jax.ShapeDtypeStruct((2, 2, 1024, 128), f32),
            jax.ShapeDtypeStruct((2, 2, 8, 128), f32),
            jax.ShapeDtypeStruct((SECTIONS,), jnp.int32),
        ),
        in_specs=[hbm_spec()] * 9,
        out_specs=(hbm_spec(), hbm_spec(), vmem_spec(), smem_spec()),
        scratch_shapes=[
            VMEM((2, 1024, 128), f32),
            VMEM((1024, 128), f32),
            VMEM((2, 64, 128), f32),
            VMEM((2, 64, 128), f32),
            VMEM((64, 128), f32),
            VMEM((64, 128), f32),
            pltpu.SMEM((8, SECTIONS), jnp.int32),
            pltpu.SMEM((SECTIONS,), jnp.int32),
            pltpu.SMEM((2, SECTIONS), jnp.int32),
            VMEM((ROWS_HELD, 8, 8, 128), f32),
            VMEM((ROWS_HELD, 8, 8, 128), f32),
            VMEM((ROWS_HELD, 8, 8, 128), f32),
            VMEM((ROWS_HELD, 8, 8, 128), f32),
            VMEM((3, 8, 8, 128), f32),
            VMEM((2, 1024, 128), f32),
            VMEM((2, 2, 1024, 128), f32),
            pltpu.SMEM((SECTIONS,), jnp.int32),
            pltpu.SMEM((SECTIONS,), jnp.int32),
            pltpu.SemaphoreType.DMA((9,)),
            pltpu.SemaphoreType.DMA((3, 2)),
        ],
        compiler_params=pltpu.CompilerParams(vmem_limit_bytes=62 << 20),
        name="outer",
    )(wet_tiles.T, nest_host, nest_anchor.T, eta, depth, *halos)


def lane_ids():
    return lax.broadcasted_iota(jnp.int32, (8, 128), 1)


def sub_ids():
    return lax.broadcasted_iota(jnp.int32, (8, 128), 0)


def interleave(parts):
    lane = lane_ids()
    out = []
    for t in range(3):
        origin = (3 * lax.rem((lane - t + 128) * 43, 128) + t) // 128
        mixed = jnp.where(origin == 0, parts[0], jnp.where(origin == 1, parts[1], parts[2]))
        out.append(jnp.take_along_axis(mixed, lax.rem(3 * lane + t, 128), axis=1))
    return out


def straighten(parts):
    lane = lane_ids()
    spread_parts = []
    origins = []
    for t in range(3):
        spot = lax.rem((lane - t + 128) * 43, 128)
        spread_parts.append(jnp.take_along_axis(parts[t], spot, axis=1))
        origins.append((3 * spot + t) // 128)
    return [
        jnp.where(origins[0] == t, spread_parts[0], jnp.where(origins[1] == t, spread_parts[1], spread_parts[2]))
        for t in range(3)
    ]


def spread_edges(edge_ref, cols, rows, steps):
    lane = lane_ids()
    sub = sub_ids()

    def spread(row, index):
        wide = jnp.broadcast_to(row, (8, 128))
        return jnp.take_along_axis(wide, index, axis=1)

    for step in steps:
        for m in range(2):
            at = m * 8 + step * 2
            level = edge_ref[at : at + 1, :]
            upright = edge_ref[at + 1 : at + 2, :]
            for q in range(8):
                cols[step, m, 0, q] = spread(upright, sub * 8 + q)
                cols[step, m, 1, q] = spread(upright, sub * 8 + q + 64)
            for side in range(2):
                for t in range(3):
                    value = spread(level, (3 * lane + t) // REFINE + 64 * side)
                    if t == 0:
                        value = jnp.where(lane == 0, cols[step, m, 0, 7 * side], value)
                    if t == 2:
                        value = jnp.where(lane == 127, cols[step, m, 1, 7 * side], value)
                    rows[step, m, side, t] = value


def force_sides(value, t, sides):
    lane = lane_ids()
    if t == 0:
        value = jnp.where(lane == 0, sides[0], value)
    if t == 2:
        value = jnp.where(lane == 127, sides[1], value)
    return value


def fix_rows(h, rows, step, m):
    sub = sub_ids()
    for t in range(3):
        h[m, 0, t] = jnp.where(sub == 0, rows[step, m, 0, t], h[m, 0, t])
        h[m, STRIP - 1, t] = jnp.where(sub == 7, rows[step, m, 1, t], h[m, STRIP - 1, t])


def load_depth(dsrc, coef, d2):
    def load(i, _):
        parts = interleave([dsrc[t, pl.ds(i, 8, stride=STRIP), :] for t in range(3)])
        for t in range(3):
            coef[i, t] = parts[t]
        d2[i] = pltpu.roll(parts[2], 1, 1)
        return 0

    lax.fori_loop(0, STRIP, load, 0, unroll=4)


def load_source(src, h, div, m):
    def load(i, _):
        parts = interleave([src[m, t, pl.ds(i, 8, stride=STRIP), :] for t in range(3)])
        for t in range(3):
            h[m, i, t] = parts[t]
            div[m, i, t] = jnp.zeros((8, 128), jnp.float32)
        return 0

    lax.fori_loop(0, STRIP, load, 0, unroll=4)


def first_substep(h, peak, cols, rows, m):
    def start(q, _):
        sides = [cols[0, m, side, q] for side in range(2)]
        for r in range(REFINE):
            for t in range(3):
                i = q * REFINE + r
                value = force_sides(h[m, i, t], t, sides)
                if t != 1:
                    h[m, i, t] = value
                peak[m, i, t] = value
        return 0

    lax.fori_loop(0, STRIP // REFINE, start, 0)
    fix_rows(h, rows, 0, m)


def advance(m, start, step, carry, h, div, peak, coef, d2, cols):
    now, above = carry
    for r in range(BATCH):
        i = start + r
        if r % REFINE == 0:
            sides = [cols[step, m, side, i // REFINE] for side in range(2)]
        following = [h[m, i + 1, t] for t in range(3)]
        d = [coef[i, t] for t in range(3)]
        beyond = [now[1], now[2], pltpu.roll(now[0], 127, 1)]
        f = [d[t] * (beyond[t] - now[t]) for t in range(3)]
        behind = [d2[i] * (now[0] - pltpu.roll(now[2], 1, 1)), f[0], f[1]]
        g = []
        for t in range(3):
            g.append(d[t] * (following[t] - now[t]))
            change = div[m, i, t] - ((f[t] - behind[t]) + (g[t] - above[t]))
            value = force_sides(now[t] - change, t, sides)
            div[m, i, t] = change
            h[m, i, t] = value
            peak[m, i, t] = jnp.maximum(peak[m, i, t], value)
        now, above = following, g
    return now, above


def substeps(m, low, high, h, div, peak, coef, d2, cols, rows):
    def substep(k, _):
        step = k // REFINE
        now = [h[m, 0, t] for t in range(3)]
        above = []
        for t in range(3):
            wrapped = pltpu.roll(now[t], 7, 0)
            h[m, STRIP, t] = wrapped
            above.append(pltpu.roll(coef[STRIP - 1, t] * (wrapped - h[m, STRIP - 1, t]), 1, 0))
        lax.fori_loop(
            0,
            STRIP // BATCH,
            lambda b, c: advance(m, b * BATCH, step, c, h, div, peak, coef, d2, cols),
            (now, above),
        )
        fix_rows(h, rows, step, m)
        return 0

    lax.fori_loop(low, high, substep, 0)


def store_peak(peak, peak_ref, rows, m):
    sub = sub_ids()
    for t in range(3):
        for side, i, edge_sub in ((0, 0, 0), (1, STRIP - 1, 7)):
            top = jnp.maximum(
                jnp.maximum(rows[0, m, side, t], rows[1, m, side, t]), rows[2, m, side, t]
            )
            peak[m, i, t] = jnp.where(sub == edge_sub, top, peak[m, i, t])

    def store(i, _):
        parts = straighten([peak[m, i, t] for t in range(3)])
        for t in range(3):
            peak_ref[m, t, pl.ds(i, 8, stride=STRIP), :] = parts[t]
        return 0

    lax.fori_loop(0, STRIP, store, 0, unroll=4)


def coast_kernel(
    host_ref, pick_ref, edges_ref, source_ref, depth_ref, mean_ref, var_ref,
    gathered, outgoing, incoming, own_edge,
    h, div, peak, coef, d2, cols, rows, src, dsrc, pn,
    r1, st, r2, mv,
    load_sem, send_x, recv_x, send_z, recv_z, s1, q1, s2, q2, s3, q3, s4, q4, osem,
):
    sec = lax.axis_index("sec")
    plane = sec // Z_CORES
    spot = lax.rem(sec, Z_CORES)
    mem = lax.axis_index("mem")
    near = mem + 1 - 2 * lax.rem(mem, 2)
    far = 3 - mem
    high = mem // 2
    gray = lax.rem(lax.rem(mem, 2) + high, 2)

    loads = []
    for t in range(3):
        part = pl.ds(128 * t, 128)
        loads.append(pltpu.make_async_copy(depth_ref.at[0, :, part], dsrc.at[t], load_sem.at[t]))
    for m in range(2):
        for t in range(3):
            part = pl.ds(128 * t, 128)
            loads.append(
                pltpu.make_async_copy(
                    source_ref.at[m, 0, :, part], src.at[m, t], load_sem.at[3 + 3 * m + t]
                )
            )
    for copy in loads:
        copy.start()

    barrier = pltpu.get_barrier_semaphore()
    for step in range(1, X_PLANES):
        peer = lax.rem(plane + step, X_PLANES) * Z_CORES + spot
        pl.semaphore_signal(barrier, inc=1, device_id={"sec": peer}, device_id_type=MESH)
    for step in range(1, Z_CORES):
        peer = plane * Z_CORES + lax.rem(spot + step, Z_CORES)
        pl.semaphore_signal(barrier, inc=1, device_id={"sec": peer}, device_id_type=MESH)
    for peer in (near, far):
        pl.semaphore_signal(barrier, inc=1, device_id={"mem": peer}, device_id_type=MESH)
    gathered[plane] = edges_ref[...]
    pl.semaphore_wait(barrier, X_PLANES + Z_CORES)

    along_x = []
    for step in range(1, X_PLANES):
        peer = lax.rem(plane + step, X_PLANES) * Z_CORES + spot
        copy = pltpu.make_async_remote_copy(
            src_ref=edges_ref,
            dst_ref=gathered.at[plane],
            send_sem=send_x.at[step - 1],
            recv_sem=recv_x.at[step - 1],
            device_id={"sec": peer},
            device_id_type=MESH,
        )
        copy.start()
        along_x.append(copy)
    for copy in loads[:3]:
        copy.wait()
    load_depth(dsrc, coef, d2)
    for copy in along_x:
        copy.wait()
    along_z = []
    for step in range(Z_CORES):
        target = lax.rem(spot + step, Z_CORES)
        choice = pick_ref[plane * Z_CORES + target]
        message = gathered[choice // 2, lax.rem(choice, 2)]
        if step == 0:
            incoming[spot] = message
            continue
        outgoing[step] = message
        copy = pltpu.make_async_remote_copy(
            src_ref=outgoing.at[step],
            dst_ref=incoming.at[spot],
            send_sem=send_z.at[step - 1],
            recv_sem=recv_z.at[step - 1],
            device_id={"sec": plane * Z_CORES + target},
            device_id_type=MESH,
        )
        copy.start()
        along_z.append(copy)
    for copy in loads[3:]:
        copy.wait()
    for m in range(2):
        load_source(src, h, div, m)
    for copy in along_z:
        copy.wait()
    own_edge[...] = incoming[lax.rem(host_ref[sec], Z_CORES)]
    spread_edges(own_edge, cols, rows, range(STEPS))

    one = (near, far)
    two = (far, near)
    keep1 = (gray, high)
    keep2 = (high, gray)
    flows = [(t, half) for t in range(3) for half in range(2)]

    def rows_of(half, bit1):
        return pl.multiple_of(half * 192 + bit1 * 96, 8)

    def remote(src_ref, dst_ref, send, recv, peer):
        return pltpu.make_async_remote_copy(
            src_ref=src_ref, dst_ref=dst_ref, send_sem=send, recv_sem=recv,
            device_id={"mem": peer}, device_id_type=MESH,
        )

    first = {}
    for m in range(2):
        first_substep(h, peak, cols, rows, m)
        substeps(m, 1, STEPS * REFINE, h, div, peak, coef, d2, cols, rows)
        store_peak(peak, pn, rows, m)
        for t, half in flows:
            n = 2 * t + half
            away = pl.ds(rows_of(half, 1 - keep1[half]), 96)
            first[m, n] = remote(pn.at[m, t, away, :], r1.at[n, m], s1.at[n, m], q1.at[n, m], one[half])
            first[m, n].start()

    second = {}
    for t, half in flows:
        n = 2 * t + half
        for m in range(2):
            first[m, n].wait_recv()
        kept = rows_of(half, keep1[half])

        def merge_part(part, n=n, t=t, kept=kept):
            for index in range(6):
                local = pl.multiple_of(part * 48 + index * 8, 8)
                here = pl.ds(pl.multiple_of(kept + local, 8), 8)
                a = pn[0, t, here, :]
                b = pn[1, t, here, :]
                c = r1[n, 0, pl.ds(local, 8), :]
                d = r1[n, 1, pl.ds(local, 8), :]
                total = (a + b) + (c + d)
                middle = total * 0.25
                a = a - middle
                b = b - middle
                c = c - middle
                d = d - middle
                st[n, 0, pl.ds(local, 8), :] = total
                st[n, 1, pl.ds(local, 8), :] = (a * a + b * b) + (c * c + d * d)

        merge_part(1 - keep2[half])
        away = pl.ds(pl.multiple_of((1 - keep2[half]) * 48, 8), 48)
        second[n] = remote(st.at[n, :, away, :], r2.at[n], s2.at[n], q2.at[n], two[half])
        second[n].start()
        merge_part(keep2[half])

    third = {}
    for t, half in flows:
        n = 2 * t + half
        second[n].wait_recv()
        kept = rows_of(half, keep1[half])
        for index in range(6):
            offset = index * 8
            local = pl.multiple_of(keep2[half] * 48 + offset, 8)
            mine = st[n, 0, pl.ds(local, 8), :]
            other = r2[n, 0, offset : offset + 8, :]
            gap = mine - other
            squares = (st[n, 1, pl.ds(local, 8), :] + r2[n, 1, offset : offset + 8, :]) + gap * gap * 0.125
            here = pl.ds(pl.multiple_of(kept + local, 8), 8)
            mv[0, t, here, :] = (mine + other) * 0.125
            mv[1, t, here, :] = squares * 0.125
        block = pl.ds(pl.multiple_of(kept + keep2[half] * 48, 8), 48)
        third[n] = remote(mv.at[:, t, block, :], mv.at[:, t, block, :], s3.at[n], q3.at[n], two[half])
        third[n].start()

    fourth = {}
    for t, half in flows:
        n = 2 * t + half
        third[n].wait_recv()
        kept = pl.ds(rows_of(half, keep1[half]), 96)
        fourth[n] = remote(mv.at[:, t, kept, :], mv.at[:, t, kept, :], s4.at[n], q4.at[n], one[half])
        fourth[n].start()

    outs = []
    for t in range(3):
        for half in range(2):
            fourth[2 * t + half].wait_recv()
        part = pl.ds(128 * t, 128)
        for number, target in enumerate((mean_ref, var_ref)):
            copy = pltpu.make_async_copy(mv.at[number, t], target.at[0, :, part], osem.at[number, t])
            copy.start()
            outs.append(copy)
    for n in range(6):
        for m in range(2):
            first[m, n].wait_send()
        second[n].wait_send()
        third[n].wait_send()
        fourth[n].wait_send()
    for copy in outs:
        copy.wait()


def advance_coast(nest_host, pick, edges, source, depth):
    shape = jax.ShapeDtypeStruct((1, 384, 384), jnp.float32)
    dma = pltpu.SemaphoreType.DMA
    return pl.pallas_call(
        coast_kernel,
        out_shape=(shape, shape),
        in_specs=[smem_spec(), smem_spec(), vmem_spec(), hbm_spec(), hbm_spec()],
        out_specs=(hbm_spec(), hbm_spec()),
        scratch_shapes=[
            VMEM((X_PLANES, 2, 16, 128), jnp.float32),
            VMEM((Z_CORES, 16, 128), jnp.float32),
            VMEM((Z_CORES, 16, 128), jnp.float32),
            VMEM((16, 128), jnp.float32),
            VMEM((2, STRIP + 1, 3, 8, 128), jnp.float32),
            VMEM((2, STRIP, 3, 8, 128), jnp.float32),
            VMEM((2, STRIP, 3, 8, 128), jnp.float32),
            VMEM((STRIP, 3, 8, 128), jnp.float32),
            VMEM((STRIP, 8, 128), jnp.float32),
            VMEM((STEPS, 2, 2, 8, 8, 128), jnp.float32),
            VMEM((STEPS, 2, 2, 3, 8, 128), jnp.float32),
            VMEM((2, 3, 384, 128), jnp.float32),
            VMEM((3, 384, 128), jnp.float32),
            VMEM((2, 3, 384, 128), jnp.float32),
            VMEM((6, 2, 96, 128), jnp.float32),
            VMEM((6, 2, 96, 128), jnp.float32),
            VMEM((6, 2, 48, 128), jnp.float32),
            VMEM((2, 3, 384, 128), jnp.float32),
            dma((9,)),
            dma((X_PLANES - 1,)),
            dma((X_PLANES - 1,)),
            dma((Z_CORES - 1,)),
            dma((Z_CORES - 1,)),
            dma((6, 2)),
            dma((6, 2)),
            *([dma((6,))] * 6),
            dma((2, 3)),
        ],
        compiler_params=pltpu.CompilerParams(
            collective_id=1, has_side_effects=True, vmem_limit_bytes=62 << 20
        ),
        name="coast",
    )(nest_host, pick, edges, source, depth)


def tiled(field):
    lead = field.shape[:-2]
    n = len(lead)
    split = field.reshape(*lead, 16, 8, 8, 128)
    return jnp.swapaxes(split, n + 1, n + 2).reshape(*lead, 1024, 128)


def untiled(field):
    lead = field.shape[:-2]
    n = len(lead)
    split = field.reshape(*lead, 16, 8, 8, 128)
    return jnp.swapaxes(split, n + 1, n + 2).reshape(*lead, 128, 1024)


def body(outer_source, outer_depth, wet_tiles, nest_host, nest_anchor, nest_source, nest_depth):
    eta = tiled(outer_source)
    depth = tiled(outer_depth)
    halos = exchange_halos(eta, depth)
    level, flux, edges, pick = outer_steps(wet_tiles, nest_host, nest_anchor, eta, depth, halos)
    edges = edges.reshape(2, 16, 128)
    mean, var = advance_coast(nest_host, pick, edges, nest_source, nest_depth)
    return (untiled(level), untiled(flux), mean, var)


def solution(mesh):
    return jax.shard_map(
        body,
        mesh=mesh,
        in_specs=(
            P("mem", "sec", None),
            P("sec", None),
            P(),
            P(),
            P(),
            P("mem", "sec", None, None),
            P("sec", None, None),
        ),
        out_specs=(
            P("mem", "sec", None),
            P(None, "mem", "sec", None),
            P("sec", None, None),
            P("sec", None, None),
        ),
        check_vma=False,
    )
```

```python
import jax
import jax.numpy as jnp
from jax import lax
from jax.experimental import pallas as pl
from jax.experimental.pallas import tpu as pltpu
from jax.sharding import PartitionSpec as P

MESH = pl.DeviceIdType.MESH
STEPS = 3
REFINE = 6
SECTIONS = 64
X_PLANES = 4
Z_CORES = 16
STRIP = 48
BATCH = 48
VMEM = pltpu.VMEM


def vmem_spec():
    return pl.BlockSpec(memory_space=pltpu.VMEM)


def smem_spec():
    return pl.BlockSpec(memory_space=pltpu.SMEM)


def hbm_spec():
    return pl.BlockSpec(memory_space=pltpu.HBM)


def halo_kernel(eta_ref, depth_ref, up_eta, dn_eta, up_depth, dn_depth, send_sem, recv_sem):
    me = lax.axis_index("sec")
    below = lax.rem(me + 1, SECTIONS)
    above = lax.rem(me + SECTIONS - 1, SECTIONS)
    barrier = pltpu.get_barrier_semaphore()
    for peer in (below, above):
        pl.semaphore_signal(barrier, inc=1, device_id={"sec": peer}, device_id_type=MESH)
    pl.semaphore_wait(barrier, 2)
    bottom = pl.ds(960, 64)
    top = pl.ds(0, 64)
    plan = (
        (eta_ref.at[:, bottom, :], up_eta, below),
        (eta_ref.at[:, top, :], dn_eta, above),
        (depth_ref.at[bottom, :], up_depth, below),
        (depth_ref.at[top, :], dn_depth, above),
    )
    copies = []
    for number, (source, target, peer) in enumerate(plan):
        copy = pltpu.make_async_remote_copy(
            src_ref=source,
            dst_ref=target,
            send_sem=send_sem.at[number],
            recv_sem=recv_sem.at[number],
            device_id={"sec": peer},
            device_id_type=MESH,
        )
        copy.start()
        copies.append(copy)
    for copy in copies:
        copy.wait()


def exchange_halos(eta, depth):
    rows = jax.ShapeDtypeStruct((2, 64, 128), jnp.float32)
    coef = jax.ShapeDtypeStruct((64, 128), jnp.float32)
    return pl.pallas_call(
        halo_kernel,
        out_shape=(rows, rows, coef, coef),
        in_specs=[hbm_spec()] * 2,
        out_specs=(hbm_spec(),) * 4,
        scratch_shapes=[pltpu.SemaphoreType.DMA((4,)), pltpu.SemaphoreType.DMA((4,))],
        compiler_params=pltpu.CompilerParams(collective_id=0, has_side_effects=True),
        name="halo",
    )(eta, depth)


LOW = 2
ROWS_HELD = 21


def outer_kernel(
    wet_hbm, host_hbm, anchor_hbm, eta_hbm, depth_hbm, up_eta_hbm, dn_eta_hbm, up_depth_hbm, dn_depth_hbm,
    level_hbm, flux_hbm, edges_ref, pick_ref,
    eta_in, depth_in, up_eta, dn_eta, up_depth, dn_depth, wet, host, anchor,
    eta, fx, fy, dw, masks, levels, flux_out, first, last,
    in_sem, out_sem,
):
    section = lax.axis_index("sec")
    lane = lane_ids()
    sub = sub_ids()
    loads = [
        pltpu.make_async_copy(source, target, in_sem.at[number])
        for number, (source, target) in enumerate(
            (
                (wet_hbm, wet),
                (host_hbm, host),
                (anchor_hbm, anchor),
                (depth_hbm, depth_in),
                (up_depth_hbm, up_depth),
                (dn_depth_hbm, dn_depth),
                (eta_hbm, eta_in),
                (up_eta_hbm, up_eta),
                (dn_eta_hbm, dn_eta),
            )
        )
    ]
    for copy in loads:
        copy.start()
    for copy in loads[:3]:
        copy.wait()

    first[section] = 0
    last[section] = 0

    def note(n, _):
        last[host[n]] = n
        first[host[SECTIONS - 1 - n]] = SECTIONS - 1 - n
        return 0

    lax.fori_loop(0, SECTIONS, note, 0, unroll=8)

    def choose(n, _):
        section_of = host[n]
        pick_ref[n] = (section_of // Z_CORES) * 2 + jnp.where(first[section_of] == n, 0, 1)
        return 0

    lax.fori_loop(0, SECTIONS, choose, 0, unroll=8)

    def flag(row, t):
        inside = (row >= 0) & (row < SECTIONS)
        value = jnp.where(inside, wet[t, jnp.clip(row, 0, SECTIONS - 1)], 0)
        return jnp.full((8, 128), value, jnp.int32).astype(jnp.float32)

    for t in range(8):
        own = flag(section, t)
        masks[0, t] = jnp.where(sub == 0, flag(section - 1, t), own)
        masks[1, t] = own
        masks[2, t] = jnp.where(sub == 7, flag(section + 1, t), own)

    def strip(ref, i, t):
        return ref[pl.ds((i // 8) * 64 + t * 8 + i % 8, 8, stride=128), :]

    def held(ref, before, after, i, t):
        if i < 0:
            edge = before[t * 8 + 8 + i : t * 8 + 9 + i, :]
            return jnp.where(sub == 0, jnp.broadcast_to(edge, (8, 128)), pltpu.roll(strip(ref, i + 16, t), 1, 0))
        if i > 15:
            edge = after[t * 8 + i - 16 : t * 8 + i - 15, :]
            return jnp.where(sub == 7, jnp.broadcast_to(edge, (8, 128)), pltpu.roll(strip(ref, i - 16, t), 7, 0))
        return strip(ref, i, t)

    def mask_of(i, t):
        return masks[0 if i < 0 else 1 if i < 16 else 2, t]

    for copy in loads[3:6]:
        copy.wait()
    for i in range(-2, 18):
        for t in range(8):
            dw[i + LOW, t] = mask_of(i, t) * held(depth_in, up_depth, dn_depth, i, t)

    def east_change(now):
        rolled = [pltpu.roll(now[t], 127, 1) for t in range(8)]
        out = []
        for t in range(8):
            beyond = jnp.where(lane == 127, 0.0 if t == 7 else rolled[t + 1], rolled[t])
            out.append(beyond - now[t])
        return out

    def west_change(flow):
        rolled = [pltpu.roll(flow[t], 1, 1) for t in range(8)]
        out = []
        for t in range(8):
            behind = jnp.where(lane == 0, 0.0 if t == 0 else rolled[t - 1], rolled[t])
            out.append(flow[t] - behind)
        return out

    def place(ref, i, t, value):
        ref[pl.ds((i // 8) * 64 + t * 8 + i % 8, 8, stride=128), :] = value

    def edges(m, step):
        level = levels.at[m]
        for slot in range(2):
            nest = (first if slot == 0 else last)[section]
            r0 = anchor[0, nest]
            c0 = anchor[1, nest]
            shift = lax.rem(c0, 128)
            t0 = c0 // 128
            t1 = jnp.minimum(t0 + 1, 7)
            t2 = (c0 + 63) // 128

            def row_of(r, offset):
                spot = lane - offset + shift
                index = lax.rem(spot + 128, 128)
                at = (r // 8) * 64 + lax.rem(r, 8)
                here = jnp.broadcast_to(level[pl.ds(at + t0 * 8, 1), :], (8, 128))
                there = jnp.broadcast_to(level[pl.ds(at + t1 * 8, 1), :], (8, 128))
                return jnp.where(
                    spot < 128,
                    jnp.take_along_axis(here, index, axis=1),
                    jnp.take_along_axis(there, index, axis=1),
                )

            pair = jnp.where(lane < 64, row_of(r0, 0), row_of(r0 + 63, 64))
            part = 0 if step == 0 else 1
            at = 2 * m + (4 if step == 2 else 0)
            edges_ref[slot, part, pl.ds(at, 1), :] = pair[0:1]
            total = jnp.zeros((8, 128), jnp.float32)
            for tile in range(16):
                west_block = level[pl.ds(pl.multiple_of(tile * 64 + t0 * 8, 8), 8), :]
                east_block = level[pl.ds(pl.multiple_of(tile * 64 + t2 * 8, 8), 8), :]
                west_col = jnp.take_along_axis(west_block, jnp.full((8, 128), shift, jnp.int32), axis=1)
                east_col = jnp.take_along_axis(
                    east_block, jnp.full((8, 128), lax.rem(c0 + 63, 128), jnp.int32), axis=1
                )
                column = jnp.where(lane < 64, west_col, east_col)
                row = tile * 8 + sub - r0
                wanted = (row >= 0) & (row < 64) & (lax.rem(lane, 64) == row)
                total = total + jnp.where(wanted, column, 0.0)
            edges_ref[slot, part, pl.ds(at + 1, 1), :] = jnp.sum(total, axis=0, keepdims=True)

    for slot in range(2):
        edges_ref[slot, 0, 4:8, :] = jnp.zeros((4, 128), jnp.float32)
    for copy in loads[6:]:
        copy.wait()

    def member(m, _):
        before = None
        for i in range(-2, 19):
            now = [
                mask_of(i, t) * held(eta_in.at[m], up_eta.at[m], dn_eta.at[m], i, t) for t in range(8)
            ]
            change = east_change(now) if -1 <= i <= 17 else None
            for t in range(8):
                eta[i + LOW, t] = now[t]
                if 0 <= i <= 15:
                    place(levels.at[m], i, t, now[t])
                if change is not None:
                    fx[i + LOW, t] = -(dw[i + LOW, t] * change[t])
                if before is not None:
                    fy[i - 1 + LOW, t] = -(dw[i - 1 + LOW, t] * (now[t] - before[t]))
            before = now
        edges(m, 0)

        for step, low, high in ((1, -1, 17), (2, 0, 16)):
            before = None
            flow_before = [fy[low - 1 + LOW, t] for t in range(8)]
            for i in range(low, high + 1):
                px = [fx[i + LOW, t] for t in range(8)]
                py = [fy[i + LOW, t] for t in range(8)]
                leave = west_change(px)
                now = [
                    mask_of(i, t) * (eta[i + LOW, t] - leave[t] - (py[t] - flow_before[t])) for t in range(8)
                ]
                change = east_change(now) if (0 if step == 1 else low) <= i < high or step == 1 else None
                for t in range(8):
                    if step == 1:
                        eta[i + LOW, t] = now[t]
                    if 0 <= i <= 15:
                        place(levels.at[m], i, t, now[t])
                    if change is not None:
                        value = px[t] - dw[i + LOW, t] * change[t]
                        if step == 1:
                            fx[i + LOW, t] = value
                        else:
                            place(flux_out.at[0, m], i, t, value)
                    if before is not None:
                        value = flow_before[t] - dw[i - 1 + LOW, t] * (now[t] - before[t])
                        if step == 1:
                            fy[i - 1 + LOW, t] = value
                        else:
                            place(flux_out.at[1, m], i - 1, t, value)
                before = now
                flow_before = py
            if step == 2:
                pltpu.make_async_copy(levels.at[m], level_hbm.at[m], out_sem.at[0, m]).start()
                for side in range(2):
                    pltpu.make_async_copy(
                        flux_out.at[side, m], flux_hbm.at[side, m], out_sem.at[1 + side, m]
                    ).start()
            edges(m, step)
        return 0

    lax.fori_loop(0, 2, member, 0)
    for m in range(2):
        pltpu.make_async_copy(levels.at[m], level_hbm.at[m], out_sem.at[0, m]).wait()
        for side in range(2):
            pltpu.make_async_copy(
                flux_out.at[side, m], flux_hbm.at[side, m], out_sem.at[1 + side, m]
            ).wait()


def outer_steps(wet_tiles, nest_host, nest_anchor, eta, depth, halos):
    f32 = jnp.float32
    return pl.pallas_call(
        outer_kernel,
        out_shape=(
            jax.ShapeDtypeStruct((2, 1024, 128), f32),
            jax.ShapeDtypeStruct((2, 2, 1024, 128), f32),
            jax.ShapeDtypeStruct((2, 2, 8, 128), f32),
            jax.ShapeDtypeStruct((SECTIONS,), jnp.int32),
        ),
        in_specs=[hbm_spec()] * 9,
        out_specs=(hbm_spec(), hbm_spec(), vmem_spec(), smem_spec()),
        scratch_shapes=[
            VMEM((2, 1024, 128), f32),
            VMEM((1024, 128), f32),
            VMEM((2, 64, 128), f32),
            VMEM((2, 64, 128), f32),
            VMEM((64, 128), f32),
            VMEM((64, 128), f32),
            pltpu.SMEM((8, SECTIONS), jnp.int32),
            pltpu.SMEM((SECTIONS,), jnp.int32),
            pltpu.SMEM((2, SECTIONS), jnp.int32),
            VMEM((ROWS_HELD, 8, 8, 128), f32),
            VMEM((ROWS_HELD, 8, 8, 128), f32),
            VMEM((ROWS_HELD, 8, 8, 128), f32),
            VMEM((ROWS_HELD, 8, 8, 128), f32),
            VMEM((3, 8, 8, 128), f32),
            VMEM((2, 1024, 128), f32),
            VMEM((2, 2, 1024, 128), f32),
            pltpu.SMEM((SECTIONS,), jnp.int32),
            pltpu.SMEM((SECTIONS,), jnp.int32),
            pltpu.SemaphoreType.DMA((9,)),
            pltpu.SemaphoreType.DMA((3, 2)),
        ],
        compiler_params=pltpu.CompilerParams(vmem_limit_bytes=62 << 20),
        name="outer",
    )(wet_tiles.T, nest_host, nest_anchor.T, eta, depth, *halos)


def lane_ids():
    return lax.broadcasted_iota(jnp.int32, (8, 128), 1)


def sub_ids():
    return lax.broadcasted_iota(jnp.int32, (8, 128), 0)


def interleave(parts):
    lane = lane_ids()
    out = []
    for t in range(3):
        origin = (3 * lax.rem((lane - t + 128) * 43, 128) + t) // 128
        mixed = jnp.where(origin == 0, parts[0], jnp.where(origin == 1, parts[1], parts[2]))
        out.append(jnp.take_along_axis(mixed, lax.rem(3 * lane + t, 128), axis=1))
    return out


def straighten(parts):
    lane = lane_ids()
    spread_parts = []
    origins = []
    for t in range(3):
        spot = lax.rem((lane - t + 128) * 43, 128)
        spread_parts.append(jnp.take_along_axis(parts[t], spot, axis=1))
        origins.append((3 * spot + t) // 128)
    return [
        jnp.where(origins[0] == t, spread_parts[0], jnp.where(origins[1] == t, spread_parts[1], spread_parts[2]))
        for t in range(3)
    ]


def spread_edges(edge_ref, cols, rows, steps):
    lane = lane_ids()
    sub = sub_ids()

    def spread(row, index):
        wide = jnp.broadcast_to(row, (8, 128))
        return jnp.take_along_axis(wide, index, axis=1)

    for step in steps:
        for m in range(2):
            at = m * 2 + (4 if step == 2 else 0)
            level = edge_ref[at : at + 1, :]
            upright = edge_ref[at + 1 : at + 2, :]
            for q in range(8):
                cols[step, m, 0, q] = spread(upright, sub * 8 + q)
                cols[step, m, 1, q] = spread(upright, sub * 8 + q + 64)
            for side in range(2):
                for t in range(3):
                    value = spread(level, (3 * lane + t) // REFINE + 64 * side)
                    if t == 0:
                        value = jnp.where(lane == 0, cols[step, m, 0, 7 * side], value)
                    if t == 2:
                        value = jnp.where(lane == 127, cols[step, m, 1, 7 * side], value)
                    rows[step, m, side, t] = value


def force_sides(value, t, sides):
    lane = lane_ids()
    if t == 0:
        value = jnp.where(lane == 0, sides[0], value)
    if t == 2:
        value = jnp.where(lane == 127, sides[1], value)
    return value


def fix_rows(h, rows, step, m):
    sub = sub_ids()
    for t in range(3):
        h[m, 0, t] = jnp.where(sub == 0, rows[step, m, 0, t], h[m, 0, t])
        h[m, STRIP - 1, t] = jnp.where(sub == 7, rows[step, m, 1, t], h[m, STRIP - 1, t])


def load_depth(dsrc, coef, d2):
    def load(i, _):
        parts = interleave([dsrc[t, pl.ds(i, 8, stride=STRIP), :] for t in range(3)])
        for t in range(3):
            coef[i, t] = parts[t]
        d2[i] = pltpu.roll(parts[2], 1, 1)
        return 0

    lax.fori_loop(0, STRIP, load, 0, unroll=4)


def load_source(src, h, div, m):
    def load(i, _):
        parts = interleave([src[m, t, pl.ds(i, 8, stride=STRIP), :] for t in range(3)])
        for t in range(3):
            h[m, i, t] = parts[t]
            div[m, i, t] = jnp.zeros((8, 128), jnp.float32)
        return 0

    lax.fori_loop(0, STRIP, load, 0, unroll=4)


def first_substep(h, peak, cols, rows, m):
    def start(q, _):
        sides = [cols[0, m, side, q] for side in range(2)]
        for r in range(REFINE):
            for t in range(3):
                i = q * REFINE + r
                value = force_sides(h[m, i, t], t, sides)
                if t != 1:
                    h[m, i, t] = value
                peak[m, i, t] = value
        return 0

    lax.fori_loop(0, STRIP // REFINE, start, 0)
    fix_rows(h, rows, 0, m)


def advance(m, start, step, carry, h, div, peak, coef, d2, cols):
    now, above = carry
    for r in range(BATCH):
        i = start + r
        if r % REFINE == 0:
            sides = [cols[step, m, side, i // REFINE] for side in range(2)]
        following = [h[m, i + 1, t] for t in range(3)]
        d = [coef[i, t] for t in range(3)]
        beyond = [now[1], now[2], pltpu.roll(now[0], 127, 1)]
        f = [d[t] * (beyond[t] - now[t]) for t in range(3)]
        behind = [d2[i] * (now[0] - pltpu.roll(now[2], 1, 1)), f[0], f[1]]
        g = []
        for t in range(3):
            g.append(d[t] * (following[t] - now[t]))
            change = div[m, i, t] - ((f[t] - behind[t]) + (g[t] - above[t]))
            value = force_sides(now[t] - change, t, sides)
            div[m, i, t] = change
            h[m, i, t] = value
            peak[m, i, t] = jnp.maximum(peak[m, i, t], value)
        now, above = following, g
    return now, above


def substeps(m, low, high, h, div, peak, coef, d2, cols, rows):
    def substep(k, _):
        step = k // REFINE
        now = [h[m, 0, t] for t in range(3)]
        above = []
        for t in range(3):
            wrapped = pltpu.roll(now[t], 7, 0)
            h[m, STRIP, t] = wrapped
            above.append(pltpu.roll(coef[STRIP - 1, t] * (wrapped - h[m, STRIP - 1, t]), 1, 0))
        lax.fori_loop(
            0,
            STRIP // BATCH,
            lambda b, c: advance(m, b * BATCH, step, c, h, div, peak, coef, d2, cols),
            (now, above),
        )
        fix_rows(h, rows, step, m)
        return 0

    lax.fori_loop(low, high, substep, 0)


def settle_peak(peak, rows, m):
    sub = sub_ids()
    for t in range(3):
        for side, i, edge_sub in ((0, 0, 0), (1, STRIP - 1, 7)):
            top = jnp.maximum(
                jnp.maximum(rows[0, m, side, t], rows[1, m, side, t]), rows[2, m, side, t]
            )
            peak[m, i, t] = jnp.where(sub == edge_sub, top, peak[m, i, t])


def coast_kernel(
    host_ref, pick_ref, edges_ref, source_ref, depth_ref, mean_ref, var_ref,
    gathered, outgoing, incoming_first, incoming_later, own_edge,
    h, div, peak, coef, d2, cols, rows, src, dsrc,
    r1, st, r2, mv,
    load_sem, send_x, recv_x, send_z, recv_z, s1, q1, s2, q2, s3, q3, s4, q4,
):
    sec = lax.axis_index("sec")
    plane = sec // Z_CORES
    spot = lax.rem(sec, Z_CORES)
    mem = lax.axis_index("mem")
    near = mem + 1 - 2 * lax.rem(mem, 2)
    far = 3 - mem
    high = mem // 2
    gray = lax.rem(lax.rem(mem, 2) + high, 2)

    loads = []
    for t in range(3):
        part = pl.ds(128 * t, 128)
        loads.append(pltpu.make_async_copy(depth_ref.at[0, :, part], dsrc.at[t], load_sem.at[t]))
    for m in range(2):
        for t in range(3):
            part = pl.ds(128 * t, 128)
            loads.append(
                pltpu.make_async_copy(
                    source_ref.at[m, 0, :, part], src.at[m, t], load_sem.at[3 + 3 * m + t]
                )
            )
    for copy in loads:
        copy.start()

    barrier = pltpu.get_barrier_semaphore()
    for step in range(1, X_PLANES):
        peer = lax.rem(plane + step, X_PLANES) * Z_CORES + spot
        pl.semaphore_signal(barrier, inc=1, device_id={"sec": peer}, device_id_type=MESH)
    for step in range(1, Z_CORES):
        peer = plane * Z_CORES + lax.rem(spot + step, Z_CORES)
        pl.semaphore_signal(barrier, inc=1, device_id={"sec": peer}, device_id_type=MESH)
    for peer in (near, far):
        pl.semaphore_signal(barrier, inc=1, device_id={"mem": peer}, device_id_type=MESH)
    gathered[plane] = edges_ref[...]
    pl.semaphore_wait(barrier, X_PLANES + Z_CORES)

    along_x = []
    for step in range(1, X_PLANES):
        peer = lax.rem(plane + step, X_PLANES) * Z_CORES + spot
        copy = pltpu.make_async_remote_copy(
            src_ref=edges_ref,
            dst_ref=gathered.at[plane],
            send_sem=send_x.at[step - 1],
            recv_sem=recv_x.at[step - 1],
            device_id={"sec": peer},
            device_id_type=MESH,
        )
        copy.start()
        along_x.append(copy)
    for copy in loads[:3]:
        copy.wait()
    load_depth(dsrc, coef, d2)
    for copy in along_x:
        copy.wait()
    along_z = []
    incoming = (incoming_first, incoming_later)
    for part in range(2):
        for step in range(Z_CORES):
            target = lax.rem(spot + step, Z_CORES)
            choice = pick_ref[plane * Z_CORES + target]
            message = gathered[choice // 2, lax.rem(choice, 2), part]
            if step == 0:
                incoming[part][spot] = message
                continue
            outgoing[part, step] = message
            copy = pltpu.make_async_remote_copy(
                src_ref=outgoing.at[part, step],
                dst_ref=incoming[part].at[spot],
                send_sem=send_z.at[part, step - 1],
                recv_sem=recv_z.at[part, step - 1],
                device_id={"sec": plane * Z_CORES + target},
                device_id_type=MESH,
            )
            copy.start()
            along_z.append(copy)
    for copy in loads[3:]:
        copy.wait()
    for m in range(2):
        load_source(src, h, div, m)
    host_spot = lax.rem(host_ref[sec], Z_CORES)
    for copy in along_z[: Z_CORES - 1]:
        copy.wait_recv()
    own_edge[0] = incoming_first[host_spot]
    spread_edges(own_edge.at[0], cols, rows, (0,))

    def early(m, _):
        first_substep(h, peak, cols, rows, m)
        substeps(m, 1, REFINE, h, div, peak, coef, d2, cols, rows)
        return 0

    lax.fori_loop(0, 2, early, 0)
    for copy in along_z[Z_CORES - 1 :]:
        copy.wait_recv()
    own_edge[1] = incoming_later[host_spot]
    spread_edges(own_edge.at[1], cols, rows, (1, 2))

    one = (near, far)
    two = (far, near)
    keep1 = (gray, high)
    keep2 = (high, gray)
    flows = [(chunk, half) for chunk in range(3) for half in range(2)]

    def quad(chunk, half, bit1):
        return half * 24 + chunk * 8 + bit1 * 4

    def remote(src_ref, dst_ref, send, recv, peer):
        return pltpu.make_async_remote_copy(
            src_ref=src_ref, dst_ref=dst_ref, send_sem=send, recv_sem=recv,
            device_id={"mem": peer}, device_id_type=MESH,
        )

    def first(m, chunk, half):
        n = 2 * chunk + half
        away = pl.ds(quad(chunk, half, 1 - keep1[half]), 4)
        return remote(peak.at[m, away], r1.at[n, m], s1.at[n, m], q1.at[n, m], one[half])

    def late(m, _):
        substeps(m, REFINE, STEPS * REFINE, h, div, peak, coef, d2, cols, rows)
        settle_peak(peak, rows, m)
        for chunk, half in flows:
            first(m, chunk, half).start()
        return 0

    lax.fori_loop(0, 2, late, 0)

    second = {}
    for chunk, half in flows:
        n = 2 * chunk + half
        for m in range(2):
            first(m, chunk, half).wait_recv()
        kept = quad(chunk, half, keep1[half])

        def merge_pair(bit2, n=n, kept=kept):
            for r in range(2):
                local = bit2 * 2 + r
                for t in range(3):
                    a = peak[0, kept + local, t]
                    b = peak[1, kept + local, t]
                    c = r1[n, 0, local, t]
                    d = r1[n, 1, local, t]
                    total = (a + b) + (c + d)
                    middle = total * 0.25
                    a = a - middle
                    b = b - middle
                    c = c - middle
                    d = d - middle
                    st[n, 0, local, t] = total
                    st[n, 1, local, t] = (a * a + b * b) + (c * c + d * d)

        merge_pair(1 - keep2[half])
        away = pl.ds((1 - keep2[half]) * 2, 2)
        second[n] = remote(st.at[n, :, away], r2.at[n], s2.at[n], q2.at[n], two[half])
        second[n].start()
        merge_pair(keep2[half])

    def straight_rows(start, count):
        for r in range(count):
            i = start + r
            for number, target in enumerate((mean_ref, var_ref)):
                parts = straighten([mv[number, i, t] for t in range(3)])
                for t in range(3):
                    target[t, pl.ds(i, 8, stride=STRIP), :] = parts[t]

    third = {}
    for chunk, half in flows:
        n = 2 * chunk + half
        second[n].wait_recv()
        pair = quad(chunk, half, keep1[half]) + keep2[half] * 2
        for r in range(2):
            local = keep2[half] * 2 + r
            for t in range(3):
                mine = st[n, 0, local, t]
                other = r2[n, 0, r, t]
                gap = mine - other
                squares = (st[n, 1, local, t] + r2[n, 1, r, t]) + gap * gap * 0.125
                mv[0, pair + r, t] = (mine + other) * 0.125
                mv[1, pair + r, t] = squares * 0.125
        block = pl.ds(pair, 2)
        third[n] = remote(mv.at[:, block], mv.at[:, block], s3.at[n], q3.at[n], two[half])
        third[n].start()

    fourth = {}
    for chunk, half in flows:
        n = 2 * chunk + half
        third[n].wait_recv()
        kept = pl.ds(quad(chunk, half, keep1[half]), 4)
        fourth[n] = remote(mv.at[:, kept], mv.at[:, kept], s4.at[n], q4.at[n], one[half])
        fourth[n].start()

    for chunk, half in flows:
        straight_rows(quad(chunk, half, keep1[half]), 4)
    for chunk, half in flows:
        n = 2 * chunk + half
        fourth[n].wait_recv()
        straight_rows(quad(chunk, half, 1 - keep1[half]), 4)
    for copy in along_z:
        copy.wait_send()
    for chunk, half in flows:
        n = 2 * chunk + half
        for m in range(2):
            first(m, chunk, half).wait_send()
        second[n].wait_send()
        third[n].wait_send()
        fourth[n].wait_send()


def advance_coast(nest_host, pick, edges, source, depth):
    shape = jax.ShapeDtypeStruct((3, 384, 128), jnp.float32)
    dma = pltpu.SemaphoreType.DMA
    return pl.pallas_call(
        coast_kernel,
        out_shape=(shape, shape),
        in_specs=[smem_spec(), smem_spec(), vmem_spec(), hbm_spec(), hbm_spec()],
        out_specs=(vmem_spec(), vmem_spec()),
        scratch_shapes=[
            VMEM((X_PLANES, 2, 2, 8, 128), jnp.float32),
            VMEM((2, Z_CORES, 8, 128), jnp.float32),
            VMEM((Z_CORES, 8, 128), jnp.float32),
            VMEM((Z_CORES, 8, 128), jnp.float32),
            VMEM((2, 8, 128), jnp.float32),
            VMEM((2, STRIP + 1, 3, 8, 128), jnp.float32),
            VMEM((2, STRIP, 3, 8, 128), jnp.float32),
            VMEM((2, STRIP, 3, 8, 128), jnp.float32),
            VMEM((STRIP, 3, 8, 128), jnp.float32),
            VMEM((STRIP, 8, 128), jnp.float32),
            VMEM((STEPS, 2, 2, 8, 8, 128), jnp.float32),
            VMEM((STEPS, 2, 2, 3, 8, 128), jnp.float32),
            VMEM((2, 3, 384, 128), jnp.float32),
            VMEM((3, 384, 128), jnp.float32),
            VMEM((6, 2, 4, 3, 8, 128), jnp.float32),
            VMEM((6, 2, 4, 3, 8, 128), jnp.float32),
            VMEM((6, 2, 2, 3, 8, 128), jnp.float32),
            VMEM((2, STRIP, 3, 8, 128), jnp.float32),
            dma((9,)),
            dma((X_PLANES - 1,)),
            dma((X_PLANES - 1,)),
            dma((2, Z_CORES - 1)),
            dma((2, Z_CORES - 1)),
            dma((6, 2)),
            dma((6, 2)),
            *([dma((6,))] * 6),
        ],
        compiler_params=pltpu.CompilerParams(
            collective_id=1, has_side_effects=True, vmem_limit_bytes=40 << 20
        ),
        name="coast",
    )(nest_host, pick, edges, source, depth)


def tiled(field):
    lead = field.shape[:-2]
    n = len(lead)
    split = field.reshape(*lead, 16, 8, 8, 128)
    return jnp.swapaxes(split, n + 1, n + 2).reshape(*lead, 1024, 128)


def untiled(field):
    lead = field.shape[:-2]
    n = len(lead)
    split = field.reshape(*lead, 16, 8, 8, 128)
    return jnp.swapaxes(split, n + 1, n + 2).reshape(*lead, 128, 1024)


def body(outer_source, outer_depth, wet_tiles, nest_host, nest_anchor, nest_source, nest_depth):
    eta = tiled(outer_source)
    depth = tiled(outer_depth)
    halos = exchange_halos(eta, depth)
    level, flux, edges, pick = outer_steps(wet_tiles, nest_host, nest_anchor, eta, depth, halos)
    mean, var = advance_coast(nest_host, pick, edges, nest_source, nest_depth)
    mean = jnp.swapaxes(mean, 0, 1).reshape(1, 384, 384)
    var = jnp.swapaxes(var, 0, 1).reshape(1, 384, 384)
    return (untiled(level), untiled(flux), mean, var)


def solution(mesh):
    return jax.shard_map(
        body,
        mesh=mesh,
        in_specs=(
            P("mem", "sec", None),
            P("sec", None),
            P(),
            P(),
            P(),
            P("mem", "sec", None, None),
            P("sec", None, None),
        ),
        out_specs=(
            P("mem", "sec", None),
            P(None, "mem", "sec", None),
            P("sec", None, None),
            P("sec", None, None),
        ),
        check_vma=False,
    )
```

```python
import jax
import jax.numpy as jnp
from jax import lax
from jax.experimental import pallas as pl
from jax.experimental.pallas import tpu as pltpu
from jax.sharding import PartitionSpec as P

MESH = pl.DeviceIdType.MESH
STEPS = 3
REFINE = 6
SECTIONS = 64
X_PLANES = 4
Z_CORES = 16
STRIP = 48
BATCH = 48
VMEM = pltpu.VMEM


def vmem_spec():
    return pl.BlockSpec(memory_space=pltpu.VMEM)


def smem_spec():
    return pl.BlockSpec(memory_space=pltpu.SMEM)


def hbm_spec():
    return pl.BlockSpec(memory_space=pltpu.HBM)


def halo_kernel(eta_ref, depth_ref, up_eta, dn_eta, up_depth, dn_depth, send_sem, recv_sem):
    me = lax.axis_index("sec")
    below = lax.rem(me + 1, SECTIONS)
    above = lax.rem(me + SECTIONS - 1, SECTIONS)
    barrier = pltpu.get_barrier_semaphore()
    for peer in (below, above):
        pl.semaphore_signal(barrier, inc=1, device_id={"sec": peer}, device_id_type=MESH)
    pl.semaphore_wait(barrier, 2)
    bottom = pl.ds(960, 64)
    top = pl.ds(0, 64)
    plan = (
        (eta_ref.at[:, bottom, :], up_eta, below),
        (eta_ref.at[:, top, :], dn_eta, above),
        (depth_ref.at[bottom, :], up_depth, below),
        (depth_ref.at[top, :], dn_depth, above),
    )
    copies = []
    for number, (source, target, peer) in enumerate(plan):
        copy = pltpu.make_async_remote_copy(
            src_ref=source,
            dst_ref=target,
            send_sem=send_sem.at[number],
            recv_sem=recv_sem.at[number],
            device_id={"sec": peer},
            device_id_type=MESH,
        )
        copy.start()
        copies.append(copy)
    for copy in copies:
        copy.wait()


def exchange_halos(eta, depth):
    rows = jax.ShapeDtypeStruct((2, 64, 128), jnp.float32)
    coef = jax.ShapeDtypeStruct((64, 128), jnp.float32)
    return pl.pallas_call(
        halo_kernel,
        out_shape=(rows, rows, coef, coef),
        in_specs=[hbm_spec()] * 2,
        out_specs=(hbm_spec(),) * 4,
        scratch_shapes=[pltpu.SemaphoreType.DMA((4,)), pltpu.SemaphoreType.DMA((4,))],
        compiler_params=pltpu.CompilerParams(collective_id=0, has_side_effects=True),
        name="halo",
    )(eta, depth)


LOW = 2
ROWS_HELD = 21


def outer_kernel(
    wet_hbm, host_hbm, anchor_hbm, eta_hbm, depth_hbm, up_eta_hbm, dn_eta_hbm, up_depth_hbm, dn_depth_hbm,
    level_hbm, flux_hbm, edges_ref, pick_ref,
    eta_in, depth_in, up_eta, dn_eta, up_depth, dn_depth, wet, host, anchor,
    eta, fx, fy, dw, masks, levels, flux_out, first, last,
    in_sem, out_sem,
):
    section = lax.axis_index("sec")
    lane = lane_ids()
    sub = sub_ids()
    loads = [
        pltpu.make_async_copy(source, target, in_sem.at[number])
        for number, (source, target) in enumerate(
            (
                (wet_hbm, wet),
                (host_hbm, host),
                (anchor_hbm, anchor),
                (depth_hbm, depth_in),
                (up_depth_hbm, up_depth),
                (dn_depth_hbm, dn_depth),
                (eta_hbm, eta_in),
                (up_eta_hbm, up_eta),
                (dn_eta_hbm, dn_eta),
            )
        )
    ]
    for copy in loads:
        copy.start()
    for copy in loads[:3]:
        copy.wait()

    first[section] = 0
    last[section] = 0

    def note(n, _):
        last[host[n]] = n
        first[host[SECTIONS - 1 - n]] = SECTIONS - 1 - n
        return 0

    lax.fori_loop(0, SECTIONS, note, 0, unroll=8)

    def choose(n, _):
        section_of = host[n]
        pick_ref[n] = (section_of // Z_CORES) * 2 + jnp.where(first[section_of] == n, 0, 1)
        return 0

    lax.fori_loop(0, SECTIONS, choose, 0, unroll=8)

    def flag(row, t):
        inside = (row >= 0) & (row < SECTIONS)
        value = jnp.where(inside, wet[t, jnp.clip(row, 0, SECTIONS - 1)], 0)
        return jnp.full((8, 128), value, jnp.int32).astype(jnp.float32)

    for t in range(8):
        own = flag(section, t)
        masks[0, t] = jnp.where(sub == 0, flag(section - 1, t), own)
        masks[1, t] = own
        masks[2, t] = jnp.where(sub == 7, flag(section + 1, t), own)

    def strip(ref, i, t):
        return ref[pl.ds((i // 8) * 64 + t * 8 + i % 8, 8, stride=128), :]

    def held(ref, before, after, i, t):
        if i < 0:
            edge = before[t * 8 + 8 + i : t * 8 + 9 + i, :]
            return jnp.where(sub == 0, jnp.broadcast_to(edge, (8, 128)), pltpu.roll(strip(ref, i + 16, t), 1, 0))
        if i > 15:
            edge = after[t * 8 + i - 16 : t * 8 + i - 15, :]
            return jnp.where(sub == 7, jnp.broadcast_to(edge, (8, 128)), pltpu.roll(strip(ref, i - 16, t), 7, 0))
        return strip(ref, i, t)

    def mask_of(i, t):
        return masks[0 if i < 0 else 1 if i < 16 else 2, t]

    for copy in loads[3:6]:
        copy.wait()
    for i in range(-2, 18):
        for t in range(8):
            dw[i + LOW, t] = mask_of(i, t) * held(depth_in, up_depth, dn_depth, i, t)

    def place(ref, i, t, value):
        ref[pl.ds((i // 8) * 64 + t * 8 + i % 8, 8, stride=128), :] = value

    def edges(m, step):
        level = levels.at[m]
        for slot in range(2):
            nest = (first if slot == 0 else last)[section]
            r0 = anchor[0, nest]
            c0 = anchor[1, nest]
            shift = lax.rem(c0, 128)
            t0 = c0 // 128
            t1 = jnp.minimum(t0 + 1, 7)
            t2 = (c0 + 63) // 128

            def row_of(r, offset):
                spot = lane - offset + shift
                index = lax.rem(spot + 128, 128)
                at = (r // 8) * 64 + lax.rem(r, 8)
                here = jnp.broadcast_to(level[pl.ds(at + t0 * 8, 1), :], (8, 128))
                there = jnp.broadcast_to(level[pl.ds(at + t1 * 8, 1), :], (8, 128))
                return jnp.where(
                    spot < 128,
                    jnp.take_along_axis(here, index, axis=1),
                    jnp.take_along_axis(there, index, axis=1),
                )

            pair = jnp.where(lane < 64, row_of(r0, 0), row_of(r0 + 63, 64))
            part = 0 if step == 0 else 1
            at = 2 * m + (4 if step == 2 else 0)
            edges_ref[slot, part, pl.ds(at, 1), :] = pair[0:1]
            total = jnp.zeros((8, 128), jnp.float32)
            for tile in range(16):
                west_block = level[pl.ds(pl.multiple_of(tile * 64 + t0 * 8, 8), 8), :]
                east_block = level[pl.ds(pl.multiple_of(tile * 64 + t2 * 8, 8), 8), :]
                west_col = jnp.take_along_axis(west_block, jnp.full((8, 128), shift, jnp.int32), axis=1)
                east_col = jnp.take_along_axis(
                    east_block, jnp.full((8, 128), lax.rem(c0 + 63, 128), jnp.int32), axis=1
                )
                column = jnp.where(lane < 64, west_col, east_col)
                row = tile * 8 + sub - r0
                wanted = (row >= 0) & (row < 64) & (lax.rem(lane, 64) == row)
                total = total + jnp.where(wanted, column, 0.0)
            edges_ref[slot, part, pl.ds(at + 1, 1), :] = jnp.sum(total, axis=0, keepdims=True)

    for slot in range(2):
        edges_ref[slot, 0, 4:8, :] = jnp.zeros((4, 128), jnp.float32)
    for copy in loads[6:]:
        copy.wait()

    def level_pass(m, low, high):
        for i in range(low, high + 1):
            carried = 0.0
            for t in range(8):
                flow = fx[i + LOW, t]
                rolled = pltpu.roll(flow, 1, 1)
                behind = jnp.where(lane == 0, carried, rolled)
                carried = rolled
                down = fy[i + LOW, t] - fy[i - 1 + LOW, t]
                now = mask_of(i, t) * (eta[i + LOW, t] - (flow - behind) - down)
                eta[i + LOW, t] = now
                if 0 <= i <= 15:
                    place(levels.at[m], i, t, now)

    def flux_pass(m, step, x_range, y_range):
        for i in range(min(x_range[0], y_range[0]), max(x_range[1], y_range[1]) + 1):
            carried = 0.0
            for t in reversed(range(8)):
                now = eta[i + LOW, t]
                coef = dw[i + LOW, t]
                if x_range[0] <= i <= x_range[1]:
                    rolled = pltpu.roll(now, 127, 1)
                    change = coef * (jnp.where(lane == 127, carried, rolled) - now)
                    carried = rolled
                    value = -change if step == 0 else fx[i + LOW, t] - change
                    if step == 2:
                        place(flux_out.at[0, m], i, t, value)
                    else:
                        fx[i + LOW, t] = value
                if y_range[0] <= i <= y_range[1]:
                    change = coef * (eta[i + 1 + LOW, t] - now)
                    value = -change if step == 0 else fy[i + LOW, t] - change
                    if step == 2:
                        place(flux_out.at[1, m], i, t, value)
                    else:
                        fy[i + LOW, t] = value

    def member(m, _):
        for i in range(-2, 19):
            for t in range(8):
                now = mask_of(i, t) * held(eta_in.at[m], up_eta.at[m], dn_eta.at[m], i, t)
                eta[i + LOW, t] = now
                if 0 <= i <= 15:
                    place(levels.at[m], i, t, now)
        edges(m, 0)
        flux_pass(m, 0, (-1, 17), (-2, 17))
        level_pass(m, -1, 17)
        edges(m, 1)
        flux_pass(m, 1, (0, 16), (-1, 16))
        level_pass(m, 0, 16)
        pltpu.make_async_copy(levels.at[m], level_hbm.at[m], out_sem.at[0, m]).start()
        flux_pass(m, 2, (0, 15), (0, 15))
        for side in range(2):
            pltpu.make_async_copy(
                flux_out.at[side, m], flux_hbm.at[side, m], out_sem.at[1 + side, m]
            ).start()
        edges(m, 2)
        return 0

    lax.fori_loop(0, 2, member, 0)
    for m in range(2):
        pltpu.make_async_copy(levels.at[m], level_hbm.at[m], out_sem.at[0, m]).wait()
        for side in range(2):
            pltpu.make_async_copy(
                flux_out.at[side, m], flux_hbm.at[side, m], out_sem.at[1 + side, m]
            ).wait()


def outer_steps(wet_tiles, nest_host, nest_anchor, eta, depth, halos):
    f32 = jnp.float32
    return pl.pallas_call(
        outer_kernel,
        out_shape=(
            jax.ShapeDtypeStruct((2, 1024, 128), f32),
            jax.ShapeDtypeStruct((2, 2, 1024, 128), f32),
            jax.ShapeDtypeStruct((2, 2, 8, 128), f32),
            jax.ShapeDtypeStruct((SECTIONS,), jnp.int32),
        ),
        in_specs=[hbm_spec()] * 9,
        out_specs=(hbm_spec(), hbm_spec(), vmem_spec(), smem_spec()),
        scratch_shapes=[
            VMEM((2, 1024, 128), f32),
            VMEM((1024, 128), f32),
            VMEM((2, 64, 128), f32),
            VMEM((2, 64, 128), f32),
            VMEM((64, 128), f32),
            VMEM((64, 128), f32),
            pltpu.SMEM((8, SECTIONS), jnp.int32),
            pltpu.SMEM((SECTIONS,), jnp.int32),
            pltpu.SMEM((2, SECTIONS), jnp.int32),
            VMEM((ROWS_HELD, 8, 8, 128), f32),
            VMEM((ROWS_HELD, 8, 8, 128), f32),
            VMEM((ROWS_HELD, 8, 8, 128), f32),
            VMEM((ROWS_HELD, 8, 8, 128), f32),
            VMEM((3, 8, 8, 128), f32),
            VMEM((2, 1024, 128), f32),
            VMEM((2, 2, 1024, 128), f32),
            pltpu.SMEM((SECTIONS,), jnp.int32),
            pltpu.SMEM((SECTIONS,), jnp.int32),
            pltpu.SemaphoreType.DMA((9,)),
            pltpu.SemaphoreType.DMA((3, 2)),
        ],
        compiler_params=pltpu.CompilerParams(vmem_limit_bytes=62 << 20),
        name="outer",
    )(wet_tiles.T, nest_host, nest_anchor.T, eta, depth, *halos)


def lane_ids():
    return lax.broadcasted_iota(jnp.int32, (8, 128), 1)


def sub_ids():
    return lax.broadcasted_iota(jnp.int32, (8, 128), 0)


def interleave(parts):
    lane = lane_ids()
    out = []
    for t in range(3):
        origin = (3 * lax.rem((lane - t + 128) * 43, 128) + t) // 128
        mixed = jnp.where(origin == 0, parts[0], jnp.where(origin == 1, parts[1], parts[2]))
        out.append(jnp.take_along_axis(mixed, lax.rem(3 * lane + t, 128), axis=1))
    return out


def straighten(parts):
    lane = lane_ids()
    spread_parts = []
    origins = []
    for t in range(3):
        spot = lax.rem((lane - t + 128) * 43, 128)
        spread_parts.append(jnp.take_along_axis(parts[t], spot, axis=1))
        origins.append((3 * spot + t) // 128)
    return [
        jnp.where(origins[0] == t, spread_parts[0], jnp.where(origins[1] == t, spread_parts[1], spread_parts[2]))
        for t in range(3)
    ]


def spread_edges(edge_ref, cols, rows, steps):
    lane = lane_ids()
    sub = sub_ids()

    def spread(row, index):
        wide = jnp.broadcast_to(row, (8, 128))
        return jnp.take_along_axis(wide, index, axis=1)

    for step in steps:
        for m in range(2):
            at = m * 2 + (4 if step == 2 else 0)
            level = edge_ref[at : at + 1, :]
            upright = edge_ref[at + 1 : at + 2, :]
            for q in range(8):
                cols[step, m, 0, q] = spread(upright, sub * 8 + q)
                cols[step, m, 1, q] = spread(upright, sub * 8 + q + 64)
            for side in range(2):
                for t in range(3):
                    value = spread(level, (3 * lane + t) // REFINE + 64 * side)
                    if t == 0:
                        value = jnp.where(lane == 0, cols[step, m, 0, 7 * side], value)
                    if t == 2:
                        value = jnp.where(lane == 127, cols[step, m, 1, 7 * side], value)
                    rows[step, m, side, t] = value


def force_sides(value, t, sides):
    lane = lane_ids()
    if t == 0:
        value = jnp.where(lane == 0, sides[0], value)
    if t == 2:
        value = jnp.where(lane == 127, sides[1], value)
    return value


def fix_rows(h, rows, step, m):
    sub = sub_ids()
    for t in range(3):
        h[m, 0, t] = jnp.where(sub == 0, rows[step, m, 0, t], h[m, 0, t])
        h[m, STRIP - 1, t] = jnp.where(sub == 7, rows[step, m, 1, t], h[m, STRIP - 1, t])


def load_depth(dsrc, coef, d2):
    def load(i, _):
        parts = interleave([dsrc[t, pl.ds(i, 8, stride=STRIP), :] for t in range(3)])
        for t in range(3):
            coef[i, t] = parts[t]
        d2[i] = pltpu.roll(parts[2], 1, 1)
        return 0

    lax.fori_loop(0, STRIP, load, 0, unroll=4)


def load_source(src, h, div, m):
    def load(i, _):
        parts = interleave([src[m, t, pl.ds(i, 8, stride=STRIP), :] for t in range(3)])
        for t in range(3):
            h[m, i, t] = parts[t]
            div[m, i, t] = jnp.zeros((8, 128), jnp.float32)
        return 0

    lax.fori_loop(0, STRIP, load, 0, unroll=4)


def first_substep(h, peak, cols, rows, m):
    def start(q, _):
        sides = [cols[0, m, side, q] for side in range(2)]
        for r in range(REFINE):
            for t in range(3):
                i = q * REFINE + r
                value = force_sides(h[m, i, t], t, sides)
                if t != 1:
                    h[m, i, t] = value
                peak[m, i, t] = value
        return 0

    lax.fori_loop(0, STRIP // REFINE, start, 0)
    fix_rows(h, rows, 0, m)


def advance(m, start, step, carry, h, div, peak, coef, d2, cols):
    now, above = carry
    for r in range(BATCH):
        i = start + r
        if r % REFINE == 0:
            sides = [cols[step, m, side, i // REFINE] for side in range(2)]
        following = [h[m, i + 1, t] for t in range(3)]
        d = [coef[i, t] for t in range(3)]
        beyond = [now[1], now[2], pltpu.roll(now[0], 127, 1)]
        f = [d[t] * (beyond[t] - now[t]) for t in range(3)]
        behind = [d2[i] * (now[0] - pltpu.roll(now[2], 1, 1)), f[0], f[1]]
        g = []
        for t in range(3):
            g.append(d[t] * (following[t] - now[t]))
            change = div[m, i, t] - ((f[t] - behind[t]) + (g[t] - above[t]))
            value = force_sides(now[t] - change, t, sides)
            div[m, i, t] = change
            h[m, i, t] = value
            peak[m, i, t] = jnp.maximum(peak[m, i, t], value)
        now, above = following, g
    return now, above


def substeps(m, low, high, h, div, peak, coef, d2, cols, rows):
    def substep(k, _):
        step = k // REFINE
        now = [h[m, 0, t] for t in range(3)]
        above = []
        for t in range(3):
            wrapped = pltpu.roll(now[t], 7, 0)
            h[m, STRIP, t] = wrapped
            above.append(pltpu.roll(coef[STRIP - 1, t] * (wrapped - h[m, STRIP - 1, t]), 1, 0))
        lax.fori_loop(
            0,
            STRIP // BATCH,
            lambda b, c: advance(m, b * BATCH, step, c, h, div, peak, coef, d2, cols),
            (now, above),
        )
        fix_rows(h, rows, step, m)
        return 0

    lax.fori_loop(low, high, substep, 0)


def settle_peak(peak, rows, m):
    sub = sub_ids()
    for t in range(3):
        for side, i, edge_sub in ((0, 0, 0), (1, STRIP - 1, 7)):
            top = jnp.maximum(
                jnp.maximum(rows[0, m, side, t], rows[1, m, side, t]), rows[2, m, side, t]
            )
            peak[m, i, t] = jnp.where(sub == edge_sub, top, peak[m, i, t])


def coast_kernel(
    host_ref, pick_ref, edges_ref, source_ref, depth_ref, mean_ref, var_ref,
    gathered, outgoing, incoming_first, incoming_later, own_edge,
    h, div, peak, coef, d2, cols, rows, src, dsrc,
    r1, st, r2, mv,
    load_sem, send_x, recv_x, send_z, recv_z, s1, q1, s2, q2, s3, q3, s4, q4,
):
    sec = lax.axis_index("sec")
    plane = sec // Z_CORES
    spot = lax.rem(sec, Z_CORES)
    mem = lax.axis_index("mem")
    near = mem + 1 - 2 * lax.rem(mem, 2)
    far = 3 - mem
    high = mem // 2
    gray = lax.rem(lax.rem(mem, 2) + high, 2)

    loads = []
    for t in range(3):
        part = pl.ds(128 * t, 128)
        loads.append(pltpu.make_async_copy(depth_ref.at[0, :, part], dsrc.at[t], load_sem.at[t]))
    for m in range(2):
        for t in range(3):
            part = pl.ds(128 * t, 128)
            loads.append(
                pltpu.make_async_copy(
                    source_ref.at[m, 0, :, part], src.at[m, t], load_sem.at[3 + 3 * m + t]
                )
            )
    for copy in loads:
        copy.start()

    barrier = pltpu.get_barrier_semaphore()
    for step in range(1, X_PLANES):
        peer = lax.rem(plane + step, X_PLANES) * Z_CORES + spot
        pl.semaphore_signal(barrier, inc=1, device_id={"sec": peer}, device_id_type=MESH)
    for step in range(1, Z_CORES):
        peer = plane * Z_CORES + lax.rem(spot + step, Z_CORES)
        pl.semaphore_signal(barrier, inc=1, device_id={"sec": peer}, device_id_type=MESH)
    for peer in (near, far):
        pl.semaphore_signal(barrier, inc=1, device_id={"mem": peer}, device_id_type=MESH)
    gathered[plane] = edges_ref[...]
    pl.semaphore_wait(barrier, X_PLANES + Z_CORES)

    along_x = []
    for step in range(1, X_PLANES):
        peer = lax.rem(plane + step, X_PLANES) * Z_CORES + spot
        copy = pltpu.make_async_remote_copy(
            src_ref=edges_ref,
            dst_ref=gathered.at[plane],
            send_sem=send_x.at[step - 1],
            recv_sem=recv_x.at[step - 1],
            device_id={"sec": peer},
            device_id_type=MESH,
        )
        copy.start()
        along_x.append(copy)
    for copy in loads[:3]:
        copy.wait()
    load_depth(dsrc, coef, d2)
    for copy in along_x:
        copy.wait()
    along_z = []
    incoming = (incoming_first, incoming_later)
    for part in range(2):
        for step in range(Z_CORES):
            target = lax.rem(spot + step, Z_CORES)
            choice = pick_ref[plane * Z_CORES + target]
            message = gathered[choice // 2, lax.rem(choice, 2), part]
            if step == 0:
                incoming[part][spot] = message
                continue
            outgoing[part, step] = message
            copy = pltpu.make_async_remote_copy(
                src_ref=outgoing.at[part, step],
                dst_ref=incoming[part].at[spot],
                send_sem=send_z.at[part, step - 1],
                recv_sem=recv_z.at[part, step - 1],
                device_id={"sec": plane * Z_CORES + target},
                device_id_type=MESH,
            )
            copy.start()
            along_z.append(copy)
    for copy in loads[3:]:
        copy.wait()
    for m in range(2):
        load_source(src, h, div, m)
    host_spot = lax.rem(host_ref[sec], Z_CORES)
    for copy in along_z[: Z_CORES - 1]:
        copy.wait_recv()
    own_edge[0] = incoming_first[host_spot]
    spread_edges(own_edge.at[0], cols, rows, (0,))

    def early(m, _):
        first_substep(h, peak, cols, rows, m)
        substeps(m, 1, REFINE, h, div, peak, coef, d2, cols, rows)
        return 0

    lax.fori_loop(0, 2, early, 0)
    for copy in along_z[Z_CORES - 1 :]:
        copy.wait_recv()
    own_edge[1] = incoming_later[host_spot]
    spread_edges(own_edge.at[1], cols, rows, (1, 2))

    one = (near, far)
    two = (far, near)
    keep1 = (gray, high)
    keep2 = (high, gray)
    flows = [(chunk, half) for chunk in range(3) for half in range(2)]

    def quad(chunk, half, bit1):
        return half * 24 + chunk * 8 + bit1 * 4

    def remote(src_ref, dst_ref, send, recv, peer):
        return pltpu.make_async_remote_copy(
            src_ref=src_ref, dst_ref=dst_ref, send_sem=send, recv_sem=recv,
            device_id={"mem": peer}, device_id_type=MESH,
        )

    def first(m, chunk, half):
        n = 2 * chunk + half
        away = pl.ds(quad(chunk, half, 1 - keep1[half]), 4)
        return remote(peak.at[m, away], r1.at[n, m], s1.at[n, m], q1.at[n, m], one[half])

    def late(m, _):
        substeps(m, REFINE, STEPS * REFINE, h, div, peak, coef, d2, cols, rows)
        settle_peak(peak, rows, m)
        for chunk, half in flows:
            first(m, chunk, half).start()
        return 0

    lax.fori_loop(0, 2, late, 0)

    second = {}
    for chunk, half in flows:
        n = 2 * chunk + half
        for m in range(2):
            first(m, chunk, half).wait_recv()
        kept = quad(chunk, half, keep1[half])

        def merge_pair(bit2, n=n, kept=kept):
            for r in range(2):
                local = bit2 * 2 + r
                for t in range(3):
                    a = peak[0, kept + local, t]
                    b = peak[1, kept + local, t]
                    c = r1[n, 0, local, t]
                    d = r1[n, 1, local, t]
                    total = (a + b) + (c + d)
                    middle = total * 0.25
                    a = a - middle
                    b = b - middle
                    c = c - middle
                    d = d - middle
                    st[n, 0, local, t] = total
                    st[n, 1, local, t] = (a * a + b * b) + (c * c + d * d)

        merge_pair(1 - keep2[half])
        away = pl.ds((1 - keep2[half]) * 2, 2)
        second[n] = remote(st.at[n, :, away], r2.at[n], s2.at[n], q2.at[n], two[half])
        second[n].start()
        merge_pair(keep2[half])

    def straight_rows(start, count):
        for r in range(count):
            i = start + r
            for number, target in enumerate((mean_ref, var_ref)):
                parts = straighten([mv[number, i, t] for t in range(3)])
                for t in range(3):
                    target[t, pl.ds(i, 8, stride=STRIP), :] = parts[t]

    third = {}
    for chunk, half in flows:
        n = 2 * chunk + half
        second[n].wait_recv()
        pair = quad(chunk, half, keep1[half]) + keep2[half] * 2
        for r in range(2):
            local = keep2[half] * 2 + r
            for t in range(3):
                mine = st[n, 0, local, t]
                other = r2[n, 0, r, t]
                gap = mine - other
                squares = (st[n, 1, local, t] + r2[n, 1, r, t]) + gap * gap * 0.125
                mv[0, pair + r, t] = (mine + other) * 0.125
                mv[1, pair + r, t] = squares * 0.125
        block = pl.ds(pair, 2)
        third[n] = remote(mv.at[:, block], mv.at[:, block], s3.at[n], q3.at[n], two[half])
        third[n].start()

    fourth = {}
    for chunk, half in flows:
        n = 2 * chunk + half
        third[n].wait_recv()
        kept = pl.ds(quad(chunk, half, keep1[half]), 4)
        fourth[n] = remote(mv.at[:, kept], mv.at[:, kept], s4.at[n], q4.at[n], one[half])
        fourth[n].start()

    for chunk, half in flows:
        straight_rows(quad(chunk, half, keep1[half]), 4)
    for chunk, half in flows:
        n = 2 * chunk + half
        fourth[n].wait_recv()
        straight_rows(quad(chunk, half, 1 - keep1[half]), 4)
    for copy in along_z:
        copy.wait_send()
    for chunk, half in flows:
        n = 2 * chunk + half
        for m in range(2):
            first(m, chunk, half).wait_send()
        second[n].wait_send()
        third[n].wait_send()
        fourth[n].wait_send()


def advance_coast(nest_host, pick, edges, source, depth):
    shape = jax.ShapeDtypeStruct((3, 384, 128), jnp.float32)
    dma = pltpu.SemaphoreType.DMA
    return pl.pallas_call(
        coast_kernel,
        out_shape=(shape, shape),
        in_specs=[smem_spec(), smem_spec(), vmem_spec(), hbm_spec(), hbm_spec()],
        out_specs=(vmem_spec(), vmem_spec()),
        scratch_shapes=[
            VMEM((X_PLANES, 2, 2, 8, 128), jnp.float32),
            VMEM((2, Z_CORES, 8, 128), jnp.float32),
            VMEM((Z_CORES, 8, 128), jnp.float32),
            VMEM((Z_CORES, 8, 128), jnp.float32),
            VMEM((2, 8, 128), jnp.float32),
            VMEM((2, STRIP + 1, 3, 8, 128), jnp.float32),
            VMEM((2, STRIP, 3, 8, 128), jnp.float32),
            VMEM((2, STRIP, 3, 8, 128), jnp.float32),
            VMEM((STRIP, 3, 8, 128), jnp.float32),
            VMEM((STRIP, 8, 128), jnp.float32),
            VMEM((STEPS, 2, 2, 8, 8, 128), jnp.float32),
            VMEM((STEPS, 2, 2, 3, 8, 128), jnp.float32),
            VMEM((2, 3, 384, 128), jnp.float32),
            VMEM((3, 384, 128), jnp.float32),
            VMEM((6, 2, 4, 3, 8, 128), jnp.float32),
            VMEM((6, 2, 4, 3, 8, 128), jnp.float32),
            VMEM((6, 2, 2, 3, 8, 128), jnp.float32),
            VMEM((2, STRIP, 3, 8, 128), jnp.float32),
            dma((9,)),
            dma((X_PLANES - 1,)),
            dma((X_PLANES - 1,)),
            dma((2, Z_CORES - 1)),
            dma((2, Z_CORES - 1)),
            dma((6, 2)),
            dma((6, 2)),
            *([dma((6,))] * 6),
        ],
        compiler_params=pltpu.CompilerParams(
            collective_id=1, has_side_effects=True, vmem_limit_bytes=62 << 20
        ),
        name="coast",
    )(nest_host, pick, edges, source, depth)


def emit_kernel(mean_ref, var_ref, mean_hbm, var_hbm, sem):
    copies = []
    for number, (source, target) in enumerate(((mean_ref, mean_hbm), (var_ref, var_hbm))):
        for t in range(3):
            copy = pltpu.make_async_copy(
                source.at[t], target.at[0, :, pl.ds(128 * t, 128)], sem.at[number, t]
            )
            copy.start()
            copies.append(copy)
    for copy in copies:
        copy.wait()


def emit(mean, var):
    shape = jax.ShapeDtypeStruct((1, 384, 384), jnp.float32)
    return pl.pallas_call(
        emit_kernel,
        out_shape=(shape, shape),
        in_specs=[vmem_spec()] * 2,
        out_specs=(hbm_spec(), hbm_spec()),
        scratch_shapes=[pltpu.SemaphoreType.DMA((2, 3))],
        name="emit",
    )(mean, var)


def tiled(field):
    lead = field.shape[:-2]
    n = len(lead)
    split = field.reshape(*lead, 16, 8, 8, 128)
    return jnp.swapaxes(split, n + 1, n + 2).reshape(*lead, 1024, 128)


def untiled(field):
    lead = field.shape[:-2]
    n = len(lead)
    split = field.reshape(*lead, 16, 8, 8, 128)
    return jnp.swapaxes(split, n + 1, n + 2).reshape(*lead, 128, 1024)


def body(outer_source, outer_depth, wet_tiles, nest_host, nest_anchor, nest_source, nest_depth):
    eta = tiled(outer_source)
    depth = tiled(outer_depth)
    halos = exchange_halos(eta, depth)
    level, flux, edges, pick = outer_steps(wet_tiles, nest_host, nest_anchor, eta, depth, halos)
    mean, var = advance_coast(nest_host, pick, edges, nest_source, nest_depth)
    mean, var = emit(mean, var)
    return (untiled(level), untiled(flux), mean, var)


def solution(mesh):
    return jax.shard_map(
        body,
        mesh=mesh,
        in_specs=(
            P("mem", "sec", None),
            P("sec", None),
            P(),
            P(),
            P(),
            P("mem", "sec", None, None),
            P("sec", None, None),
        ),
        out_specs=(
            P("mem", "sec", None),
            P(None, "mem", "sec", None),
            P("sec", None, None),
            P("sec", None, None),
        ),
        check_vma=False,
    )
```

```python
import jax
import jax.numpy as jnp
from jax import lax
from jax.experimental import pallas as pl
from jax.experimental.pallas import tpu as pltpu
from jax.sharding import PartitionSpec as P

MESH = pl.DeviceIdType.MESH
STEPS = 3
REFINE = 6
SECTIONS = 64
Z_CORES = 16
Z_LINE = 8
GROUP = 8
STRIP = 48
BATCH = 48
VMEM = pltpu.VMEM


def vmem_spec():
    return pl.BlockSpec(memory_space=pltpu.VMEM)


def smem_spec():
    return pl.BlockSpec(memory_space=pltpu.SMEM)


def hbm_spec():
    return pl.BlockSpec(memory_space=pltpu.HBM)


def halo_kernel(eta_ref, depth_ref, up_eta, dn_eta, up_depth, dn_depth, send_sem, recv_sem):
    me = lax.axis_index("sec")
    below = lax.rem(me + 1, SECTIONS)
    above = lax.rem(me + SECTIONS - 1, SECTIONS)
    barrier = pltpu.get_barrier_semaphore()
    for peer in (below, above):
        pl.semaphore_signal(barrier, inc=1, device_id={"sec": peer}, device_id_type=MESH)
    pl.semaphore_wait(barrier, 2)
    bottom = pl.ds(960, 64)
    top = pl.ds(0, 64)
    plan = (
        (eta_ref.at[:, bottom, :], up_eta, below),
        (eta_ref.at[:, top, :], dn_eta, above),
        (depth_ref.at[bottom, :], up_depth, below),
        (depth_ref.at[top, :], dn_depth, above),
    )
    copies = []
    for number, (source, target, peer) in enumerate(plan):
        copy = pltpu.make_async_remote_copy(
            src_ref=source,
            dst_ref=target,
            send_sem=send_sem.at[number],
            recv_sem=recv_sem.at[number],
            device_id={"sec": peer},
            device_id_type=MESH,
        )
        copy.start()
        copies.append(copy)
    for copy in copies:
        copy.wait()


def exchange_halos(eta, depth):
    rows = jax.ShapeDtypeStruct((2, 64, 128), jnp.float32)
    coef = jax.ShapeDtypeStruct((64, 128), jnp.float32)
    return pl.pallas_call(
        halo_kernel,
        out_shape=(rows, rows, coef, coef),
        in_specs=[hbm_spec()] * 2,
        out_specs=(hbm_spec(),) * 4,
        scratch_shapes=[pltpu.SemaphoreType.DMA((4,)), pltpu.SemaphoreType.DMA((4,))],
        compiler_params=pltpu.CompilerParams(collective_id=0, has_side_effects=True),
        name="halo",
    )(eta, depth)


LOW = 2
ROWS_HELD = 21


def outer_kernel(
    wet_hbm, host_hbm, anchor_hbm, eta_hbm, depth_hbm, up_eta_hbm, dn_eta_hbm, up_depth_hbm, dn_depth_hbm,
    level_hbm, flux_hbm, edges_ref, pick_ref,
    eta_in, depth_in, up_eta, dn_eta, up_depth, dn_depth, wet, host, anchor,
    eta, fx, fy, dw, masks, levels, flux_out, first, last,
    in_sem, out_sem,
):
    section = lax.axis_index("sec")
    lane = lane_ids()
    sub = sub_ids()
    loads = [
        pltpu.make_async_copy(source, target, in_sem.at[number])
        for number, (source, target) in enumerate(
            (
                (wet_hbm, wet),
                (host_hbm, host),
                (anchor_hbm, anchor),
                (depth_hbm, depth_in),
                (up_depth_hbm, up_depth),
                (dn_depth_hbm, dn_depth),
                (eta_hbm, eta_in),
                (up_eta_hbm, up_eta),
                (dn_eta_hbm, dn_eta),
            )
        )
    ]
    for copy in loads:
        copy.start()
    for copy in loads[:3]:
        copy.wait()

    first[section] = 0
    last[section] = 0

    def note(n, _):
        last[host[n]] = n
        first[host[SECTIONS - 1 - n]] = SECTIONS - 1 - n
        return 0

    lax.fori_loop(0, SECTIONS, note, 0, unroll=8)

    def choose(n, _):
        section_of = host[n]
        group = (section_of // Z_CORES) * 2 + lax.rem(section_of, 2)
        pick_ref[n] = group * 2 + jnp.where(first[section_of] == n, 0, 1)
        return 0

    lax.fori_loop(0, SECTIONS, choose, 0, unroll=8)

    def flag(row, t):
        inside = (row >= 0) & (row < SECTIONS)
        value = jnp.where(inside, wet[t, jnp.clip(row, 0, SECTIONS - 1)], 0)
        return jnp.full((8, 128), value, jnp.int32).astype(jnp.float32)

    for t in range(8):
        own = flag(section, t)
        masks[0, t] = jnp.where(sub == 0, flag(section - 1, t), own)
        masks[1, t] = own
        masks[2, t] = jnp.where(sub == 7, flag(section + 1, t), own)

    def strip(ref, i, t):
        return ref[pl.ds((i // 8) * 64 + t * 8 + i % 8, 8, stride=128), :]

    def held(ref, before, after, i, t):
        if i < 0:
            edge = before[t * 8 + 8 + i : t * 8 + 9 + i, :]
            return jnp.where(sub == 0, jnp.broadcast_to(edge, (8, 128)), pltpu.roll(strip(ref, i + 16, t), 1, 0))
        if i > 15:
            edge = after[t * 8 + i - 16 : t * 8 + i - 15, :]
            return jnp.where(sub == 7, jnp.broadcast_to(edge, (8, 128)), pltpu.roll(strip(ref, i - 16, t), 7, 0))
        return strip(ref, i, t)

    def mask_of(i, t):
        return masks[0 if i < 0 else 1 if i < 16 else 2, t]

    for copy in loads[3:6]:
        copy.wait()
    for i in range(-2, 18):
        for t in range(8):
            dw[i + LOW, t] = mask_of(i, t) * held(depth_in, up_depth, dn_depth, i, t)

    def place(ref, i, t, value):
        ref[pl.ds((i // 8) * 64 + t * 8 + i % 8, 8, stride=128), :] = value

    def edges(m, step):
        level = levels.at[m]
        for slot in range(2):
            nest = (first if slot == 0 else last)[section]
            r0 = anchor[0, nest]
            c0 = anchor[1, nest]
            shift = lax.rem(c0, 128)
            t0 = c0 // 128
            t1 = jnp.minimum(t0 + 1, 7)
            t2 = (c0 + 63) // 128

            def row_of(r, offset):
                spot = lane - offset + shift
                index = lax.rem(spot + 128, 128)
                at = (r // 8) * 64 + lax.rem(r, 8)
                here = jnp.broadcast_to(level[pl.ds(at + t0 * 8, 1), :], (8, 128))
                there = jnp.broadcast_to(level[pl.ds(at + t1 * 8, 1), :], (8, 128))
                return jnp.where(
                    spot < 128,
                    jnp.take_along_axis(here, index, axis=1),
                    jnp.take_along_axis(there, index, axis=1),
                )

            pair = jnp.where(lane < 64, row_of(r0, 0), row_of(r0 + 63, 64))
            part = 0 if step == 0 else 1
            at = 2 * m + (4 if step == 2 else 0)
            edges_ref[slot, part, pl.ds(at, 1), :] = pair[0:1]
            total = jnp.zeros((8, 128), jnp.float32)
            for tile in range(16):
                west_block = level[pl.ds(pl.multiple_of(tile * 64 + t0 * 8, 8), 8), :]
                east_block = level[pl.ds(pl.multiple_of(tile * 64 + t2 * 8, 8), 8), :]
                west_col = jnp.take_along_axis(west_block, jnp.full((8, 128), shift, jnp.int32), axis=1)
                east_col = jnp.take_along_axis(
                    east_block, jnp.full((8, 128), lax.rem(c0 + 63, 128), jnp.int32), axis=1
                )
                column = jnp.where(lane < 64, west_col, east_col)
                row = tile * 8 + sub - r0
                wanted = (row >= 0) & (row < 64) & (lax.rem(lane, 64) == row)
                total = total + jnp.where(wanted, column, 0.0)
            edges_ref[slot, part, pl.ds(at + 1, 1), :] = jnp.sum(total, axis=0, keepdims=True)

    for slot in range(2):
        edges_ref[slot, 0, 4:8, :] = jnp.zeros((4, 128), jnp.float32)
    for copy in loads[6:]:
        copy.wait()

    def level_pass(m, low, high):
        for i in range(low, high + 1):
            carried = 0.0
            for t in range(8):
                flow = fx[i + LOW, t]
                rolled = pltpu.roll(flow, 1, 1)
                behind = jnp.where(lane == 0, carried, rolled)
                carried = rolled
                down = fy[i + LOW, t] - fy[i - 1 + LOW, t]
                now = mask_of(i, t) * (eta[i + LOW, t] - (flow - behind) - down)
                eta[i + LOW, t] = now
                if 0 <= i <= 15:
                    place(levels.at[m], i, t, now)

    def flux_pass(m, step, x_range, y_range):
        for i in range(min(x_range[0], y_range[0]), max(x_range[1], y_range[1]) + 1):
            carried = 0.0
            for t in reversed(range(8)):
                now = eta[i + LOW, t]
                coef = dw[i + LOW, t]
                if x_range[0] <= i <= x_range[1]:
                    rolled = pltpu.roll(now, 127, 1)
                    change = coef * (jnp.where(lane == 127, carried, rolled) - now)
                    carried = rolled
                    value = -change if step == 0 else fx[i + LOW, t] - change
                    if step == 2:
                        place(flux_out.at[0, m], i, t, value)
                    else:
                        fx[i + LOW, t] = value
                if y_range[0] <= i <= y_range[1]:
                    change = coef * (eta[i + 1 + LOW, t] - now)
                    value = -change if step == 0 else fy[i + LOW, t] - change
                    if step == 2:
                        place(flux_out.at[1, m], i, t, value)
                    else:
                        fy[i + LOW, t] = value

    def member(m, _):
        for i in range(-2, 19):
            for t in range(8):
                now = mask_of(i, t) * held(eta_in.at[m], up_eta.at[m], dn_eta.at[m], i, t)
                eta[i + LOW, t] = now
                if 0 <= i <= 15:
                    place(levels.at[m], i, t, now)
        edges(m, 0)
        flux_pass(m, 0, (-1, 17), (-2, 17))
        level_pass(m, -1, 17)
        edges(m, 1)
        flux_pass(m, 1, (0, 16), (-1, 16))
        level_pass(m, 0, 16)
        pltpu.make_async_copy(levels.at[m], level_hbm.at[m], out_sem.at[0, m]).start()
        flux_pass(m, 2, (0, 15), (0, 15))
        for side in range(2):
            pltpu.make_async_copy(
                flux_out.at[side, m], flux_hbm.at[side, m], out_sem.at[1 + side, m]
            ).start()
        edges(m, 2)
        return 0

    lax.fori_loop(0, 2, member, 0)
    for m in range(2):
        pltpu.make_async_copy(levels.at[m], level_hbm.at[m], out_sem.at[0, m]).wait()
        for side in range(2):
            pltpu.make_async_copy(
                flux_out.at[side, m], flux_hbm.at[side, m], out_sem.at[1 + side, m]
            ).wait()


def outer_steps(wet_tiles, nest_host, nest_anchor, eta, depth, halos):
    f32 = jnp.float32
    return pl.pallas_call(
        outer_kernel,
        out_shape=(
            jax.ShapeDtypeStruct((2, 1024, 128), f32),
            jax.ShapeDtypeStruct((2, 2, 1024, 128), f32),
            jax.ShapeDtypeStruct((2, 2, 8, 128), f32),
            jax.ShapeDtypeStruct((SECTIONS,), jnp.int32),
        ),
        in_specs=[hbm_spec()] * 9,
        out_specs=(hbm_spec(), hbm_spec(), vmem_spec(), smem_spec()),
        scratch_shapes=[
            VMEM((2, 1024, 128), f32),
            VMEM((1024, 128), f32),
            VMEM((2, 64, 128), f32),
            VMEM((2, 64, 128), f32),
            VMEM((64, 128), f32),
            VMEM((64, 128), f32),
            pltpu.SMEM((8, SECTIONS), jnp.int32),
            pltpu.SMEM((SECTIONS,), jnp.int32),
            pltpu.SMEM((2, SECTIONS), jnp.int32),
            VMEM((ROWS_HELD, 8, 8, 128), f32),
            VMEM((ROWS_HELD, 8, 8, 128), f32),
            VMEM((ROWS_HELD, 8, 8, 128), f32),
            VMEM((ROWS_HELD, 8, 8, 128), f32),
            VMEM((3, 8, 8, 128), f32),
            VMEM((2, 1024, 128), f32),
            VMEM((2, 2, 1024, 128), f32),
            pltpu.SMEM((SECTIONS,), jnp.int32),
            pltpu.SMEM((SECTIONS,), jnp.int32),
            pltpu.SemaphoreType.DMA((9,)),
            pltpu.SemaphoreType.DMA((3, 2)),
        ],
        compiler_params=pltpu.CompilerParams(vmem_limit_bytes=62 << 20),
        name="outer",
    )(wet_tiles.T, nest_host, nest_anchor.T, eta, depth, *halos)


def lane_ids():
    return lax.broadcasted_iota(jnp.int32, (8, 128), 1)


def sub_ids():
    return lax.broadcasted_iota(jnp.int32, (8, 128), 0)


def interleave(parts):
    lane = lane_ids()
    out = []
    for t in range(3):
        origin = (3 * lax.rem((lane - t + 128) * 43, 128) + t) // 128
        mixed = jnp.where(origin == 0, parts[0], jnp.where(origin == 1, parts[1], parts[2]))
        out.append(jnp.take_along_axis(mixed, lax.rem(3 * lane + t, 128), axis=1))
    return out


def straighten(parts):
    lane = lane_ids()
    spread_parts = []
    origins = []
    for t in range(3):
        spot = lax.rem((lane - t + 128) * 43, 128)
        spread_parts.append(jnp.take_along_axis(parts[t], spot, axis=1))
        origins.append((3 * spot + t) // 128)
    return [
        jnp.where(origins[0] == t, spread_parts[0], jnp.where(origins[1] == t, spread_parts[1], spread_parts[2]))
        for t in range(3)
    ]


def spread_edges(edge_ref, cols, rows, steps):
    lane = lane_ids()
    sub = sub_ids()

    def spread(row, index):
        wide = jnp.broadcast_to(row, (8, 128))
        return jnp.take_along_axis(wide, index, axis=1)

    for step in steps:
        for m in range(2):
            at = m * 2 + (4 if step == 2 else 0)
            level = edge_ref[at : at + 1, :]
            upright = edge_ref[at + 1 : at + 2, :]
            for q in range(8):
                cols[step, m, 0, q] = spread(upright, sub * 8 + q)
                cols[step, m, 1, q] = spread(upright, sub * 8 + q + 64)
            for side in range(2):
                for t in range(3):
                    value = spread(level, (3 * lane + t) // REFINE + 64 * side)
                    if t == 0:
                        value = jnp.where(lane == 0, cols[step, m, 0, 7 * side], value)
                    if t == 2:
                        value = jnp.where(lane == 127, cols[step, m, 1, 7 * side], value)
                    rows[step, m, side, t] = value


def force_sides(value, t, sides):
    lane = lane_ids()
    if t == 0:
        value = jnp.where(lane == 0, sides[0], value)
    if t == 2:
        value = jnp.where(lane == 127, sides[1], value)
    return value


def fix_rows(h, rows, step, m):
    sub = sub_ids()
    for t in range(3):
        h[m, 0, t] = jnp.where(sub == 0, rows[step, m, 0, t], h[m, 0, t])
        h[m, STRIP - 1, t] = jnp.where(sub == 7, rows[step, m, 1, t], h[m, STRIP - 1, t])


def load_depth(dsrc, coef, d2):
    def load(i, _):
        parts = interleave([dsrc[t, pl.ds(i, 8, stride=STRIP), :] for t in range(3)])
        for t in range(3):
            coef[i, t] = parts[t]
        d2[i] = pltpu.roll(parts[2], 1, 1)
        return 0

    lax.fori_loop(0, STRIP, load, 0, unroll=4)


def load_source(src, h, div, m):
    def load(i, _):
        parts = interleave([src[m, t, pl.ds(i, 8, stride=STRIP), :] for t in range(3)])
        for t in range(3):
            h[m, i, t] = parts[t]
            div[m, i, t] = jnp.zeros((8, 128), jnp.float32)
        return 0

    lax.fori_loop(0, STRIP, load, 0, unroll=4)


def first_substep(h, peak, cols, rows, m):
    def start(q, _):
        sides = [cols[0, m, side, q] for side in range(2)]
        for r in range(REFINE):
            for t in range(3):
                i = q * REFINE + r
                value = force_sides(h[m, i, t], t, sides)
                if t != 1:
                    h[m, i, t] = value
                peak[m, i, t] = value
        return 0

    lax.fori_loop(0, STRIP // REFINE, start, 0)
    fix_rows(h, rows, 0, m)


def advance(m, start, step, carry, h, div, peak, coef, d2, cols):
    now, above = carry
    for r in range(BATCH):
        i = start + r
        if r % REFINE == 0:
            sides = [cols[step, m, side, i // REFINE] for side in range(2)]
        following = [h[m, i + 1, t] for t in range(3)]
        d = [coef[i, t] for t in range(3)]
        beyond = [now[1], now[2], pltpu.roll(now[0], 127, 1)]
        f = [d[t] * (beyond[t] - now[t]) for t in range(3)]
        behind = [d2[i] * (now[0] - pltpu.roll(now[2], 1, 1)), f[0], f[1]]
        g = []
        for t in range(3):
            g.append(d[t] * (following[t] - now[t]))
            change = div[m, i, t] - ((f[t] - behind[t]) + (g[t] - above[t]))
            value = force_sides(now[t] - change, t, sides)
            div[m, i, t] = change
            h[m, i, t] = value
            peak[m, i, t] = jnp.maximum(peak[m, i, t], value)
        now, above = following, g
    return now, above


def substeps(m, low, high, h, div, peak, coef, d2, cols, rows):
    def substep(k, _):
        step = k // REFINE
        now = [h[m, 0, t] for t in range(3)]
        above = []
        for t in range(3):
            wrapped = pltpu.roll(now[t], 7, 0)
            h[m, STRIP, t] = wrapped
            above.append(pltpu.roll(coef[STRIP - 1, t] * (wrapped - h[m, STRIP - 1, t]), 1, 0))
        lax.fori_loop(
            0,
            STRIP // BATCH,
            lambda b, c: advance(m, b * BATCH, step, c, h, div, peak, coef, d2, cols),
            (now, above),
        )
        fix_rows(h, rows, step, m)
        return 0

    lax.fori_loop(low, high, substep, 0)


def settle_peak(peak, rows, m):
    sub = sub_ids()
    for t in range(3):
        for side, i, edge_sub in ((0, 0, 0), (1, STRIP - 1, 7)):
            top = jnp.maximum(
                jnp.maximum(rows[0, m, side, t], rows[1, m, side, t]), rows[2, m, side, t]
            )
            peak[m, i, t] = jnp.where(sub == edge_sub, top, peak[m, i, t])


def coast_kernel(
    host_ref, pick_ref, edges_ref, source_ref, depth_ref, mean_ref, var_ref,
    gathered, outgoing, incoming_first, incoming_later, own_edge,
    h, div, peak, coef, d2, cols, rows, src, dsrc,
    r1, st, r2, mv,
    load_sem, send_x, recv_x, send_z, recv_z, s1, q1, s2, q2, s3, q3, s4, q4,
):
    sec = lax.axis_index("sec")
    plane = sec // Z_CORES
    core = lax.rem(sec, 2)
    spot = lax.rem(sec, Z_CORES) // 2
    group = plane * 2 + core
    mem = lax.axis_index("mem")
    near = mem + 1 - 2 * lax.rem(mem, 2)
    far = 3 - mem
    high = mem // 2
    gray = lax.rem(lax.rem(mem, 2) + high, 2)

    loads = []
    for t in range(3):
        part = pl.ds(128 * t, 128)
        loads.append(pltpu.make_async_copy(depth_ref.at[0, :, part], dsrc.at[t], load_sem.at[t]))
    for m in range(2):
        for t in range(3):
            part = pl.ds(128 * t, 128)
            loads.append(
                pltpu.make_async_copy(
                    source_ref.at[m, 0, :, part], src.at[m, t], load_sem.at[3 + 3 * m + t]
                )
            )
    for copy in loads:
        copy.start()

    def in_group(step):
        other = lax.rem(group + step, GROUP)
        return (other // 2) * Z_CORES + spot * 2 + lax.rem(other, 2)

    def in_line(step):
        return plane * Z_CORES + lax.rem(spot + step, Z_LINE) * 2 + core

    barrier = pltpu.get_barrier_semaphore()
    for step in range(1, GROUP):
        pl.semaphore_signal(barrier, inc=1, device_id={"sec": in_group(step)}, device_id_type=MESH)
    for step in range(1, Z_LINE):
        pl.semaphore_signal(barrier, inc=1, device_id={"sec": in_line(step)}, device_id_type=MESH)
    for peer in (near, far):
        pl.semaphore_signal(barrier, inc=1, device_id={"mem": peer}, device_id_type=MESH)
    for copy in loads[:3]:
        copy.wait()
    load_depth(dsrc, coef, d2)
    gathered[group] = edges_ref[...]
    pl.semaphore_wait(barrier, GROUP + Z_LINE)

    along_x = []
    for step in range(1, GROUP):
        copy = pltpu.make_async_remote_copy(
            src_ref=edges_ref,
            dst_ref=gathered.at[group],
            send_sem=send_x.at[step - 1],
            recv_sem=recv_x.at[step - 1],
            device_id={"sec": in_group(step)},
            device_id_type=MESH,
        )
        copy.start()
        along_x.append(copy)
    for copy in loads[3:]:
        copy.wait()
    load_source(src, h, div, 0)
    for copy in along_x:
        copy.wait()
    along_z = []
    incoming = (incoming_first, incoming_later)
    for part in range(2):
        for step in range(Z_LINE):
            choice = pick_ref[in_line(step)]
            message = gathered[choice // 2, lax.rem(choice, 2), part]
            if step == 0:
                incoming[part][spot] = message
                continue
            outgoing[part, step] = message
            copy = pltpu.make_async_remote_copy(
                src_ref=outgoing.at[part, step],
                dst_ref=incoming[part].at[spot],
                send_sem=send_z.at[part, step - 1],
                recv_sem=recv_z.at[part, step - 1],
                device_id={"sec": in_line(step)},
                device_id_type=MESH,
            )
            copy.start()
            along_z.append(copy)
    load_source(src, h, div, 1)
    host_spot = lax.rem(host_ref[sec], Z_CORES) // 2
    for copy in along_z[: Z_LINE - 1]:
        copy.wait_recv()
    own_edge[0] = incoming_first[host_spot]
    spread_edges(own_edge.at[0], cols, rows, (0,))

    def early(m, _):
        first_substep(h, peak, cols, rows, m)
        substeps(m, 1, REFINE, h, div, peak, coef, d2, cols, rows)
        return 0

    lax.fori_loop(0, 2, early, 0)
    for copy in along_z[Z_LINE - 1 :]:
        copy.wait_recv()
    own_edge[1] = incoming_later[host_spot]
    spread_edges(own_edge.at[1], cols, rows, (1, 2))

    one = (near, far)
    two = (far, near)
    keep1 = (gray, high)
    keep2 = (high, gray)
    flows = [(chunk, half) for chunk in range(3) for half in range(2)]

    def quad(chunk, half, bit1):
        return half * 24 + chunk * 8 + bit1 * 4

    def remote(src_ref, dst_ref, send, recv, peer):
        return pltpu.make_async_remote_copy(
            src_ref=src_ref, dst_ref=dst_ref, send_sem=send, recv_sem=recv,
            device_id={"mem": peer}, device_id_type=MESH,
        )

    def first(m, chunk, half):
        n = 2 * chunk + half
        away = pl.ds(quad(chunk, half, 1 - keep1[half]), 4)
        return remote(peak.at[m, away], r1.at[n, m], s1.at[n, m], q1.at[n, m], one[half])

    def late(m, _):
        substeps(m, REFINE, STEPS * REFINE, h, div, peak, coef, d2, cols, rows)
        settle_peak(peak, rows, m)
        for chunk, half in flows:
            first(m, chunk, half).start()
        return 0

    lax.fori_loop(0, 2, late, 0)

    second = {}
    for chunk, half in flows:
        n = 2 * chunk + half
        for m in range(2):
            first(m, chunk, half).wait_recv()
        kept = quad(chunk, half, keep1[half])

        def merge_pair(bit2, n=n, kept=kept):
            for r in range(2):
                local = bit2 * 2 + r
                for t in range(3):
                    a = peak[0, kept + local, t]
                    b = peak[1, kept + local, t]
                    c = r1[n, 0, local, t]
                    d = r1[n, 1, local, t]
                    total = (a + b) + (c + d)
                    middle = total * 0.25
                    a = a - middle
                    b = b - middle
                    c = c - middle
                    d = d - middle
                    st[n, 0, local, t] = total
                    st[n, 1, local, t] = (a * a + b * b) + (c * c + d * d)

        merge_pair(1 - keep2[half])
        away = pl.ds((1 - keep2[half]) * 2, 2)
        second[n] = remote(st.at[n, :, away], r2.at[n], s2.at[n], q2.at[n], two[half])
        second[n].start()
        merge_pair(keep2[half])

    def straight_rows(start, count):
        for r in range(count):
            i = start + r
            for number, target in enumerate((mean_ref, var_ref)):
                parts = straighten([mv[number, i, t] for t in range(3)])
                for t in range(3):
                    target[t, pl.ds(i, 8, stride=STRIP), :] = parts[t]

    third = {}
    for chunk, half in flows:
        n = 2 * chunk + half
        second[n].wait_recv()
        pair = quad(chunk, half, keep1[half]) + keep2[half] * 2
        for r in range(2):
            local = keep2[half] * 2 + r
            for t in range(3):
                mine = st[n, 0, local, t]
                other = r2[n, 0, r, t]
                gap = mine - other
                squares = (st[n, 1, local, t] + r2[n, 1, r, t]) + gap * gap * 0.125
                mv[0, pair + r, t] = (mine + other) * 0.125
                mv[1, pair + r, t] = squares * 0.125
        block = pl.ds(pair, 2)
        third[n] = remote(mv.at[:, block], mv.at[:, block], s3.at[n], q3.at[n], two[half])
        third[n].start()

    fourth = {}
    for chunk, half in flows:
        n = 2 * chunk + half
        third[n].wait_recv()
        kept = pl.ds(quad(chunk, half, keep1[half]), 4)
        fourth[n] = remote(mv.at[:, kept], mv.at[:, kept], s4.at[n], q4.at[n], one[half])
        fourth[n].start()

    for chunk, half in flows:
        straight_rows(quad(chunk, half, keep1[half]), 4)
    for chunk, half in flows:
        n = 2 * chunk + half
        fourth[n].wait_recv()
        straight_rows(quad(chunk, half, 1 - keep1[half]), 4)
    for copy in along_z:
        copy.wait_send()
    for chunk, half in flows:
        n = 2 * chunk + half
        for m in range(2):
            first(m, chunk, half).wait_send()
        second[n].wait_send()
        third[n].wait_send()
        fourth[n].wait_send()


def advance_coast(nest_host, pick, edges, source, depth):
    shape = jax.ShapeDtypeStruct((3, 384, 128), jnp.float32)
    dma = pltpu.SemaphoreType.DMA
    return pl.pallas_call(
        coast_kernel,
        out_shape=(shape, shape),
        in_specs=[smem_spec(), smem_spec(), vmem_spec(), hbm_spec(), hbm_spec()],
        out_specs=(vmem_spec(), vmem_spec()),
        scratch_shapes=[
            VMEM((GROUP, 2, 2, 8, 128), jnp.float32),
            VMEM((2, Z_LINE, 8, 128), jnp.float32),
            VMEM((Z_LINE, 8, 128), jnp.float32),
            VMEM((Z_LINE, 8, 128), jnp.float32),
            VMEM((2, 8, 128), jnp.float32),
            VMEM((2, STRIP + 1, 3, 8, 128), jnp.float32),
            VMEM((2, STRIP, 3, 8, 128), jnp.float32),
            VMEM((2, STRIP, 3, 8, 128), jnp.float32),
            VMEM((STRIP, 3, 8, 128), jnp.float32),
            VMEM((STRIP, 8, 128), jnp.float32),
            VMEM((STEPS, 2, 2, 8, 8, 128), jnp.float32),
            VMEM((STEPS, 2, 2, 3, 8, 128), jnp.float32),
            VMEM((2, 3, 384, 128), jnp.float32),
            VMEM((3, 384, 128), jnp.float32),
            VMEM((6, 2, 4, 3, 8, 128), jnp.float32),
            VMEM((6, 2, 4, 3, 8, 128), jnp.float32),
            VMEM((6, 2, 2, 3, 8, 128), jnp.float32),
            VMEM((2, STRIP, 3, 8, 128), jnp.float32),
            dma((9,)),
            dma((GROUP - 1,)),
            dma((GROUP - 1,)),
            dma((2, Z_LINE - 1)),
            dma((2, Z_LINE - 1)),
            dma((6, 2)),
            dma((6, 2)),
            *([dma((6,))] * 6),
        ],
        compiler_params=pltpu.CompilerParams(
            collective_id=1, has_side_effects=True, vmem_limit_bytes=62 << 20
        ),
        name="coast",
    )(nest_host, pick, edges, source, depth)


def emit_kernel(mean_ref, var_ref, mean_hbm, var_hbm, sem):
    copies = []
    for number, (source, target) in enumerate(((mean_ref, mean_hbm), (var_ref, var_hbm))):
        for t in range(3):
            copy = pltpu.make_async_copy(
                source.at[t], target.at[0, :, pl.ds(128 * t, 128)], sem.at[number, t]
            )
            copy.start()
            copies.append(copy)
    for copy in copies:
        copy.wait()


def emit(mean, var):
    shape = jax.ShapeDtypeStruct((1, 384, 384), jnp.float32)
    return pl.pallas_call(
        emit_kernel,
        out_shape=(shape, shape),
        in_specs=[vmem_spec()] * 2,
        out_specs=(hbm_spec(), hbm_spec()),
        scratch_shapes=[pltpu.SemaphoreType.DMA((2, 3))],
        name="emit",
    )(mean, var)


def tiled(field):
    lead = field.shape[:-2]
    n = len(lead)
    split = field.reshape(*lead, 16, 8, 8, 128)
    return jnp.swapaxes(split, n + 1, n + 2).reshape(*lead, 1024, 128)


def untiled(field):
    lead = field.shape[:-2]
    n = len(lead)
    split = field.reshape(*lead, 16, 8, 8, 128)
    return jnp.swapaxes(split, n + 1, n + 2).reshape(*lead, 128, 1024)


def body(outer_source, outer_depth, wet_tiles, nest_host, nest_anchor, nest_source, nest_depth):
    eta = tiled(outer_source)
    depth = tiled(outer_depth)
    halos = exchange_halos(eta, depth)
    level, flux, edges, pick = outer_steps(wet_tiles, nest_host, nest_anchor, eta, depth, halos)
    mean, var = advance_coast(nest_host, pick, edges, nest_source, nest_depth)
    mean, var = emit(mean, var)
    return (untiled(level), untiled(flux), mean, var)


def solution(mesh):
    return jax.shard_map(
        body,
        mesh=mesh,
        in_specs=(
            P("mem", "sec", None),
            P("sec", None),
            P(),
            P(),
            P(),
            P("mem", "sec", None, None),
            P("sec", None, None),
        ),
        out_specs=(
            P("mem", "sec", None),
            P(None, "mem", "sec", None),
            P("sec", None, None),
            P("sec", None, None),
        ),
        check_vma=False,
    )
```

```python
import jax
import jax.numpy as jnp
from jax import lax
from jax.experimental import pallas as pl
from jax.experimental.pallas import tpu as pltpu
from jax.sharding import PartitionSpec as P

MESH = pl.DeviceIdType.MESH
STEPS = 3
REFINE = 6
SECTIONS = 64
Z_CORES = 16
Z_LINE = 8
GROUP = 8
STRIP = 48
BATCH = 48
VMEM = pltpu.VMEM


def vmem_spec():
    return pl.BlockSpec(memory_space=pltpu.VMEM)


def smem_spec():
    return pl.BlockSpec(memory_space=pltpu.SMEM)


def hbm_spec():
    return pl.BlockSpec(memory_space=pltpu.HBM)


def halo_kernel(eta_ref, depth_ref, up_eta, dn_eta, up_depth, dn_depth, send_sem, recv_sem):
    me = lax.axis_index("sec")
    below = lax.rem(me + 1, SECTIONS)
    above = lax.rem(me + SECTIONS - 1, SECTIONS)
    barrier = pltpu.get_barrier_semaphore()
    for peer in (below, above):
        pl.semaphore_signal(barrier, inc=1, device_id={"sec": peer}, device_id_type=MESH)
    pl.semaphore_wait(barrier, 2)
    bottom = pl.ds(960, 64)
    top = pl.ds(0, 64)
    plan = (
        (eta_ref.at[:, bottom, :], up_eta, below),
        (eta_ref.at[:, top, :], dn_eta, above),
        (depth_ref.at[bottom, :], up_depth, below),
        (depth_ref.at[top, :], dn_depth, above),
    )
    copies = []
    for number, (source, target, peer) in enumerate(plan):
        copy = pltpu.make_async_remote_copy(
            src_ref=source,
            dst_ref=target,
            send_sem=send_sem.at[number],
            recv_sem=recv_sem.at[number],
            device_id={"sec": peer},
            device_id_type=MESH,
        )
        copy.start()
        copies.append(copy)
    for copy in copies:
        copy.wait()


def exchange_halos(eta, depth):
    rows = jax.ShapeDtypeStruct((2, 64, 128), jnp.float32)
    coef = jax.ShapeDtypeStruct((64, 128), jnp.float32)
    return pl.pallas_call(
        halo_kernel,
        out_shape=(rows, rows, coef, coef),
        in_specs=[hbm_spec()] * 2,
        out_specs=(hbm_spec(),) * 4,
        scratch_shapes=[pltpu.SemaphoreType.DMA((4,)), pltpu.SemaphoreType.DMA((4,))],
        compiler_params=pltpu.CompilerParams(collective_id=0, has_side_effects=True),
        name="halo",
    )(eta, depth)


LOW = 2
ROWS_HELD = 21


def outer_kernel(
    wet_hbm, host_hbm, anchor_hbm, eta_hbm, depth_hbm, up_eta_hbm, dn_eta_hbm, up_depth_hbm, dn_depth_hbm,
    level_hbm, flux_hbm, edges_ref, pick_ref,
    eta_in, depth_in, up_eta, dn_eta, up_depth, dn_depth, wet, host, anchor,
    eta, fx, fy, dw, masks, levels, flux_out, first, last,
    in_sem, out_sem,
):
    section = lax.axis_index("sec")
    lane = lane_ids()
    sub = sub_ids()
    loads = [
        pltpu.make_async_copy(source, target, in_sem.at[number])
        for number, (source, target) in enumerate(
            (
                (wet_hbm, wet),
                (host_hbm, host),
                (anchor_hbm, anchor),
                (depth_hbm, depth_in),
                (up_depth_hbm, up_depth),
                (dn_depth_hbm, dn_depth),
                (eta_hbm, eta_in),
                (up_eta_hbm, up_eta),
                (dn_eta_hbm, dn_eta),
            )
        )
    ]
    for copy in loads:
        copy.start()
    for copy in loads[:3]:
        copy.wait()

    first[section] = 0
    last[section] = 0

    def note(n, _):
        last[host[n]] = n
        first[host[SECTIONS - 1 - n]] = SECTIONS - 1 - n
        return 0

    lax.fori_loop(0, SECTIONS, note, 0, unroll=8)

    def choose(n, _):
        section_of = host[n]
        group = (section_of // Z_CORES) * 2 + lax.rem(section_of, 2)
        pick_ref[n] = group * 2 + jnp.where(first[section_of] == n, 0, 1)
        return 0

    lax.fori_loop(0, SECTIONS, choose, 0, unroll=8)

    def flag(row, t):
        inside = (row >= 0) & (row < SECTIONS)
        value = jnp.where(inside, wet[t, jnp.clip(row, 0, SECTIONS - 1)], 0)
        return jnp.full((8, 128), value, jnp.int32).astype(jnp.float32)

    for t in range(8):
        own = flag(section, t)
        masks[0, t] = jnp.where(sub == 0, flag(section - 1, t), own)
        masks[1, t] = own
        masks[2, t] = jnp.where(sub == 7, flag(section + 1, t), own)

    def strip(ref, i, t):
        return ref[pl.ds((i // 8) * 64 + t * 8 + i % 8, 8, stride=128), :]

    def held(ref, before, after, i, t):
        if i < 0:
            edge = before[t * 8 + 8 + i : t * 8 + 9 + i, :]
            return jnp.where(sub == 0, jnp.broadcast_to(edge, (8, 128)), pltpu.roll(strip(ref, i + 16, t), 1, 0))
        if i > 15:
            edge = after[t * 8 + i - 16 : t * 8 + i - 15, :]
            return jnp.where(sub == 7, jnp.broadcast_to(edge, (8, 128)), pltpu.roll(strip(ref, i - 16, t), 7, 0))
        return strip(ref, i, t)

    def mask_of(i, t):
        return masks[0 if i < 0 else 1 if i < 16 else 2, t]

    for copy in loads[3:6]:
        copy.wait()
    for i in range(-2, 18):
        for t in range(8):
            dw[i + LOW, t] = mask_of(i, t) * held(depth_in, up_depth, dn_depth, i, t)

    def place(ref, i, t, value):
        ref[pl.ds((i // 8) * 64 + t * 8 + i % 8, 8, stride=128), :] = value

    def edges(m, step):
        level = levels.at[m]
        for slot in range(2):
            nest = (first if slot == 0 else last)[section]
            r0 = anchor[0, nest]
            c0 = anchor[1, nest]
            shift = lax.rem(c0, 128)
            t0 = c0 // 128
            t1 = jnp.minimum(t0 + 1, 7)
            t2 = (c0 + 63) // 128

            def row_of(r, offset):
                spot = lane - offset + shift
                index = lax.rem(spot + 128, 128)
                at = (r // 8) * 64 + lax.rem(r, 8)
                here = jnp.broadcast_to(level[pl.ds(at + t0 * 8, 1), :], (8, 128))
                there = jnp.broadcast_to(level[pl.ds(at + t1 * 8, 1), :], (8, 128))
                return jnp.where(
                    spot < 128,
                    jnp.take_along_axis(here, index, axis=1),
                    jnp.take_along_axis(there, index, axis=1),
                )

            pair = jnp.where(lane < 64, row_of(r0, 0), row_of(r0 + 63, 64))
            part = 0 if step == 0 else 1
            at = 2 * m + (4 if step == 2 else 0)
            edges_ref[slot, part, pl.ds(at, 1), :] = pair[0:1]
            total = jnp.zeros((8, 128), jnp.float32)
            for tile in range(16):
                west_block = level[pl.ds(pl.multiple_of(tile * 64 + t0 * 8, 8), 8), :]
                east_block = level[pl.ds(pl.multiple_of(tile * 64 + t2 * 8, 8), 8), :]
                west_col = jnp.take_along_axis(west_block, jnp.full((8, 128), shift, jnp.int32), axis=1)
                east_col = jnp.take_along_axis(
                    east_block, jnp.full((8, 128), lax.rem(c0 + 63, 128), jnp.int32), axis=1
                )
                column = jnp.where(lane < 64, west_col, east_col)
                row = tile * 8 + sub - r0
                wanted = (row >= 0) & (row < 64) & (lax.rem(lane, 64) == row)
                total = total + jnp.where(wanted, column, 0.0)
            edges_ref[slot, part, pl.ds(at + 1, 1), :] = jnp.sum(total, axis=0, keepdims=True)

    for slot in range(2):
        edges_ref[slot, 0, 4:8, :] = jnp.zeros((4, 128), jnp.float32)
    for copy in loads[6:]:
        copy.wait()

    def level_pass(m, low, high):
        for i in range(low, high + 1):
            carried = 0.0
            for t in range(8):
                flow = fx[i + LOW, t]
                rolled = pltpu.roll(flow, 1, 1)
                behind = jnp.where(lane == 0, carried, rolled)
                carried = rolled
                down = fy[i + LOW, t] - fy[i - 1 + LOW, t]
                now = mask_of(i, t) * (eta[i + LOW, t] - (flow - behind) - down)
                eta[i + LOW, t] = now
                if 0 <= i <= 15:
                    place(levels.at[m], i, t, now)

    def flux_pass(m, step, x_range, y_range):
        for i in range(min(x_range[0], y_range[0]), max(x_range[1], y_range[1]) + 1):
            carried = 0.0
            for t in reversed(range(8)):
                now = eta[i + LOW, t]
                coef = dw[i + LOW, t]
                if x_range[0] <= i <= x_range[1]:
                    rolled = pltpu.roll(now, 127, 1)
                    change = coef * (jnp.where(lane == 127, carried, rolled) - now)
                    carried = rolled
                    value = -change if step == 0 else fx[i + LOW, t] - change
                    if step == 2:
                        place(flux_out.at[0, m], i, t, value)
                    else:
                        fx[i + LOW, t] = value
                if y_range[0] <= i <= y_range[1]:
                    change = coef * (eta[i + 1 + LOW, t] - now)
                    value = -change if step == 0 else fy[i + LOW, t] - change
                    if step == 2:
                        place(flux_out.at[1, m], i, t, value)
                    else:
                        fy[i + LOW, t] = value

    def member(m, _):
        for i in range(-2, 19):
            for t in range(8):
                now = mask_of(i, t) * held(eta_in.at[m], up_eta.at[m], dn_eta.at[m], i, t)
                eta[i + LOW, t] = now
                if 0 <= i <= 15:
                    place(levels.at[m], i, t, now)
        edges(m, 0)
        flux_pass(m, 0, (-1, 17), (-2, 17))
        level_pass(m, -1, 17)
        edges(m, 1)
        flux_pass(m, 1, (0, 16), (-1, 16))
        level_pass(m, 0, 16)
        pltpu.make_async_copy(levels.at[m], level_hbm.at[m], out_sem.at[0, m]).start()
        flux_pass(m, 2, (0, 15), (0, 15))
        for side in range(2):
            pltpu.make_async_copy(
                flux_out.at[side, m], flux_hbm.at[side, m], out_sem.at[1 + side, m]
            ).start()
        edges(m, 2)
        return 0

    lax.fori_loop(0, 2, member, 0)
    for m in range(2):
        pltpu.make_async_copy(levels.at[m], level_hbm.at[m], out_sem.at[0, m]).wait()
        for side in range(2):
            pltpu.make_async_copy(
                flux_out.at[side, m], flux_hbm.at[side, m], out_sem.at[1 + side, m]
            ).wait()


def outer_steps(wet_tiles, nest_host, nest_anchor, eta, depth, halos):
    f32 = jnp.float32
    return pl.pallas_call(
        outer_kernel,
        out_shape=(
            jax.ShapeDtypeStruct((2, 1024, 128), f32),
            jax.ShapeDtypeStruct((2, 2, 1024, 128), f32),
            jax.ShapeDtypeStruct((2, 2, 8, 128), f32),
            jax.ShapeDtypeStruct((SECTIONS,), jnp.int32),
        ),
        in_specs=[hbm_spec()] * 9,
        out_specs=(hbm_spec(), hbm_spec(), vmem_spec(), smem_spec()),
        scratch_shapes=[
            VMEM((2, 1024, 128), f32),
            VMEM((1024, 128), f32),
            VMEM((2, 64, 128), f32),
            VMEM((2, 64, 128), f32),
            VMEM((64, 128), f32),
            VMEM((64, 128), f32),
            pltpu.SMEM((8, SECTIONS), jnp.int32),
            pltpu.SMEM((SECTIONS,), jnp.int32),
            pltpu.SMEM((2, SECTIONS), jnp.int32),
            VMEM((ROWS_HELD, 8, 8, 128), f32),
            VMEM((ROWS_HELD, 8, 8, 128), f32),
            VMEM((ROWS_HELD, 8, 8, 128), f32),
            VMEM((ROWS_HELD, 8, 8, 128), f32),
            VMEM((3, 8, 8, 128), f32),
            VMEM((2, 1024, 128), f32),
            VMEM((2, 2, 1024, 128), f32),
            pltpu.SMEM((SECTIONS,), jnp.int32),
            pltpu.SMEM((SECTIONS,), jnp.int32),
            pltpu.SemaphoreType.DMA((9,)),
            pltpu.SemaphoreType.DMA((3, 2)),
        ],
        compiler_params=pltpu.CompilerParams(vmem_limit_bytes=62 << 20),
        name="outer",
    )(wet_tiles.T, nest_host, nest_anchor.T, eta, depth, *halos)


def lane_ids():
    return lax.broadcasted_iota(jnp.int32, (8, 128), 1)


def sub_ids():
    return lax.broadcasted_iota(jnp.int32, (8, 128), 0)


def interleave(parts):
    lane = lane_ids()
    out = []
    for t in range(3):
        origin = (3 * lax.rem((lane - t + 128) * 43, 128) + t) // 128
        mixed = jnp.where(origin == 0, parts[0], jnp.where(origin == 1, parts[1], parts[2]))
        out.append(jnp.take_along_axis(mixed, lax.rem(3 * lane + t, 128), axis=1))
    return out


def straighten(parts):
    lane = lane_ids()
    spread_parts = []
    origins = []
    for t in range(3):
        spot = lax.rem((lane - t + 128) * 43, 128)
        spread_parts.append(jnp.take_along_axis(parts[t], spot, axis=1))
        origins.append((3 * spot + t) // 128)
    return [
        jnp.where(origins[0] == t, spread_parts[0], jnp.where(origins[1] == t, spread_parts[1], spread_parts[2]))
        for t in range(3)
    ]


def spread_edges(edge_ref, cols, rows, steps):
    lane = lane_ids()
    sub = sub_ids()

    def spread(row, index):
        wide = jnp.broadcast_to(row, (8, 128))
        return jnp.take_along_axis(wide, index, axis=1)

    for step in steps:
        for m in range(2):
            at = m * 2 + (4 if step == 2 else 0)
            level = edge_ref[at : at + 1, :]
            upright = edge_ref[at + 1 : at + 2, :]
            for q in range(8):
                cols[step, m, 0, q] = spread(upright, sub * 8 + q)
                cols[step, m, 1, q] = spread(upright, sub * 8 + q + 64)
            for side in range(2):
                for t in range(3):
                    value = spread(level, (3 * lane + t) // REFINE + 64 * side)
                    if t == 0:
                        value = jnp.where(lane == 0, cols[step, m, 0, 7 * side], value)
                    if t == 2:
                        value = jnp.where(lane == 127, cols[step, m, 1, 7 * side], value)
                    rows[step, m, side, t] = value


def force_sides(value, t, sides):
    lane = lane_ids()
    if t == 0:
        value = jnp.where(lane == 0, sides[0], value)
    if t == 2:
        value = jnp.where(lane == 127, sides[1], value)
    return value


def fix_rows(h, rows, step, m):
    sub = sub_ids()
    for t in range(3):
        h[m, 0, t] = jnp.where(sub == 0, rows[step, m, 0, t], h[m, 0, t])
        h[m, STRIP - 1, t] = jnp.where(sub == 7, rows[step, m, 1, t], h[m, STRIP - 1, t])


def load_depth(dsrc, coef, d2):
    def load(i, _):
        parts = interleave([dsrc[t, pl.ds(i, 8, stride=STRIP), :] for t in range(3)])
        for t in range(3):
            coef[i, t] = parts[t]
        d2[i] = pltpu.roll(parts[2], 1, 1)
        return 0

    lax.fori_loop(0, STRIP, load, 0, unroll=4)


def load_source(src, h, div, m):
    def load(i, _):
        parts = interleave([src[m, t, pl.ds(i, 8, stride=STRIP), :] for t in range(3)])
        for t in range(3):
            h[m, i, t] = parts[t]
            div[m, i, t] = jnp.zeros((8, 128), jnp.float32)
        return 0

    lax.fori_loop(0, STRIP, load, 0, unroll=4)


def first_substep(h, peak, cols, rows, m):
    def start(q, _):
        sides = [cols[0, m, side, q] for side in range(2)]
        for r in range(REFINE):
            for t in range(3):
                i = q * REFINE + r
                value = force_sides(h[m, i, t], t, sides)
                if t != 1:
                    h[m, i, t] = value
                peak[m, i, t] = value
        return 0

    lax.fori_loop(0, STRIP // REFINE, start, 0)
    fix_rows(h, rows, 0, m)


def advance(m, start, step, carry, h, div, peak, coef, d2, cols):
    now, above = carry
    for r in range(BATCH):
        i = start + r
        if r % REFINE == 0:
            sides = [cols[step, m, side, i // REFINE] for side in range(2)]
        following = [h[m, i + 1, t] for t in range(3)]
        d = [coef[i, t] for t in range(3)]
        beyond = [now[1], now[2], pltpu.roll(now[0], 127, 1)]
        f = [d[t] * (beyond[t] - now[t]) for t in range(3)]
        behind = [d2[i] * (now[0] - pltpu.roll(now[2], 1, 1)), f[0], f[1]]
        g = []
        for t in range(3):
            g.append(d[t] * (following[t] - now[t]))
            change = div[m, i, t] - ((f[t] - behind[t]) + (g[t] - above[t]))
            value = force_sides(now[t] - change, t, sides)
            div[m, i, t] = change
            h[m, i, t] = value
            peak[m, i, t] = jnp.maximum(peak[m, i, t], value)
        now, above = following, g
    return now, above


def substeps(m, low, high, h, div, peak, coef, d2, cols, rows):
    def substep(k, _):
        step = k // REFINE
        now = [h[m, 0, t] for t in range(3)]
        above = []
        for t in range(3):
            wrapped = pltpu.roll(now[t], 7, 0)
            h[m, STRIP, t] = wrapped
            above.append(pltpu.roll(coef[STRIP - 1, t] * (wrapped - h[m, STRIP - 1, t]), 1, 0))
        lax.fori_loop(
            0,
            STRIP // BATCH,
            lambda b, c: advance(m, b * BATCH, step, c, h, div, peak, coef, d2, cols),
            (now, above),
        )
        fix_rows(h, rows, step, m)
        return 0

    lax.fori_loop(low, high, substep, 0)


def settle_peak(peak, rows, m):
    sub = sub_ids()
    for t in range(3):
        for side, i, edge_sub in ((0, 0, 0), (1, STRIP - 1, 7)):
            top = jnp.maximum(
                jnp.maximum(rows[0, m, side, t], rows[1, m, side, t]), rows[2, m, side, t]
            )
            peak[m, i, t] = jnp.where(sub == edge_sub, top, peak[m, i, t])


def coast_kernel(
    host_ref, pick_ref, edges_ref, source_ref, depth_ref, mean_ref, var_ref,
    gathered, outgoing, incoming_first, incoming_later, own_edge,
    h, div, peak, coef, d2, cols, rows, src, dsrc,
    r1, st, r2, mv,
    load_sem, send_x, recv_x, send_z, recv_z, s1, q1, s2, q2, s3, q3, s4, q4,
):
    sec = lax.axis_index("sec")
    plane = sec // Z_CORES
    core = lax.rem(sec, 2)
    spot = lax.rem(sec, Z_CORES) // 2
    group = plane * 2 + core
    mem = lax.axis_index("mem")
    near = mem + 1 - 2 * lax.rem(mem, 2)
    far = 3 - mem
    high = mem // 2
    gray = lax.rem(lax.rem(mem, 2) + high, 2)

    loads = []
    for t in range(3):
        part = pl.ds(128 * t, 128)
        loads.append(pltpu.make_async_copy(depth_ref.at[0, :, part], dsrc.at[t], load_sem.at[t]))
    for m in range(2):
        for t in range(3):
            part = pl.ds(128 * t, 128)
            loads.append(
                pltpu.make_async_copy(
                    source_ref.at[m, 0, :, part], src.at[m, t], load_sem.at[3 + 3 * m + t]
                )
            )
    for copy in loads:
        copy.start()

    def in_group(step):
        other = lax.rem(group + step, GROUP)
        return (other // 2) * Z_CORES + spot * 2 + lax.rem(other, 2)

    def in_line(step):
        return plane * Z_CORES + lax.rem(spot + step, Z_LINE) * 2 + core

    barrier = pltpu.get_barrier_semaphore()
    for step in range(1, GROUP):
        pl.semaphore_signal(barrier, inc=1, device_id={"sec": in_group(step)}, device_id_type=MESH)
    for step in range(1, Z_LINE):
        pl.semaphore_signal(barrier, inc=1, device_id={"sec": in_line(step)}, device_id_type=MESH)
    for peer in (near, far):
        pl.semaphore_signal(barrier, inc=1, device_id={"mem": peer}, device_id_type=MESH)
    for copy in loads[:3]:
        copy.wait()
    load_depth(dsrc, coef, d2)
    gathered[group] = edges_ref[...]
    pl.semaphore_wait(barrier, GROUP + Z_LINE)

    along_x = []
    for step in range(1, GROUP):
        copy = pltpu.make_async_remote_copy(
            src_ref=edges_ref,
            dst_ref=gathered.at[group],
            send_sem=send_x.at[step - 1],
            recv_sem=recv_x.at[step - 1],
            device_id={"sec": in_group(step)},
            device_id_type=MESH,
        )
        copy.start()
        along_x.append(copy)
    for copy in loads[3:]:
        copy.wait()
    load_source(src, h, div, 0)
    for copy in along_x:
        copy.wait()
    along_z = []
    incoming = (incoming_first, incoming_later)
    for part in range(2):
        for step in range(Z_LINE):
            choice = pick_ref[in_line(step)]
            message = gathered[choice // 2, lax.rem(choice, 2), part]
            if step == 0:
                incoming[part][spot] = message
                continue
            outgoing[part, step] = message
            copy = pltpu.make_async_remote_copy(
                src_ref=outgoing.at[part, step],
                dst_ref=incoming[part].at[spot],
                send_sem=send_z.at[part, step - 1],
                recv_sem=recv_z.at[part, step - 1],
                device_id={"sec": in_line(step)},
                device_id_type=MESH,
            )
            copy.start()
            along_z.append(copy)
    load_source(src, h, div, 1)
    host_spot = lax.rem(host_ref[sec], Z_CORES) // 2
    for copy in along_z[: Z_LINE - 1]:
        copy.wait_recv()
    own_edge[0] = incoming_first[host_spot]
    spread_edges(own_edge.at[0], cols, rows, (0,))

    def early(m, _):
        first_substep(h, peak, cols, rows, m)
        substeps(m, 1, REFINE, h, div, peak, coef, d2, cols, rows)
        return 0

    lax.fori_loop(0, 2, early, 0)
    for copy in along_z[Z_LINE - 1 :]:
        copy.wait_recv()
    own_edge[1] = incoming_later[host_spot]
    spread_edges(own_edge.at[1], cols, rows, (1, 2))

    one = (near, far)
    two = (far, near)
    keep1 = (gray, high)
    keep2 = (high, gray)
    flows = [(chunk, half) for chunk in range(3) for half in range(2)]

    def quad(chunk, half, bit1):
        return half * 24 + chunk * 8 + bit1 * 4

    def remote(src_ref, dst_ref, send, recv, peer):
        return pltpu.make_async_remote_copy(
            src_ref=src_ref, dst_ref=dst_ref, send_sem=send, recv_sem=recv,
            device_id={"mem": peer}, device_id_type=MESH,
        )

    def first(m, chunk, half):
        n = 2 * chunk + half
        away = pl.ds(quad(chunk, half, 1 - keep1[half]), 4)
        return remote(peak.at[m, away], r1.at[n, m], s1.at[n, m], q1.at[n, m], one[half])

    def late(m, _):
        substeps(m, REFINE, STEPS * REFINE, h, div, peak, coef, d2, cols, rows)
        settle_peak(peak, rows, m)
        for chunk, half in flows:
            first(m, chunk, half).start()
        return 0

    lax.fori_loop(0, 2, late, 0)

    second = {}
    for chunk, half in flows:
        n = 2 * chunk + half
        for m in range(2):
            first(m, chunk, half).wait_recv()
        kept = quad(chunk, half, keep1[half])

        def merge_pair(bit2, n=n, kept=kept):
            for r in range(2):
                local = bit2 * 2 + r
                for t in range(3):
                    a = peak[0, kept + local, t]
                    b = peak[1, kept + local, t]
                    c = r1[n, 0, local, t]
                    d = r1[n, 1, local, t]
                    total = (a + b) + (c + d)
                    middle = total * 0.25
                    a = a - middle
                    b = b - middle
                    c = c - middle
                    d = d - middle
                    st[n, 0, local, t] = total
                    st[n, 1, local, t] = (a * a + b * b) + (c * c + d * d)

        merge_pair(1 - keep2[half])
        away = pl.ds((1 - keep2[half]) * 2, 2)
        second[n] = remote(st.at[n, :, away], r2.at[n], s2.at[n], q2.at[n], two[half])
        second[n].start()
        merge_pair(keep2[half])

    def straight_rows(start, count):
        for r in range(count):
            i = start + r
            for number, target in enumerate((mean_ref, var_ref)):
                parts = straighten([mv[number, i, t] for t in range(3)])
                for t in range(3):
                    target[t, pl.ds(i, 8, stride=STRIP), :] = parts[t]

    third = {}
    for chunk, half in flows:
        n = 2 * chunk + half
        second[n].wait_recv()
        pair = quad(chunk, half, keep1[half]) + keep2[half] * 2
        for r in range(2):
            local = keep2[half] * 2 + r
            for t in range(3):
                mine = st[n, 0, local, t]
                other = r2[n, 0, r, t]
                gap = mine - other
                squares = (st[n, 1, local, t] + r2[n, 1, r, t]) + gap * gap * 0.125
                mv[0, pair + r, t] = (mine + other) * 0.125
                mv[1, pair + r, t] = squares * 0.125
        block = pl.ds(pair, 2)
        third[n] = remote(mv.at[:, block], mv.at[:, block], s3.at[n], q3.at[n], two[half])
        third[n].start()

    fourth = {}
    for chunk, half in flows:
        n = 2 * chunk + half
        third[n].wait_recv()
        kept = pl.ds(quad(chunk, half, keep1[half]), 4)
        fourth[n] = remote(mv.at[:, kept], mv.at[:, kept], s4.at[n], q4.at[n], one[half])
        fourth[n].start()

    for chunk, half in flows:
        straight_rows(quad(chunk, half, keep1[half]), 4)
    for chunk, half in flows:
        n = 2 * chunk + half
        fourth[n].wait_recv()
        straight_rows(quad(chunk, half, 1 - keep1[half]), 4)
    for copy in along_z:
        copy.wait_send()
    for chunk, half in flows:
        n = 2 * chunk + half
        for m in range(2):
            first(m, chunk, half).wait_send()
        second[n].wait_send()
        third[n].wait_send()
        fourth[n].wait_send()


def advance_coast(nest_host, pick, edges, source, depth):
    shape = jax.ShapeDtypeStruct((3, 384, 128), jnp.float32)
    dma = pltpu.SemaphoreType.DMA
    return pl.pallas_call(
        coast_kernel,
        out_shape=(shape, shape),
        in_specs=[smem_spec(), smem_spec(), vmem_spec(), hbm_spec(), hbm_spec()],
        out_specs=(vmem_spec(), vmem_spec()),
        scratch_shapes=[
            VMEM((GROUP, 2, 2, 8, 128), jnp.float32),
            VMEM((2, Z_LINE, 8, 128), jnp.float32),
            VMEM((Z_LINE, 8, 128), jnp.float32),
            VMEM((Z_LINE, 8, 128), jnp.float32),
            VMEM((2, 8, 128), jnp.float32),
            VMEM((2, STRIP + 1, 3, 8, 128), jnp.float32),
            VMEM((2, STRIP, 3, 8, 128), jnp.float32),
            VMEM((2, STRIP, 3, 8, 128), jnp.float32),
            VMEM((STRIP, 3, 8, 128), jnp.float32),
            VMEM((STRIP, 8, 128), jnp.float32),
            VMEM((STEPS, 2, 2, 8, 8, 128), jnp.float32),
            VMEM((STEPS, 2, 2, 3, 8, 128), jnp.float32),
            VMEM((2, 3, 384, 128), jnp.float32),
            VMEM((3, 384, 128), jnp.float32),
            VMEM((6, 2, 4, 3, 8, 128), jnp.float32),
            VMEM((6, 2, 4, 3, 8, 128), jnp.float32),
            VMEM((6, 2, 2, 3, 8, 128), jnp.float32),
            VMEM((2, STRIP, 3, 8, 128), jnp.float32),
            dma((9,)),
            dma((GROUP - 1,)),
            dma((GROUP - 1,)),
            dma((2, Z_LINE - 1)),
            dma((2, Z_LINE - 1)),
            dma((6, 2)),
            dma((6, 2)),
            *([dma((6,))] * 6),
        ],
        compiler_params=pltpu.CompilerParams(
            collective_id=1, has_side_effects=True, vmem_limit_bytes=62 << 20
        ),
        name="coast",
    )(nest_host, pick, edges, source, depth)


def emit_kernel(mean_ref, var_ref, mean_hbm, var_hbm, held, in_sem, out_sem):
    parts = [
        (number, t, source, target)
        for number, (source, target) in enumerate(((mean_ref, mean_hbm), (var_ref, var_hbm)))
        for t in range(3)
    ]
    loads = [
        pltpu.make_async_copy(source.at[t], held.at[number, t], in_sem.at[number, t])
        for number, t, source, _ in parts
    ]
    stores = [
        pltpu.make_async_copy(
            held.at[number, t], target.at[0, :, pl.ds(128 * t, 128)], out_sem.at[number, t]
        )
        for number, t, _, target in parts
    ]
    for copy in loads:
        copy.start()
    for load, store in zip(loads, stores):
        load.wait()
        store.start()
    for copy in stores:
        copy.wait()


def emit(mean, var):
    shape = jax.ShapeDtypeStruct((1, 384, 384), jnp.float32)
    return pl.pallas_call(
        emit_kernel,
        out_shape=(shape, shape),
        in_specs=[hbm_spec()] * 2,
        out_specs=(hbm_spec(), hbm_spec()),
        scratch_shapes=[
            VMEM((2, 3, 384, 128), jnp.float32),
            pltpu.SemaphoreType.DMA((2, 3)),
            pltpu.SemaphoreType.DMA((2, 3)),
        ],
        compiler_params=pltpu.CompilerParams(vmem_limit_bytes=62 << 20),
        name="emit",
    )(mean, var)


def tiled(field):
    lead = field.shape[:-2]
    n = len(lead)
    split = field.reshape(*lead, 16, 8, 8, 128)
    return jnp.swapaxes(split, n + 1, n + 2).reshape(*lead, 1024, 128)


def untiled(field):
    lead = field.shape[:-2]
    n = len(lead)
    split = field.reshape(*lead, 16, 8, 8, 128)
    return jnp.swapaxes(split, n + 1, n + 2).reshape(*lead, 128, 1024)


def body(outer_source, outer_depth, wet_tiles, nest_host, nest_anchor, nest_source, nest_depth):
    eta = tiled(outer_source)
    depth = tiled(outer_depth)
    halos = exchange_halos(eta, depth)
    level, flux, edges, pick = outer_steps(wet_tiles, nest_host, nest_anchor, eta, depth, halos)
    mean, var = advance_coast(nest_host, pick, edges, nest_source, nest_depth)
    mean, var = emit(mean, var)
    return (untiled(level), untiled(flux), mean, var)


def solution(mesh):
    return jax.shard_map(
        body,
        mesh=mesh,
        in_specs=(
            P("mem", "sec", None),
            P("sec", None),
            P(),
            P(),
            P(),
            P("mem", "sec", None, None),
            P("sec", None, None),
        ),
        out_specs=(
            P("mem", "sec", None),
            P(None, "mem", "sec", None),
            P("sec", None, None),
            P("sec", None, None),
        ),
        check_vma=False,
    )
```
